256 devices in a mesh: segment: 2 (over core), dom: 64 (over z, y, x_lo), rep: 2 (over x_hi).
Axes of the slice: x: 4 (x_hi: 2, x_lo: 2; x = x_hi * 2 + x_lo), y: 4, z: 8, core: 2. Of those that a mesh axis runs over, the one named last changes fastest.
Arguments:
- node_latent: bfloat16 [4, 8192, 512], P('rep', 'dom'), may hold values from -6 to 6
- edge_latent: bfloat16 [4, 24576, 512], P('rep', 'dom'), may hold values from -6 to 6
- node_cot: bfloat16 [4, 8192, 512], P('rep', 'dom'), may hold values from -6 to 6
- edge_src: int32 [24576], P('dom'), may hold values from 0 to 191, as said below
- edge_dst: int32 [24576], P('dom'), may hold values from 0 to 127
- edge_count: int32 [64], P('dom'), may hold values from 192 to 384, as said below
- send_index: int32 [64, 4, 16], P('dom'), may hold values from 0 to 127, as said below
- w_edge_in: bfloat16 [2, 1536, 512], P('segment'), may hold values from -0.15625 to 0.15625
- w_edge_out: bfloat16 [2, 512, 512], P('segment'), may hold values from -0.25 to 0.25
- w_node_in: bfloat16 [2, 1024, 512], P('segment'), may hold values from -0.1875 to 0.1875
- w_node_out: bfloat16 [2, 512, 512], P('segment'), may hold values from -0.25 to 0.25
- gain_edge: float32 [2, 512], P('segment'), may hold values from 0.1 to 1.9
- gain_node: float32 [2, 512], P('segment'), may hold values from 0.1 to 1.9
Outputs:
- node_pair: bfloat16 [2, 4, 8192, 512], P('segment', 'rep', 'dom')
- edge_pair: bfloat16 [2, 4, 24576, 512], P('segment', 'rep', 'dom')
- grad_edge_in: float32 [2, 1536, 512], P('segment', ('dom', 'rep'))
- grad_edge_out: float32 [2, 512, 512], P('segment', ('dom', 'rep'))
- grad_node_in: float32 [2, 1024, 512], P('segment', ('dom', 'rep'))
- grad_node_out: float32 [2, 512, 512], P('segment', ('dom', 'rep'))
- grad_gain_edge: float32 [2, 512], P('segment', ('dom', 'rep'))
- grad_gain_node: float32 [2, 512], P('segment', ('dom', 'rep'))
The draws below stay inside these ranges and needn't reach their ends.
Inputs may be any that keep to these rules, and one draw needn't show every extreme that they name: `edge_src`: each value is below 192; a value 128 + j * 16 + k of partition p refers to round j only where partition p - o_j exists. `edge_count`: some partition has all 384 slots live. `send_index`: the 16 rows of one partition and round are distinct.
All inputs are finite; a program needn't handle non-finite values.
Results may differ from the reference program's by a relative error of at most 0.039.
Values may be sent and summed in bfloat16 or wider, within the bound.
A program may use at most 128 MiB of HBM per device.

```python
import jax
import jax.numpy as jnp
from jax import lax

D = 512
NODE_DEV = 128
EDGE_DEV = 384
HALO = 16
ROUNDS = 4
SNAP = 4
NODES = 8192
EDGES = 24576
N_DOM = 64


def edge_lists(key):
    key_src = jax.random.fold_in(key, 11)
    key_dst = jax.random.fold_in(key, 12)
    slots = NODE_DEV + ROUNDS * HALO
    pick = jax.random.randint(key_src, (EDGES,), 0, slots)
    partition = jnp.arange(EDGES, dtype=jnp.int32) // EDGE_DEV
    round_of = jnp.clip((pick - NODE_DEV) // HALO, 0, ROUNDS - 1)
    offsets = jnp.array([1, -1, 2, -2], dtype=jnp.int32)
    anchor = partition - offsets[round_of]
    usable = (pick < NODE_DEV) | (anchor >= 0) & (anchor < N_DOM)
    sender = jnp.where(usable, pick, pick % NODE_DEV).astype(jnp.int32)
    target = jax.random.randint(key_dst, (EDGES,), 0, NODE_DEV)
    target = jnp.where(sender == target, (target + 1) % NODE_DEV, target).astype(jnp.int32)
    return (sender, target)


def draw_edge_src(key, part):
    return edge_lists(key)[0]


def draw_edge_dst(key, part):
    return edge_lists(key)[1]


def draw_edge_count(key, part):
    counts = jax.random.randint(jax.random.fold_in(key, 21), (N_DOM,), EDGE_DEV // 2, EDGE_DEV + 1)
    fullest = jax.random.randint(jax.random.fold_in(key, 22), (), 0, N_DOM)
    return jnp.where(jnp.arange(N_DOM) == fullest, EDGE_DEV, counts).astype(jnp.int32)


def draw_send_index(key, part):
    keys = jax.random.split(jax.random.fold_in(key, 31), N_DOM * ROUNDS)
    rows = jax.vmap(lambda k: jax.random.permutation(k, NODE_DEV)[:HALO])(keys)
    return rows.reshape(N_DOM, ROUNDS, HALO).astype(jnp.int32)


def level_of(own_key, extent, pieces, smallest, top_value):
    def one(position, blocks):
        heights = jax.random.uniform(jax.random.fold_in(jax.random.fold_in(own_key, 6), position), (blocks,), jnp.float32, smallest / len(pieces), top_value / len(pieces))
        return jnp.repeat(jnp.exp(heights), extent[position] // blocks).reshape((-1,) + (1,) * (len(extent) - position - 1))

    level = one(*pieces[0])
    for cut in pieces[1:]:
        level = level * one(*cut)
    return level


def normal_values(rng, extent, width, reach, cuts=(), kind=jnp.bfloat16):
    result = jax.random.normal(rng, extent, jnp.float32) * width
    if len(cuts) > 0:
        result = level_of(rng, extent, cuts, -0.22, 0.18) * result
    return jnp.clip(result, min=-reach, max=reach).astype(kind)


def setup_inputs(seed: int = 0) -> dict:
    key_list = jax.random.split(jax.random.key(seed), 14)
    return {
        "node_latent": normal_values(key_list[0], (SNAP, NODES, D), 1.0, 6.0, ((0, 2), (1, 64))),
        "edge_latent": normal_values(key_list[1], (SNAP, EDGES, D), 1.0, 6.0, ((0, 2), (1, 64))),
        "node_cot": normal_values(key_list[2], (SNAP, NODES, D), 1.0, 6.0, ((0, 2), (1, 64))),
        "edge_src": draw_edge_src(jax.random.fold_in(key_list[13], 71), 0),
        "edge_dst": draw_edge_dst(jax.random.fold_in(key_list[13], 71), 0),
        "edge_count": draw_edge_count(jax.random.fold_in(key_list[13], 71), 0),
        "send_index": draw_send_index(jax.random.fold_in(key_list[13], 71), 0),
        "w_edge_in": normal_values(key_list[7], (2, 3 * D, D), (3 * D) ** -0.5, 0.15625, ((0, 2),)),
        "w_edge_out": normal_values(key_list[8], (2, D, D), D ** -0.5, 0.25, ((0, 2),)),
        "w_node_in": normal_values(key_list[9], (2, 2 * D, D), (2 * D) ** -0.5, 0.1875, ((0, 2),)),
        "w_node_out": normal_values(key_list[10], (2, D, D), D ** -0.5, 0.25, ((0, 2),)),
        "gain_edge": jnp.clip(1.0 + 0.18 * jax.random.normal(key_list[11], (2, D), jnp.float32), 0.1, 1.9),
        "gain_node": jnp.clip(1.0 + 0.18 * jax.random.normal(key_list[12], (2, D), jnp.float32), 0.1, 1.9),
    }


OFFSETS = (1, -1, 2, -2)
EPS = 1e-05

def norm_rows(values, gain):
    center = values - lax.optimization_barrier(jnp.mean(values, axis=-1, keepdims=True))
    spread = lax.optimization_barrier(jnp.mean(center * center, axis=-1, keepdims=True))
    return center * lax.rsqrt(spread + EPS) * gain

def layer(table, edges, weights, src, dst, live):
    w_ein, w_eout, w_nin, w_nout, g_edge, g_node = weights
    own = table[:NODE_DEV]
    sender = jnp.take(table, src, axis=0)
    receiver = jnp.take(table, dst, axis=0)
    joined = jnp.concatenate([edges, sender, receiver], axis=1)
    pre = jnp.dot(joined, w_ein.astype(jnp.bfloat16), preferred_element_type=jnp.float32)
    middle = jax.nn.silu(pre).astype(jnp.bfloat16)
    outer = jnp.dot(middle, w_eout.astype(jnp.bfloat16), preferred_element_type=jnp.float32)
    moved = edges.astype(jnp.float32)
    edge_new = jnp.where(live[:, None], moved + norm_rows(outer, g_edge), moved).astype(jnp.bfloat16)
    owners = jnp.arange(NODE_DEV, dtype=jnp.int32)
    incidence = ((dst[None, :] == owners[:, None]) & live[None, :]).astype(jnp.bfloat16)
    summed = jnp.dot(incidence, edge_new, preferred_element_type=jnp.float32).astype(jnp.bfloat16)
    node_in = jnp.concatenate([own, summed], axis=1)
    pre_node = jnp.dot(node_in, w_nin.astype(jnp.bfloat16), preferred_element_type=jnp.float32)
    mid_node = jax.nn.silu(pre_node).astype(jnp.bfloat16)
    out_node = jnp.dot(mid_node, w_nout.astype(jnp.bfloat16), preferred_element_type=jnp.float32)
    node_new = (own.astype(jnp.float32) + norm_rows(out_node, g_node)).astype(jnp.bfloat16)
    return (node_new, edge_new)

def tables(own, send_index):
    parts = [own]
    for j, step in enumerate(OFFSETS):
        sent = jax.vmap(lambda rows, idx: jnp.take(rows, idx, axis=0))(own, send_index[:, j])
        blank = jnp.zeros((abs(step),) + sent.shape[1:], sent.dtype)
        if step > 0:
            got = jnp.concatenate([blank, sent[:-step]], axis=0)
        else:
            got = jnp.concatenate([sent[-step:], blank], axis=0)
        parts.append(got)
    return jnp.concatenate(parts, axis=1)

def return_halo(d_table, send_index):
    d_own = d_table[:, :NODE_DEV].astype(jnp.float32)
    owners = jnp.arange(NODE_DEV, dtype=jnp.int32)
    for j, step in enumerate(OFFSETS):
        piece = d_table[:, NODE_DEV + j * HALO:NODE_DEV + (j + 1) * HALO]
        blank = jnp.zeros((abs(step),) + piece.shape[1:], piece.dtype)
        if step > 0:
            back = jnp.concatenate([piece[step:], blank], axis=0)
        else:
            back = jnp.concatenate([blank, piece[:step]], axis=0)
        incidence = (send_index[:, j, None, :] == owners[None, :, None]).astype(jnp.float32)
        d_own = d_own + jnp.einsum('nrh,nhd->nrd', incidence, back.astype(jnp.float32))
    return d_own.astype(jnp.bfloat16)

def backward_segment(weights, table, edges, cot_node, cot_edge, src, dst, live, send_index):

    def one(total, item):
        tab, edg, c_node, c_edge, s_idx, d_idx, alive = item
        _, pull = jax.vjp(lambda a, b, w: layer(a, b, w, s_idx, d_idx, alive), tab, edg, weights)
        d_tab, d_edg, d_w = pull((c_node, c_edge))
        total = jax.tree.map(lambda x, y: x + y.astype(jnp.float32), total, d_w)
        return (total, (d_tab, d_edg))
    start = jax.tree.map(jnp.zeros_like, weights)
    total, (d_tab, d_edg) = lax.scan(one, start, (table, edges, cot_node, cot_edge, src, dst, live))
    return (total, return_halo(d_tab, send_index), d_edg)

def reference(node_latent, edge_latent, node_cot, edge_src, edge_dst, edge_count, send_index, w_edge_in, w_edge_out, w_node_in, w_node_out, gain_edge, gain_node):
    src = edge_src.reshape(N_DOM, EDGE_DEV)
    dst = edge_dst.reshape(N_DOM, EDGE_DEV)
    live = jnp.arange(EDGE_DEV, dtype=jnp.int32)[None, :] < edge_count[:, None]
    segment_w = []
    for s in range(2):
        segment_w.append((w_edge_in[s].astype(jnp.float32), w_edge_out[s].astype(jnp.float32), w_node_in[s].astype(jnp.float32), w_node_out[s].astype(jnp.float32), gain_edge[s], gain_node[s]))
    forward = jax.vmap(layer, in_axes=(0, 0, None, 0, 0, 0))
    totals = [jax.tree.map(jnp.zeros_like, segment_w[0]), jax.tree.map(jnp.zeros_like, segment_w[1])]
    grad_nodes, grad_edges, last_nodes, last_edges = ([], [], [], [])
    for k in range(SNAP):
        h_zero = node_latent[k].reshape(N_DOM, NODE_DEV, D)
        e_zero = edge_latent[k].reshape(N_DOM, EDGE_DEV, D)
        t_zero = tables(h_zero, send_index)
        h_one, e_one = forward(t_zero, e_zero, segment_w[0], src, dst, live)
        t_one = tables(h_one, send_index)
        h_two, e_two = forward(t_one, e_one, segment_w[1], src, dst, live)
        c_node = node_cot[k].reshape(N_DOM, NODE_DEV, D)
        g_one, dh_one, de_one = backward_segment(segment_w[1], t_one, e_one, c_node, jnp.zeros_like(e_two), src, dst, live, send_index)
        g_zero, dh_zero, de_zero = backward_segment(segment_w[0], t_zero, e_zero, dh_one, de_one, src, dst, live, send_index)
        totals[0] = jax.tree.map(lambda x, y: x + y, totals[0], g_zero)
        totals[1] = jax.tree.map(lambda x, y: x + y, totals[1], g_one)
        grad_nodes.append(dh_zero.reshape(NODES, D))
        grad_edges.append(de_zero.reshape(EDGES, D))
        last_nodes.append(h_two.reshape(NODES, D))
        last_edges.append(e_two.reshape(EDGES, D))
    node_pair = jnp.stack([jnp.stack(grad_nodes), jnp.stack(last_nodes)])
    edge_pair = jnp.stack([jnp.stack(grad_edges), jnp.stack(last_edges)])
    factor = float(SNAP * NODES) ** (-0.5)
    outs = [jnp.stack([totals[0][i], totals[1][i]]) * factor for i in range(6)]
    return (node_pair, edge_pair, outs[0], outs[1], outs[2], outs[3], outs[4], outs[5])
```

```python
import functools

import jax
import jax.numpy as jnp
from jax import lax
from jax.experimental import pallas as pl
from jax.experimental.pallas import tpu as pltpu
from jax.sharding import PartitionSpec as P

NODE_DEV = 128


OFFSETS = (1, -1, 2, -2)
EPS = 1e-05
MESH = pl.DeviceIdType.MESH


def shifted(block, axis, distance):
    devices = range(lax.axis_size(axis))
    route = [(i - distance, i) for i in devices if i - distance in devices]
    return lax.ppermute(block, axis, route)


def norm_rows(values, gain):
    center = values - jnp.mean(values, axis=-1, keepdims=True)
    spread = jnp.mean(center * center, axis=-1, keepdims=True)
    return center * lax.rsqrt(spread + EPS) * gain


def layer(table, edges, weights, src, dst, live):
    w_ein, w_eout, w_nin, w_nout, g_edge, g_node = weights
    own = table[:NODE_DEV]
    sender = jnp.take(table, src, axis=0)
    receiver = jnp.take(table, dst, axis=0)
    joined = jnp.concatenate([edges, sender, receiver], axis=1)
    pre = jnp.dot(joined, w_ein.astype(jnp.bfloat16), preferred_element_type=jnp.float32)
    middle = jax.nn.silu(pre).astype(jnp.bfloat16)
    outer = jnp.dot(middle, w_eout.astype(jnp.bfloat16), preferred_element_type=jnp.float32)
    moved = edges.astype(jnp.float32)
    edge_new = jnp.where(live[:, None], moved + norm_rows(outer, g_edge), moved).astype(
        jnp.bfloat16
    )
    owners = jnp.arange(NODE_DEV, dtype=jnp.int32)
    incidence = ((dst[None, :] == owners[:, None]) & live[None, :]).astype(jnp.bfloat16)
    summed = jnp.dot(incidence, edge_new, preferred_element_type=jnp.float32).astype(jnp.bfloat16)
    node_in = jnp.concatenate([own, summed], axis=1)
    pre_node = jnp.dot(node_in, w_nin.astype(jnp.bfloat16), preferred_element_type=jnp.float32)
    mid_node = jax.nn.silu(pre_node).astype(jnp.bfloat16)
    out_node = jnp.dot(mid_node, w_nout.astype(jnp.bfloat16), preferred_element_type=jnp.float32)
    node_new = (own.astype(jnp.float32) + norm_rows(out_node, g_node)).astype(jnp.bfloat16)
    return (node_new, edge_new)


def build_table(own, rounds):
    parts = [own]
    for j, step in enumerate(OFFSETS):
        sent = jnp.take(own, rounds[j], axis=0)
        parts.append(shifted(sent, "dom", step))
    return jnp.concatenate(parts, axis=0)


def return_halo(d_table, rounds):
    halo = rounds.shape[1]
    d_own = d_table[:NODE_DEV].astype(jnp.float32)
    owners = jnp.arange(NODE_DEV, dtype=jnp.int32)
    for j, step in enumerate(OFFSETS):
        piece = d_table[NODE_DEV + j * halo : NODE_DEV + (j + 1) * halo]
        back = shifted(piece, "dom", -step)
        incidence = (rounds[j][None, :] == owners[:, None]).astype(jnp.bfloat16)
        d_own = d_own + jnp.dot(incidence, back, preferred_element_type=jnp.float32)
    return d_own.astype(jnp.bfloat16)


ROWS_A = 48
ROWS_B = 64
GAIN = 16


def reduce_kernel(
    ga, gb, ein_o, eout_o, nin_o, nout_o, gain_o,
    ra1, rb1, a2, ra2, b2, rb2, c3, rc3, fin, rfin, send_sem, recv_sem,
    *, nz, factor,
):
    d = lax.axis_index("dom")
    rep = lax.axis_index("rep")
    z = d // 8
    y = (d // 2) % 4
    xt = (d % 2) * 2 + rep

    def at_y(p):
        return {"dom": z * 8 + p * 2 + d % 2}

    def at_z(p):
        return {"dom": p * 8 + d % 8}

    def at_x(p):
        return {"dom": (d // 2) * 2 + p // 2, "rep": p % 2}

    y_peers = [(y + j) % 4 for j in (1, 2, 3)]
    x_peers = [(xt + j) % 4 for j in (1, 2, 3)]
    z_peers = [(z + j) % nz for j in range(1, nz)]
    barrier = pltpu.get_barrier_semaphore()
    for p in y_peers:
        pl.semaphore_signal(barrier, inc=1, device_id=at_y(p), device_id_type=MESH)
    for p in x_peers:
        pl.semaphore_signal(barrier, inc=1, device_id=at_x(p), device_id_type=MESH)
    for p in z_peers:
        pl.semaphore_signal(barrier, inc=1, device_id=at_z(p), device_id_type=MESH)
    pl.semaphore_wait(barrier, 6 + nz - 1)

    def copy(n, src, dst, device):
        return pltpu.make_async_remote_copy(
            src_ref=src,
            dst_ref=dst,
            send_sem=send_sem.at[n],
            recv_sem=recv_sem.at[n],
            device_id=device,
            device_id_type=MESH,
        )

    first_a = [copy(j, ga.at[p], ra1.at[j], at_y(p)) for j, p in enumerate(y_peers)]
    first_b = [copy(3 + j, gb.at[p], rb1.at[j], at_x(p)) for j, p in enumerate(x_peers)]
    for u, v in zip(first_a, first_b):
        u.start()
        v.start()

    for c in first_a:
        c.wait_recv()
    rows_a = ga.shape[1]

    @pl.loop(0, rows_a // 16)
    def _(i):
        at = pl.ds(pl.multiple_of(i * 16, 16), 16)
        total = ga[y, at, :].astype(jnp.float32)
        for j in range(3):
            total = total + ra1[j, at, :].astype(jnp.float32)
        total = total.astype(jnp.bfloat16)
        for b in range(4):
            a2[b, at, :] = total[:, b * 128 : (b + 1) * 128]

    second_a = [copy(6 + j, a2.at[p], ra2.at[j], at_x(p)) for j, p in enumerate(x_peers)]
    for c in second_a:
        c.start()

    for c in first_b:
        c.wait_recv()

    @pl.loop(0, nz)
    def _(i):
        for q in range(4):
            total = gb[xt, i * 4 + q].astype(jnp.float32)
            for j in range(3):
                total = total + rb1[j, i * 4 + q].astype(jnp.float32)
            b2[q, i] = total.astype(jnp.bfloat16)

    second_b = [copy(9 + j, b2.at[p], rb2.at[j], at_y(p)) for j, p in enumerate(y_peers)]
    for c in second_b:
        c.start()

    for c in second_a:
        c.wait_recv()
    tail = pl.ds(nz * ROWS_A, GAIN)
    gains = a2[xt, tail, :].astype(jnp.float32)
    for j in range(3):
        gains = gains + ra2[j, tail, :].astype(jnp.float32)
    gains = gains.astype(jnp.bfloat16)

    @pl.loop(0, nz)
    def _(i):
        at = pl.ds(pl.multiple_of(i * ROWS_A, 16), ROWS_A)
        total = a2[xt, at, :].astype(jnp.float32)
        for j in range(3):
            total = total + ra2[j, at, :].astype(jnp.float32)
        c3[i, 0:ROWS_A, :] = total.astype(jnp.bfloat16)
        c3[i, ROWS_A : ROWS_A + GAIN, :] = gains

    for c in second_b:
        c.wait_recv()

    @pl.loop(0, nz)
    def _(i):
        total = b2[y, i].astype(jnp.float32)
        for j in range(3):
            total = total + rb2[j, i].astype(jnp.float32)
        c3[i, ROWS_A + GAIN :, :] = total.astype(jnp.bfloat16)

    third = [copy(12 + j, c3.at[p], rc3.at[j], at_z(p)) for j, p in enumerate(z_peers)]
    for c in third:
        c.start()
    total = c3[z].astype(jnp.float32)
    for j, c in enumerate(third):
        c.wait_recv()
        total = total + rc3[j].astype(jnp.float32)
    total = total * factor

    n0 = ROWS_A + GAIN
    for b in range(4):
        fin[b, 0:12, :] = total[12 * b : 12 * b + 12]
        fin[b, 12:16, :] = total[n0 + 32 + 4 * b : n0 + 32 + 4 * b + 4]
        fin[b, 16:24, :] = total[n0 + 8 * b : n0 + 8 * b + 8]
        fin[b, 24:28, :] = total[n0 + 48 + 4 * b : n0 + 48 + 4 * b + 4]
        fin[b, 28:32, :] = total[ROWS_A : ROWS_A + 4]
    base = 12 + nz - 1
    last = [copy(base + j, fin.at[p], rfin.at[xt], at_x(p)) for j, p in enumerate(x_peers)]
    for c in last:
        c.start()
    rfin[xt] = fin[xt]
    for c in last:
        c.wait_recv()
    t = d * 2 + rep
    lane = lax.broadcasted_iota(jnp.int32, (2, 128), 1)
    slot = lax.broadcasted_iota(jnp.int32, (2, 128), 1)
    picked = jnp.zeros((2, 128), jnp.float32)
    for b in range(4):
        cols = slice(b * 128, (b + 1) * 128)
        ein_o[:, cols] = rfin[b, 0:12, :]
        eout_o[:, cols] = rfin[b, 12:16, :]
        nin_o[:, cols] = rfin[b, 16:24, :]
        nout_o[:, cols] = rfin[b, 24:28, :]
        pair = rfin[b, 28:30, :]
        for i in range(4):
            hit = jnp.where(lane + b * 128 == t * 4 + i, pair, 0.0)
            value = jnp.sum(hit, axis=1, keepdims=True)
            picked = picked + jnp.where(slot == i, value, 0.0)
    gain_o[...] = picked
    for c in first_a + first_b + second_a + second_b + third + last:
        c.wait_send()


def reduce_call(ga, gb, factor):
    nz = ga.shape[1] // ROWS_A
    bf, f4 = jnp.bfloat16, jnp.float32
    rows = ga.shape[1]
    vm = pl.BlockSpec(memory_space=pltpu.VMEM)
    copies = 12 + nz - 1 + 3
    return pl.pallas_call(
        functools.partial(reduce_kernel, nz=nz, factor=factor),
        out_shape=[
            jax.ShapeDtypeStruct((12, 512), f4),
            jax.ShapeDtypeStruct((4, 512), f4),
            jax.ShapeDtypeStruct((8, 512), f4),
            jax.ShapeDtypeStruct((4, 512), f4),
            jax.ShapeDtypeStruct((2, 128), f4),
        ],
        in_specs=[vm, vm],
        out_specs=[vm] * 5,
        scratch_shapes=[
            pltpu.VMEM((3, rows, 512), bf),
            pltpu.VMEM((3, 4 * nz, ROWS_B, 128), bf),
            pltpu.VMEM((4, rows, 128), bf),
            pltpu.VMEM((3, rows, 128), bf),
            pltpu.VMEM((4, nz, ROWS_B, 128), bf),
            pltpu.VMEM((3, nz, ROWS_B, 128), bf),
            pltpu.VMEM((nz, 128, 128), bf),
            pltpu.VMEM((nz - 1, 128, 128), bf),
            pltpu.VMEM((4, 32, 128), f4),
            pltpu.VMEM((4, 32, 128), f4),
            pltpu.SemaphoreType.DMA((copies,)),
            pltpu.SemaphoreType.DMA((copies,)),
        ],
        compiler_params=pltpu.CompilerParams(
            collective_id=1, has_side_effects=True, vmem_limit_bytes=40 << 20
        ),
        name="grad_reduce_scatter",
    )(ga, gb)


def pack_gradients(total):
    g_ein, g_eout, g_nin, g_nout, g_ge, g_gn = total
    bf = jnp.bfloat16
    nz = 8
    a = g_ein.astype(bf).reshape(nz, 4, ROWS_A, 512).transpose(1, 0, 2, 3).reshape(4, nz * ROWS_A, 512)
    gains = jnp.zeros((GAIN, 512), bf).at[0].set(g_ge.astype(bf)).at[1].set(g_gn.astype(bf))
    a = jnp.concatenate([a, jnp.broadcast_to(gains[None], (4, GAIN, 512))], axis=1)
    b = jnp.concatenate(
        [
            g_nin.astype(bf).reshape(nz * 4, 32, 512),
            g_eout.astype(bf).reshape(nz * 4, 16, 512),
            g_nout.astype(bf).reshape(nz * 4, 16, 512),
        ],
        axis=1,
    )
    b = b.reshape(nz * 4, ROWS_B, 4, 128).transpose(2, 0, 1, 3)
    return a, b


def body(
    node_latent,
    edge_latent,
    node_cot,
    edge_src,
    edge_dst,
    edge_count,
    send_index,
    w_edge_in,
    w_edge_out,
    w_node_in,
    w_node_out,
    gain_edge,
    gain_node,
):
    micro = node_latent.shape[0]
    edge_rows = edge_latent.shape[1]
    first = lax.axis_index("segment") == 0
    weights = (
        w_edge_in[0].astype(jnp.float32),
        w_edge_out[0].astype(jnp.float32),
        w_node_in[0].astype(jnp.float32),
        w_node_out[0].astype(jnp.float32),
        gain_edge[0],
        gain_node[0],
    )
    live = jnp.arange(edge_rows, dtype=jnp.int32) < edge_count[0]
    rounds = send_index[0]
    inbound_node = jnp.zeros_like(node_latent[0])
    inbound_edge = jnp.zeros_like(edge_latent[0])
    saved_tables, saved_edges, outs_node, outs_edge = ([], [], [], [])
    for tick in range(micro + 1):
        pick = min(tick, micro - 1)
        enter_node = jnp.where(first, node_latent[pick], inbound_node)
        enter_edge = jnp.where(first, edge_latent[pick], inbound_edge)
        table = build_table(enter_node, rounds)
        node_new, edge_new = layer(table, enter_edge, weights, edge_src, edge_dst, live)
        saved_tables.append(table)
        saved_edges.append(enter_edge)
        outs_node.append(node_new)
        outs_edge.append(edge_new)
        if tick < micro:
            inbound_node, inbound_edge = shifted((node_new, edge_new), "segment", 1)
    factor = float(micro * lax.axis_size("rep") * NODE_DEV * lax.axis_size("dom")) ** (-0.5)
    total = jax.tree.map(jnp.zeros_like, weights)
    shares = None
    back_node = jnp.zeros_like(node_latent[0])
    back_edge = jnp.zeros_like(edge_latent[0])
    grad_nodes = [None] * micro
    grad_edges = [None] * micro
    for tick in range(micro + 1):
        late = min(tick + 1, micro)
        early = max(tick - 1, 0)
        table = jnp.where(first, saved_tables[early], saved_tables[late])
        edges = jnp.where(first, saved_edges[early], saved_edges[late])
        valid = jnp.where(first, tick >= 1, tick < micro)
        cot_node = jnp.where(first, back_node, node_cot[min(tick, micro - 1)])
        cot_edge = jnp.where(first, back_edge, jnp.zeros_like(back_edge))
        _, pull = jax.vjp(
            lambda a, b, w: layer(a, b, w, edge_src, edge_dst, live), table, edges, weights
        )
        d_table, d_edges, d_weights = pull((cot_node, cot_edge))
        d_own = return_halo(d_table, rounds)
        term = jax.tree.map(lambda g: jnp.where(valid, g, 0.0), d_weights)
        total = jax.tree.map(lambda x, y: x + y, total, term)
        if tick >= 1:
            grad_nodes[tick - 1] = d_own
            grad_edges[tick - 1] = d_edges
        if tick < micro:
            back_node, back_edge = shifted((d_own, d_edges), "segment", -1)
    packed_a, packed_b = pack_gradients(total)
    *shares, picked = reduce_call(packed_a, packed_b, factor)
    node_out = jnp.stack([jnp.where(first, grad_nodes[m], outs_node[m + 1]) for m in range(micro)])[
        None
    ]
    edge_out = jnp.stack([jnp.where(first, grad_edges[m], outs_edge[m + 1]) for m in range(micro)])[
        None
    ]
    scaled = [piece[None] for piece in shares] + [picked[0:1, :4], picked[1:2, :4]]
    return (node_out, edge_out, scaled[0], scaled[1], scaled[2], scaled[3], scaled[4], scaled[5])


def solution(mesh):
    placed = (
        P("rep", "dom", None),
        P("rep", "dom", None),
        P("rep", "dom", None),
        P("dom"),
        P("dom"),
        P("dom"),
        P("dom", None, None),
        P("segment", None, None),
        P("segment", None, None),
        P("segment", None, None),
        P("segment", None, None),
        P("segment", None),
        P("segment", None),
    )
    return jax.shard_map(
        body,
        mesh=mesh,
        in_specs=placed,
        out_specs=(
            P("segment", "rep", "dom", None),
            P("segment", "rep", "dom", None),
            P("segment", ("dom", "rep"), None),
            P("segment", ("dom", "rep"), None),
            P("segment", ("dom", "rep"), None),
            P("segment", ("dom", "rep"), None),
            P("segment", ("dom", "rep")),
            P("segment", ("dom", "rep")),
        ),
        check_vma=False,
    )
```

```python
import functools

import jax
import jax.numpy as jnp
from jax import lax
from jax.experimental import pallas as pl
from jax.experimental.pallas import tpu as pltpu
from jax.sharding import PartitionSpec as P

OFFSETS = (1, -1, 2, -2)
HALO = 16
EPS = 1e-05
MESH = pl.DeviceIdType.MESH
ROWS_A = 48
ROWS_B = 64
GAIN = 16


def reduce_kernel(
    ga, gb, ein_o, eout_o, nin_o, nout_o, gain_o,
    ra1, rb1, a2, ra2, b2, rb2, c3, rc3, fin, rfin, send_sem, recv_sem,
    *, nz, factor,
):
    d = lax.axis_index("dom")
    rep = lax.axis_index("rep")
    z = d // 8
    y = (d // 2) % 4
    xt = (d % 2) * 2 + rep

    def at_y(p):
        return {"dom": z * 8 + p * 2 + d % 2}

    def at_z(p):
        return {"dom": p * 8 + d % 8}

    def at_x(p):
        return {"dom": (d // 2) * 2 + p // 2, "rep": p % 2}

    y_peers = [(y + j) % 4 for j in (1, 2, 3)]
    x_peers = [(xt + j) % 4 for j in (1, 2, 3)]
    z_peers = [(z + j) % nz for j in range(1, nz)]
    barrier = pltpu.get_barrier_semaphore()
    for p in y_peers:
        pl.semaphore_signal(barrier, inc=1, device_id=at_y(p), device_id_type=MESH)
    for p in x_peers:
        pl.semaphore_signal(barrier, inc=1, device_id=at_x(p), device_id_type=MESH)
    for p in z_peers:
        pl.semaphore_signal(barrier, inc=1, device_id=at_z(p), device_id_type=MESH)
    pl.semaphore_wait(barrier, 6 + nz - 1)

    def copy(n, src, dst, device):
        return pltpu.make_async_remote_copy(
            src_ref=src,
            dst_ref=dst,
            send_sem=send_sem.at[n],
            recv_sem=recv_sem.at[n],
            device_id=device,
            device_id_type=MESH,
        )

    first_a = [copy(j, ga.at[p], ra1.at[j], at_y(p)) for j, p in enumerate(y_peers)]
    first_b = [copy(3 + j, gb.at[p], rb1.at[j], at_x(p)) for j, p in enumerate(x_peers)]
    for u, v in zip(first_a, first_b):
        u.start()
        v.start()

    for c in first_a:
        c.wait_recv()
    rows_a = ga.shape[1]

    @pl.loop(0, rows_a // 16)
    def _(i):
        at = pl.ds(pl.multiple_of(i * 16, 16), 16)
        total = ga[y, at, :].astype(jnp.float32)
        for j in range(3):
            total = total + ra1[j, at, :].astype(jnp.float32)
        total = total.astype(jnp.bfloat16)
        for b in range(4):
            a2[b, at, :] = total[:, b * 128 : (b + 1) * 128]

    second_a = [copy(6 + j, a2.at[p], ra2.at[j], at_x(p)) for j, p in enumerate(x_peers)]
    for c in second_a:
        c.start()

    for c in first_b:
        c.wait_recv()

    @pl.loop(0, nz)
    def _(i):
        for q in range(4):
            total = gb[xt, i * 4 + q].astype(jnp.float32)
            for j in range(3):
                total = total + rb1[j, i * 4 + q].astype(jnp.float32)
            b2[q, i] = total.astype(jnp.bfloat16)

    second_b = [copy(9 + j, b2.at[p], rb2.at[j], at_y(p)) for j, p in enumerate(y_peers)]
    for c in second_b:
        c.start()

    for c in second_a:
        c.wait_recv()
    tail = pl.ds(nz * ROWS_A, GAIN)
    gains = a2[xt, tail, :].astype(jnp.float32)
    for j in range(3):
        gains = gains + ra2[j, tail, :].astype(jnp.float32)
    gains = gains.astype(jnp.bfloat16)

    @pl.loop(0, nz)
    def _(i):
        at = pl.ds(pl.multiple_of(i * ROWS_A, 16), ROWS_A)
        total = a2[xt, at, :].astype(jnp.float32)
        for j in range(3):
            total = total + ra2[j, at, :].astype(jnp.float32)
        c3[i, 0:ROWS_A, :] = total.astype(jnp.bfloat16)
        c3[i, ROWS_A : ROWS_A + GAIN, :] = gains

    for c in second_b:
        c.wait_recv()

    @pl.loop(0, nz)
    def _(i):
        total = b2[y, i].astype(jnp.float32)
        for j in range(3):
            total = total + rb2[j, i].astype(jnp.float32)
        c3[i, ROWS_A + GAIN :, :] = total.astype(jnp.bfloat16)

    third = [copy(12 + j, c3.at[p], rc3.at[j], at_z(p)) for j, p in enumerate(z_peers)]
    for c in third:
        c.start()
    total = c3[z].astype(jnp.float32)
    for j, c in enumerate(third):
        c.wait_recv()
        total = total + rc3[j].astype(jnp.float32)
    total = total * factor

    n0 = ROWS_A + GAIN
    for b in range(4):
        fin[b, 0:12, :] = total[12 * b : 12 * b + 12]
        fin[b, 12:16, :] = total[n0 + 32 + 4 * b : n0 + 32 + 4 * b + 4]
        fin[b, 16:24, :] = total[n0 + 8 * b : n0 + 8 * b + 8]
        fin[b, 24:28, :] = total[n0 + 48 + 4 * b : n0 + 48 + 4 * b + 4]
        fin[b, 28:32, :] = total[ROWS_A : ROWS_A + 4]
    base = 12 + nz - 1
    last = [copy(base + j, fin.at[p], rfin.at[xt], at_x(p)) for j, p in enumerate(x_peers)]
    for c in last:
        c.start()
    rfin[xt] = fin[xt]
    for c in last:
        c.wait_recv()
    t = d * 2 + rep
    lane = lax.broadcasted_iota(jnp.int32, (2, 128), 1)
    slot = lax.broadcasted_iota(jnp.int32, (2, 128), 1)
    picked = jnp.zeros((2, 128), jnp.float32)
    for b in range(4):
        cols = slice(b * 128, (b + 1) * 128)
        ein_o[:, cols] = rfin[b, 0:12, :]
        eout_o[:, cols] = rfin[b, 12:16, :]
        nin_o[:, cols] = rfin[b, 16:24, :]
        nout_o[:, cols] = rfin[b, 24:28, :]
        pair = rfin[b, 28:30, :]
        for i in range(4):
            hit = jnp.where(lane + b * 128 == t * 4 + i, pair, 0.0)
            value = jnp.sum(hit, axis=1, keepdims=True)
            picked = picked + jnp.where(slot == i, value, 0.0)
    gain_o[...] = picked
    for c in first_a + first_b + second_a + second_b + third + last:
        c.wait_send()


def reduce_call(ga, gb, factor):
    nz = ga.shape[1] // ROWS_A
    bf, f4 = jnp.bfloat16, jnp.float32
    rows = ga.shape[1]
    vm = pl.BlockSpec(memory_space=pltpu.VMEM)
    copies = 12 + nz - 1 + 3
    return pl.pallas_call(
        functools.partial(reduce_kernel, nz=nz, factor=factor),
        out_shape=[
            jax.ShapeDtypeStruct((12, 512), f4),
            jax.ShapeDtypeStruct((4, 512), f4),
            jax.ShapeDtypeStruct((8, 512), f4),
            jax.ShapeDtypeStruct((4, 512), f4),
            jax.ShapeDtypeStruct((2, 128), f4),
        ],
        in_specs=[vm, vm],
        out_specs=[vm] * 5,
        scratch_shapes=[
            pltpu.VMEM((3, rows, 512), bf),
            pltpu.VMEM((3, 4 * nz, ROWS_B, 128), bf),
            pltpu.VMEM((4, rows, 128), bf),
            pltpu.VMEM((3, rows, 128), bf),
            pltpu.VMEM((4, nz, ROWS_B, 128), bf),
            pltpu.VMEM((3, nz, ROWS_B, 128), bf),
            pltpu.VMEM((nz, 128, 128), bf),
            pltpu.VMEM((nz - 1, 128, 128), bf),
            pltpu.VMEM((4, 32, 128), f4),
            pltpu.VMEM((4, 32, 128), f4),
            pltpu.SemaphoreType.DMA((copies,)),
            pltpu.SemaphoreType.DMA((copies,)),
        ],
        compiler_params=pltpu.CompilerParams(
            collective_id=1, has_side_effects=True, vmem_limit_bytes=40 << 20
        ),
        name="grad_reduce_scatter",
    )(ga, gb)


NODES_DEV = 128
EDGES_DEV = 384
HALOS = 64
TABLE = 192
BLOCK = 32
BF = jnp.bfloat16
F4 = jnp.float32


def mm(a, b):
    return jnp.dot(a, b, preferred_element_type=F4)


def mm_nt(a, b):
    return lax.dot_general(a, b, (((1,), (1,)), ((), ())), preferred_element_type=F4)


def mm_tn(a, b):
    return lax.dot_general(a, b, (((0,), (0,)), ((), ())), preferred_element_type=F4)


def silu_grad(pre):
    sig = jax.nn.sigmoid(pre)
    return sig * (1.0 + pre * (1.0 - sig))


def layer_kernel(
    src_row, dst_row, send_row, count, node_in, edge_in, cot_in,
    w_ein, w_eout, w_nin, w_nout, gain_e, gain_n,
    node_out, edge_out, ga, gb,
    oht, oh, inc, inct, sendt, sendm,
    tab, ein, cn, ce, cn32, halo1, halo2, hs1, hs2, bh,
    sr, pre, mid, tmp, xhat, rstd, enew, agg, pren, midn, tmpn, xhatn, rstdn, hnew,
    doutn, dpren, down, dagg, doute, dpre, gs, gr, de, dh, dge, dgn,
    s_halo1, s_halo2, r_halo, s_fe, r_fe, s_fh, r_fh,
    s_bh, r_bh1, r_bh2, s_be, r_be, s_bo, r_bo,
    l_node, l_edge, l_cot, l_nout, l_eout,
):
    seg = lax.axis_index("segment")
    dom = lax.axis_index("dom")
    n_dom = lax.axis_size("dom")
    first = seg == 0
    second = seg == 1

    def near(step, segment):
        return {"dom": (dom + step + n_dom) % n_dom, "segment": segment}

    barrier = pltpu.get_barrier_semaphore()
    for step in OFFSETS:
        for s in range(2):
            pl.semaphore_signal(barrier, inc=1, device_id=near(step, s), device_id_type=MESH)
    pl.semaphore_signal(barrier, inc=1, device_id={"segment": 1 - seg}, device_id_type=MESH)

    def remote(src, dst, send, recv, device):
        return pltpu.make_async_remote_copy(
            src_ref=src, dst_ref=dst, send_sem=send, recv_sem=recv,
            device_id=device, device_id_type=MESH,
        )

    def load_node(k):
        return pltpu.make_async_copy(node_in.at[k], tab.at[k, 0:NODES_DEV], l_node.at[k])

    def load_edge(k):
        return pltpu.make_async_copy(edge_in.at[k], ein.at[k], l_edge.at[k])

    def load_cot(k):
        return pltpu.make_async_copy(cot_in.at[k], cn.at[k], l_cot.at[k])

    def store_node(src, k):
        return pltpu.make_async_copy(src.at[k], node_out.at[k], l_nout.at[k])

    def store_edge(src, k):
        return pltpu.make_async_copy(src.at[k], edge_out.at[k], l_eout.at[k])

    def halo_copy(src, k, j, sems, segment):
        rows = slice(j * HALO, (j + 1) * HALO)
        into = slice(NODES_DEV + j * HALO, NODES_DEV + (j + 1) * HALO)
        return remote(
            src.at[k, rows], tab.at[k, into], sems.at[k, j], r_halo.at[k, j],
            near(OFFSETS[j], segment),
        )

    def back_copy(dst, k, j, recv):
        rows = slice(j * HALO, (j + 1) * HALO)
        return remote(
            bh.at[k, rows], dst.at[k, rows], s_bh.at[k, j], recv.at[k, j],
            near(-OFFSETS[j], 0),
        )

    def sib_e(k):
        return remote(enew.at[k], ein.at[k], s_fe.at[k], r_fe.at[k], {"segment": 1 - seg})

    def sib_h(k):
        return remote(
            hnew.at[k], tab.at[k, 0:NODES_DEV], s_fh.at[k], r_fh.at[k], {"segment": 1 - seg}
        )

    def sib_de(k):
        return remote(de.at[k], ce.at[k], s_be.at[k], r_be.at[k], {"segment": 1 - seg})

    def sib_do(k):
        return remote(down.at[k], cn32.at[k], s_bo.at[k], r_bo.at[k], {"segment": 1 - seg})

    @pl.when(first)
    def _():
        for k in range(2):
            load_node(k).start()
            load_edge(k).start()

    @pl.when(second)
    def _():
        for k in range(2):
            load_cot(k).start()

    live_count = count[0]
    hot_src = lax.broadcasted_iota(jnp.int32, (TABLE, EDGES_DEV), 0) == src_row[...]
    owner = lax.broadcasted_iota(jnp.int32, (NODES_DEV, EDGES_DEV), 0)
    slot = lax.broadcasted_iota(jnp.int32, (NODES_DEV, EDGES_DEV), 1)
    hot_dst = owner == dst_row[...]
    hot_inc = hot_dst & (slot < live_count)
    f_src = jnp.where(hot_src, 1.0, 0.0)
    f_dst = jnp.where(hot_dst, 1.0, 0.0)
    f_inc = jnp.where(hot_inc, 1.0, 0.0)
    oht[0:TABLE] = f_src.astype(BF)
    oht[TABLE:] = f_dst.astype(BF)
    inc[...] = f_inc.astype(BF)
    oh[:, 0:TABLE] = f_src.T.astype(BF)
    oh[:, TABLE:] = f_dst.T.astype(BF)
    inct[...] = f_inc.T.astype(BF)
    f_send = jnp.where(
        lax.broadcasted_iota(jnp.int32, (NODES_DEV, NODES_DEV), 0) == send_row[...], 1.0, 0.0
    )
    sendt[...] = f_send.astype(BF)
    sendm[...] = f_send.T.astype(BF)
    dge[...] = jnp.zeros_like(dge)
    dgn[...] = jnp.zeros_like(dgn)

    @pl.when(second)
    def _():
        ce[...] = jnp.zeros_like(ce)

    pl.semaphore_wait(barrier, 2 * len(OFFSETS) + 1)

    @pl.when(first)
    def _():
        for k in range(2):
            load_node(k).wait()
            hs1[k] = mm(sendm[0:HALOS], tab[k, 0:NODES_DEV]).astype(BF)
            for j in range(4):
                halo_copy(hs1, k, j, s_halo1, 0).start()

    def mean(v):
        return jnp.sum(v, axis=-1, keepdims=True) * (1.0 / 512.0)

    def norm_block(outer, at, k, x_ref, r_ref):
        center = outer - mean(outer)
        inv = lax.rsqrt(mean(center * center) + EPS)
        hat = center * inv
        x_ref[k, at, :] = hat
        r_ref[k, at, :] = jnp.broadcast_to(inv, (BLOCK, 128))
        return hat

    def norm_back(cot, gain, hat, inv):
        dy = cot * gain
        return inv * (dy - mean(dy) - hat * mean(dy * hat))

    def forward(k):
        @pl.when(first)
        def _():
            load_edge(k).wait()

        @pl.when(second)
        def _():
            sib_e(k).wait_recv()

        pre[k] = mm(ein[k], w_ein[0:512])

        @pl.when(second)
        def _():
            sib_h(k).wait_recv()

        own = tab[k, 0:NODES_DEV]
        sr[TABLE:] = mm(own, w_ein[1024:1536]).astype(BF)
        for j in range(4):
            halo_copy(hs1, k, j, s_halo1, 0).wait_recv()
        sr[0:TABLE] = mm(tab[k], w_ein[512:1024]).astype(BF)
        tmp[...] = mm(oh[...], sr[...])

        @pl.loop(0, EDGES_DEV // BLOCK)
        def _(i):
            at = pl.ds(pl.multiple_of(i * BLOCK, BLOCK), BLOCK)
            v = pre[k, at, :] + tmp[at, :]
            pre[k, at, :] = v
            mid[k, at, :] = (v * jax.nn.sigmoid(v)).astype(BF)

        tmp[...] = mm(mid[k], w_eout[...])

        @pl.loop(0, EDGES_DEV // BLOCK)
        def _(i):
            at = pl.ds(pl.multiple_of(i * BLOCK, BLOCK), BLOCK)
            hat = norm_block(tmp[at, :], at, k, xhat, rstd)
            rows = lax.broadcasted_iota(jnp.int32, (BLOCK, 512), 0) + i * BLOCK
            old = ein[k, at, :].astype(F4)
            enew[k, at, :] = jnp.where(rows < live_count, old + hat * gain_e[...], old).astype(BF)

        @pl.when(first)
        def _():
            sib_e(k).start()

        @pl.when(second)
        def _():
            store_edge(enew, k).start()

        agg[k] = mm(inc[...], enew[k]).astype(BF)
        pren[k] = mm(own, w_nin[0:512]) + mm(agg[k], w_nin[512:1024])

        @pl.loop(0, NODES_DEV // BLOCK)
        def _(i):
            at = pl.ds(pl.multiple_of(i * BLOCK, BLOCK), BLOCK)
            v = pren[k, at, :]
            midn[k, at, :] = (v * jax.nn.sigmoid(v)).astype(BF)

        tmpn[...] = mm(midn[k], w_nout[...])

        @pl.loop(0, NODES_DEV // BLOCK)
        def _(i):
            at = pl.ds(pl.multiple_of(i * BLOCK, BLOCK), BLOCK)
            hat = norm_block(tmpn[at, :], at, k, xhatn, rstdn)
            hnew[k, at, :] = (tab[k, at, :].astype(F4) + hat * gain_n[...]).astype(BF)

        @pl.when(first)
        def _():
            sib_h(k).start()
            hs2[k] = mm(sendm[0:HALOS], hnew[k]).astype(BF)
            for j in range(4):
                halo_copy(hs2, k, j, s_halo2, 1).start()

        @pl.when(second)
        def _():
            store_node(hnew, k).start()

    def backward(k):
        @pl.when(first)
        def _():
            sib_do(k).wait_recv()
            for j in range(4):
                back_copy(halo1, k, j, r_bh1).wait_recv()
            cn[k] = (cn32[k] + mm(sendt[:, 0:HALOS], halo1[k])).astype(BF)

        @pl.when(second)
        def _():
            load_cot(k).wait()

        @pl.loop(0, NODES_DEV // BLOCK)
        def _(i):
            at = pl.ds(pl.multiple_of(i * BLOCK, BLOCK), BLOCK)
            cot = cn[k, at, :].astype(F4)
            hat = xhatn[k, at, :]
            dgn[...] += jnp.sum((cot * hat).reshape(BLOCK // 8, 8, 512), axis=0)
            inv = rstdn[k, at, 0:1]
            doutn[k, at, :] = norm_back(cot, gain_n[...], hat, inv).astype(BF)

        tmpn[...] = mm_nt(doutn[k], w_nout[...])

        @pl.loop(0, NODES_DEV // BLOCK)
        def _(i):
            at = pl.ds(pl.multiple_of(i * BLOCK, BLOCK), BLOCK)
            dpren[k, at, :] = (tmpn[at, :] * silu_grad(pren[k, at, :])).astype(BF)

        dagg[...] = mm_nt(dpren[k], w_nin[512:1024]).astype(BF)

        @pl.when(first)
        def _():
            sib_de(k).wait_recv()

        tmp[...] = mm(inct[...], dagg[...])
        down[k] = cn[k].astype(F4) + mm_nt(dpren[k], w_nin[0:512])

        @pl.loop(0, EDGES_DEV // BLOCK)
        def _(i):
            at = pl.ds(pl.multiple_of(i * BLOCK, BLOCK), BLOCK)
            cot = tmp[at, :] + ce[k, at, :].astype(F4)
            tmp[at, :] = cot
            rows = lax.broadcasted_iota(jnp.int32, (BLOCK, 512), 0) + i * BLOCK
            cot = jnp.where(rows < live_count, cot, 0.0)
            hat = xhat[k, at, :]
            dge[...] += jnp.sum((cot * hat).reshape(BLOCK // 8, 8, 512), axis=0)
            inv = rstd[k, at, 0:1]
            doute[k, at, :] = norm_back(cot, gain_e[...], hat, inv).astype(BF)

        grad = mm_nt(doute[k], w_eout[...])
        pre[k] = grad * silu_grad(pre[k])
        dpre[k] = pre[k].astype(BF)
        gs[k] = mm(oht[0:TABLE], dpre[k]).astype(BF)
        gr[k] = mm(oht[TABLE:], dpre[k]).astype(BF)
        bh[k] = mm_nt(gs[k, NODES_DEV:], w_ein[512:1024]).astype(BF)

        @pl.when(first)
        def _():
            for j in range(4):
                back_copy(halo2, k, j, r_bh2).start()

        @pl.when(second)
        def _():
            for j in range(4):
                back_copy(halo1, k, j, r_bh1).start()

        down[k] += mm_nt(gs[k, 0:NODES_DEV], w_ein[512:1024]) + mm_nt(gr[k], w_ein[1024:1536])

        @pl.when(second)
        def _():
            sib_do(k).start()

        de[k] = (tmp[...] + mm_nt(dpre[k], w_ein[0:512])).astype(BF)

        @pl.when(second)
        def _():
            sib_de(k).start()

        @pl.when(first)
        def _():
            store_edge(de, k).start()

    @pl.loop(0, 4)
    def _(step):
        forward_now = (step == 0) | (step == 1 + seg)
        k = jnp.where(first, step % 2, step // 2)

        @pl.when(forward_now)
        def _():
            forward(k)

        @pl.when(jnp.logical_not(forward_now))
        def _():
            backward(k)

    def put_ein(base, value):
        for q in range(8):
            r = base + q * 16
            row = (r // 192) * ROWS_A + r % ROWS_A
            ga[(r % 192) // ROWS_A, row : row + 16, :] = value[q * 16 : q * 16 + 16].astype(BF)

    def put_b(base, width, offset, value):
        for q in range(128 // width):
            zy = base // width + q
            piece = value[q * width : (q + 1) * width].astype(BF)
            for b in range(4):
                gb[b, zy, offset : offset + width, :] = piece[:, b * 128 : (b + 1) * 128]

    def both(ref):
        return ref[...].reshape(ref.shape[0] * ref.shape[1], ref.shape[2])

    def cols(ref, m):
        return jnp.concatenate([ref[0, :, m * 128 : (m + 1) * 128], ref[1, :, m * 128 : (m + 1) * 128]], axis=0)

    def own_cols(m):
        at = slice(m * 128, (m + 1) * 128)
        return jnp.concatenate([tab[0, 0:NODES_DEV, at], tab[1, 0:NODES_DEV, at]], axis=0)

    for m in range(4):
        base = m * 128
        put_b(base, 16, 48, mm_tn(cols(midn, m), both(doutn)))
        put_b(base, 32, 0, mm_tn(own_cols(m), both(dpren)))
        put_b(512 + base, 32, 0, mm_tn(cols(agg, m), both(dpren)))
        put_b(base, 16, 32, mm_tn(cols(mid, m), both(doute)))
        put_ein(base, mm_tn(cols(ein, m), both(dpre)))
        put_ein(512 + base, mm_tn(cols(tab, m), both(gs)))
        put_ein(1024 + base, mm_tn(own_cols(m), both(gr)))
    row = lax.broadcasted_iota(jnp.int32, (GAIN, 512), 0)
    sum_e = jnp.sum(dge[...], axis=0, keepdims=True)
    sum_n = jnp.sum(dgn[...], axis=0, keepdims=True)
    gains = jnp.where(row == 0, sum_e, jnp.where(row == 1, sum_n, 0.0)).astype(BF)
    for q in range(4):
        ga[q, EDGES_DEV:, :] = gains

    @pl.when(first)
    def _():
        for k in range(2):
            for j in range(4):
                back_copy(halo2, k, j, r_bh2).wait_recv()
            dh[k] = (down[k] + mm(sendt[:, 0:HALOS], halo2[k])).astype(BF)
            store_node(dh, k).start()
        for k in range(2):
            sib_e(k).wait_send()
            sib_h(k).wait_send()
            for j in range(4):
                halo_copy(hs1, k, j, s_halo1, 0).wait_send()
                halo_copy(hs2, k, j, s_halo2, 1).wait_send()
                back_copy(halo2, k, j, r_bh2).wait_send()
            store_edge(de, k).wait()
            store_node(dh, k).wait()

    @pl.when(second)
    def _():
        for k in range(2):
            sib_do(k).wait_send()
            sib_de(k).wait_send()
            for j in range(4):
                back_copy(halo1, k, j, r_bh1).wait_send()
            store_edge(enew, k).wait()
            store_node(hnew, k).wait()


def layer_call(src, dst, send, count, node, edge, cot, weights, gains):
    vm = pl.BlockSpec(memory_space=pltpu.VMEM)
    hbm = pl.BlockSpec(memory_space=pl.ANY)
    smem = pl.BlockSpec(memory_space=pltpu.SMEM)
    nz = 8

    def bf(*shape):
        return pltpu.VMEM(shape, BF)

    def fl(*shape):
        return pltpu.VMEM(shape, F4)

    dma = pltpu.SemaphoreType.DMA
    n, e = NODES_DEV, EDGES_DEV
    return pl.pallas_call(
        layer_kernel,
        out_shape=[
            jax.ShapeDtypeStruct((2, n, 512), BF),
            jax.ShapeDtypeStruct((2, e, 512), BF),
            jax.ShapeDtypeStruct((4, nz * ROWS_A + GAIN, 512), BF),
            jax.ShapeDtypeStruct((4, nz * 4, ROWS_B, 128), BF),
        ],
        in_specs=[vm, vm, vm, smem, hbm, hbm, hbm] + [vm] * 6,
        out_specs=[hbm, hbm, vm, vm],
        scratch_shapes=[
            bf(320, e), bf(e, 320), bf(n, e), bf(e, n), bf(n, n), bf(n, n),
            bf(2, TABLE, 512), bf(2, e, 512), bf(2, n, 512), bf(2, e, 512), fl(2, n, 512),
            bf(2, HALOS, 512), bf(2, HALOS, 512), bf(2, HALOS, 512), bf(2, HALOS, 512), bf(2, HALOS, 512),
            bf(320, 512), fl(2, e, 512), bf(2, e, 512), fl(e, 512), fl(2, e, 512), fl(2, e, 128),
            bf(2, e, 512), bf(2, n, 512), fl(2, n, 512), bf(2, n, 512), fl(n, 512), fl(2, n, 512),
            fl(2, n, 128), bf(2, n, 512),
            bf(2, n, 512), bf(2, n, 512), fl(2, n, 512), bf(n, 512), bf(2, e, 512), bf(2, e, 512),
            bf(2, TABLE, 512), bf(2, n, 512), bf(2, e, 512), bf(2, n, 512), fl(8, 512), fl(8, 512),
            dma((2, 4)), dma((2, 4)), dma((2, 4)), dma((2,)), dma((2,)), dma((2,)), dma((2,)),
            dma((2, 4)), dma((2, 4)), dma((2, 4)), dma((2,)), dma((2,)), dma((2,)), dma((2,)),
            dma((2,)), dma((2,)), dma((2,)), dma((2,)), dma((2,)),
        ],
        compiler_params=pltpu.CompilerParams(
            collective_id=0, has_side_effects=True, vmem_limit_bytes=50 << 20
        ),
        name="layers",
    )(src, dst, send, count, node, edge, cot, *weights, *gains)


def body(
    node_latent, edge_latent, node_cot, edge_src, edge_dst, edge_count, send_index,
    w_edge_in, w_edge_out, w_node_in, w_node_out, gain_edge, gain_node,
):
    micro = node_latent.shape[0]
    factor = float(micro * lax.axis_size("rep") * NODES_DEV * lax.axis_size("dom")) ** (-0.5)
    send = jnp.pad(send_index.reshape(1, HALOS), ((0, 0), (0, NODES_DEV - HALOS)), constant_values=-1)
    node_out, edge_out, ga, gb = layer_call(
        edge_src.reshape(1, EDGES_DEV), edge_dst.reshape(1, EDGES_DEV), send, edge_count,
        node_latent, edge_latent, node_cot,
        (w_edge_in[0], w_edge_out[0], w_node_in[0], w_node_out[0]), (gain_edge, gain_node),
    )
    *shares, picked = reduce_call(ga, gb, factor)
    scaled = [piece[None] for piece in shares]
    return (node_out[None], edge_out[None], *scaled, picked[0:1, :4], picked[1:2, :4])


def solution(mesh):
    placed = (
        P("rep", "dom", None),
        P("rep", "dom", None),
        P("rep", "dom", None),
        P("dom"),
        P("dom"),
        P("dom"),
        P("dom", None, None),
        P("segment", None, None),
        P("segment", None, None),
        P("segment", None, None),
        P("segment", None, None),
        P("segment", None),
        P("segment", None),
    )
    return jax.shard_map(
        body,
        mesh=mesh,
        in_specs=placed,
        out_specs=(
            P("segment", "rep", "dom", None),
            P("segment", "rep", "dom", None),
            P("segment", ("dom", "rep"), None),
            P("segment", ("dom", "rep"), None),
            P("segment", ("dom", "rep"), None),
            P("segment", ("dom", "rep"), None),
            P("segment", ("dom", "rep")),
            P("segment", ("dom", "rep")),
        ),
        check_vma=False,
    )
```

```python
import functools

import jax
import jax.numpy as jnp
from jax import lax
from jax.experimental import pallas as pl
from jax.experimental.pallas import tpu as pltpu
from jax.sharding import PartitionSpec as P

OFFSETS = (1, -1, 2, -2)
HALO = 16
EPS = 1e-05
MESH = pl.DeviceIdType.MESH
ROWS_A = 48
ROWS_B = 64
GAIN = 16
NODES_DEV = 128
EDGES_DEV = 384
HALOS = 64
TABLE = 192
BLOCK = 32
BF = jnp.bfloat16
F4 = jnp.float32


def mm(a, b):
    return jnp.dot(a, b, preferred_element_type=F4)


def mm_nt(a, b):
    return lax.dot_general(a, b, (((1,), (1,)), ((), ())), preferred_element_type=F4)


def mm_tn(a, b):
    return lax.dot_general(a, b, (((0,), (0,)), ((), ())), preferred_element_type=F4)


def silu_grad(pre):
    sig = jax.nn.sigmoid(pre)
    return sig * (1.0 + pre * (1.0 - sig))


def layer_kernel(
    src_in, dst_in, send_in, count_in, node_in, edge_in, cot_in,
    w_ein_in, w_eout_in, w_nin_in, w_nout_in, gain_e_in, gain_n_in,
    node_out, edge_out, fin_out,
    src_row, dst_row, send_row, count, w_ein, w_eout, w_nin, w_nout, gain_e, gain_n, l_first,
    oht, oh, inc, inct, sendt, sendm,
    tab, ein, cn, ce, cn32, halo1, halo2, hs1, hs2, bh,
    sr, pre, mid, tmp, xhat, rstd, enew, agg, pren, midn, tmpn, xhatn, rstdn, hnew,
    doutn, dpren, down, dagg, doute, dpre, gs, gr, de, dh, dge, dgn,
    s_halo1, s_halo2, r_halo, s_fe, r_fe, s_fh, r_fh,
    s_bh, r_bh1, r_bh2, s_be, r_be, s_bo, r_bo,
    l_node, l_edge, l_cot, l_nout, l_eout,
    ga, gb, ta, ua, va, tb, ub, vb, a2, ta2, ua2, va2, b2, tb2, ub2, vb2, c3, rc3, fin, rfin,
    send_sem, recv_sem, l_fin,
    *, nz, factor,
):
    seg = lax.axis_index("segment")
    dom = lax.axis_index("dom")
    n_dom = lax.axis_size("dom")
    first = seg == 0
    second = seg == 1

    def near(step, segment):
        return {"dom": (dom + step + n_dom) % n_dom, "segment": segment}

    rep = lax.axis_index("rep")
    z = dom // 8
    y = (dom // 2) % 4
    px = rep * 2 + dom % 2

    def at_y(p):
        return {"dom": z * 8 + p * 2 + dom % 2}

    def at_z(p):
        return {"dom": p * 8 + dom % 8}

    def at_x(p):
        return {"dom": (dom // 2) * 2 + p % 2, "rep": p // 2}

    z_peers = [(z + j) % nz for j in range(1, nz)]
    x_peers = [(px + j) % 4 for j in range(1, 4)]
    greet = [near(step, s) for step in OFFSETS for s in range(2)]
    greet += [at_y((y + 1) % 4), at_y((y + 3) % 4)]
    greet += [at_x(p) for p in x_peers] + [at_z(p) for p in z_peers]
    greet += [{"segment": 1 - seg}]
    barrier = pltpu.get_barrier_semaphore()
    for device in greet:
        pl.semaphore_signal(barrier, inc=1, device_id=device, device_id_type=MESH)

    def remote(src, dst, send, recv, device):
        return pltpu.make_async_remote_copy(
            src_ref=src, dst_ref=dst, send_sem=send, recv_sem=recv,
            device_id=device, device_id_type=MESH,
        )

    def load_node(k):
        return pltpu.make_async_copy(node_in.at[k], tab.at[k, 0:NODES_DEV], l_node.at[k])

    def load_edge(k):
        return pltpu.make_async_copy(edge_in.at[k], ein.at[k], l_edge.at[k])

    def load_cot(k):
        return pltpu.make_async_copy(cot_in.at[k], cn.at[k], l_cot.at[k])

    def store_node(src, k):
        return pltpu.make_async_copy(src.at[k], node_out.at[k], l_nout.at[k])

    def store_edge(src, k):
        return pltpu.make_async_copy(src.at[k], edge_out.at[k], l_eout.at[k])

    def halo_copy(src, k, j, sems, segment):
        rows = slice(j * HALO, (j + 1) * HALO)
        into = slice(NODES_DEV + j * HALO, NODES_DEV + (j + 1) * HALO)
        return remote(
            src.at[k, rows], tab.at[k, into], sems.at[k, j], r_halo.at[k, j],
            near(OFFSETS[j], segment),
        )

    def back_copy(dst, k, j, recv):
        rows = slice(j * HALO, (j + 1) * HALO)
        return remote(
            bh.at[k, rows], dst.at[k, rows], s_bh.at[k, j], recv.at[k, j],
            near(-OFFSETS[j], 0),
        )

    def sib_e(k):
        return remote(enew.at[k], ein.at[k], s_fe.at[k], r_fe.at[k], {"segment": 1 - seg})

    def sib_h(k):
        return remote(
            hnew.at[k], tab.at[k, 0:NODES_DEV], s_fh.at[k], r_fh.at[k], {"segment": 1 - seg}
        )

    def sib_de(k):
        return remote(de.at[k], ce.at[k], s_be.at[k], r_be.at[k], {"segment": 1 - seg})

    def sib_do(k):
        return remote(down.at[k], cn32.at[k], s_bo.at[k], r_bo.at[k], {"segment": 1 - seg})

    small = [
        pltpu.make_async_copy(u, v, l_first.at[i])
        for i, (u, v) in enumerate(
            [
                (src_in, src_row), (dst_in, dst_row), (send_in, send_row), (count_in, count),
                (gain_e_in, gain_e), (gain_n_in, gain_n),
            ]
        )
    ]
    large = [
        pltpu.make_async_copy(u.at[0], v, l_first.at[6 + i])
        for i, (u, v) in enumerate(
            [(w_ein_in, w_ein), (w_eout_in, w_eout), (w_nin_in, w_nin), (w_nout_in, w_nout)]
        )
    ]
    for c in small:
        c.start()

    @pl.when(first)
    def _():
        for k in range(2):
            load_node(k).start()
            load_edge(k).start()

    @pl.when(second)
    def _():
        for k in range(2):
            load_cot(k).start()

    for c in large:
        c.start()
    for c in small:
        c.wait()
    live_count = count[0]
    hot_src = lax.broadcasted_iota(jnp.int32, (TABLE, EDGES_DEV), 0) == src_row[...].reshape(1, EDGES_DEV)
    owner = lax.broadcasted_iota(jnp.int32, (NODES_DEV, EDGES_DEV), 0)
    slot = lax.broadcasted_iota(jnp.int32, (NODES_DEV, EDGES_DEV), 1)
    hot_dst = owner == dst_row[...].reshape(1, EDGES_DEV)
    hot_inc = hot_dst & (slot < live_count)
    f_src = jnp.where(hot_src, 1.0, 0.0)
    f_dst = jnp.where(hot_dst, 1.0, 0.0)
    f_inc = jnp.where(hot_inc, 1.0, 0.0)
    oht[0:TABLE] = f_src.astype(BF)
    oht[TABLE:] = f_dst.astype(BF)
    inc[...] = f_inc.astype(BF)
    oh[:, 0:TABLE] = f_src.T.astype(BF)
    oh[:, TABLE:] = f_dst.T.astype(BF)
    inct[...] = f_inc.T.astype(BF)
    node = lax.broadcasted_iota(jnp.int32, (NODES_DEV, HALO), 0)
    hots = [jnp.where(node == send_row[0, j : j + 1, :], 1.0, 0.0) for j in range(4)]
    f_send = jnp.concatenate(hots + [jnp.zeros((NODES_DEV, NODES_DEV - HALOS), F4)], axis=1)
    sendt[...] = f_send.astype(BF)
    sendm[...] = f_send.T.astype(BF)
    dge[...] = jnp.zeros_like(dge)
    dgn[...] = jnp.zeros_like(dgn)

    @pl.when(second)
    def _():
        ce[...] = jnp.zeros_like(ce)

    pl.semaphore_wait(barrier, len(greet))

    for c in large:
        c.wait()

    @pl.when(first)
    def _():
        for k in range(2):
            load_node(k).wait()
            hs1[k] = mm(sendm[0:HALOS], tab[k, 0:NODES_DEV]).astype(BF)
            for j in range(4):
                halo_copy(hs1, k, j, s_halo1, 0).start()

    def mean(v):
        return jnp.sum(v, axis=-1, keepdims=True) * (1.0 / 512.0)

    def norm_block(outer, at, k, x_ref, r_ref):
        center = outer - mean(outer)
        inv = lax.rsqrt(mean(center * center) + EPS)
        hat = center * inv
        x_ref[k, at, :] = hat
        r_ref[k, at, :] = jnp.broadcast_to(inv, (BLOCK, 128))
        return hat

    def norm_back(cot, gain, hat, inv):
        dy = cot * gain
        return inv * (dy - mean(dy) - hat * mean(dy * hat))

    def forward(k):
        @pl.when(first)
        def _():
            load_edge(k).wait()

        @pl.when(second)
        def _():
            sib_e(k).wait_recv()

        pre[k] = mm(ein[k], w_ein[0:512])

        @pl.when(second)
        def _():
            sib_h(k).wait_recv()

        own = tab[k, 0:NODES_DEV]
        sr[TABLE:] = mm(own, w_ein[1024:1536]).astype(BF)
        for j in range(4):
            halo_copy(hs1, k, j, s_halo1, 0).wait_recv()
        sr[0:TABLE] = mm(tab[k], w_ein[512:1024]).astype(BF)
        tmp[...] = mm(oh[...], sr[...])

        @pl.loop(0, EDGES_DEV // BLOCK)
        def _(i):
            at = pl.ds(pl.multiple_of(i * BLOCK, BLOCK), BLOCK)
            v = pre[k, at, :] + tmp[at, :]
            pre[k, at, :] = v
            mid[k, at, :] = (v * jax.nn.sigmoid(v)).astype(BF)

        tmp[...] = mm(mid[k], w_eout[...])

        @pl.loop(0, EDGES_DEV // BLOCK)
        def _(i):
            at = pl.ds(pl.multiple_of(i * BLOCK, BLOCK), BLOCK)
            hat = norm_block(tmp[at, :], at, k, xhat, rstd)
            rows = lax.broadcasted_iota(jnp.int32, (BLOCK, 512), 0) + i * BLOCK
            old = ein[k, at, :].astype(F4)
            enew[k, at, :] = jnp.where(rows < live_count, old + hat * gain_e[...], old).astype(BF)

        @pl.when(first)
        def _():
            sib_e(k).start()

        @pl.when(second)
        def _():
            store_edge(enew, k).start()

        agg[k] = mm(inc[...], enew[k]).astype(BF)
        pren[k] = mm(own, w_nin[0:512]) + mm(agg[k], w_nin[512:1024])

        @pl.loop(0, NODES_DEV // BLOCK)
        def _(i):
            at = pl.ds(pl.multiple_of(i * BLOCK, BLOCK), BLOCK)
            v = pren[k, at, :]
            midn[k, at, :] = (v * jax.nn.sigmoid(v)).astype(BF)

        tmpn[...] = mm(midn[k], w_nout[...])

        @pl.loop(0, NODES_DEV // BLOCK)
        def _(i):
            at = pl.ds(pl.multiple_of(i * BLOCK, BLOCK), BLOCK)
            hat = norm_block(tmpn[at, :], at, k, xhatn, rstdn)
            hnew[k, at, :] = (tab[k, at, :].astype(F4) + hat * gain_n[...]).astype(BF)

        @pl.when(first)
        def _():
            sib_h(k).start()
            hs2[k] = mm(sendm[0:HALOS], hnew[k]).astype(BF)
            for j in range(4):
                halo_copy(hs2, k, j, s_halo2, 1).start()

        @pl.when(second)
        def _():
            store_node(hnew, k).start()

    def backward(k):
        @pl.when(first)
        def _():
            sib_do(k).wait_recv()
            for j in range(4):
                back_copy(halo1, k, j, r_bh1).wait_recv()
            cn[k] = (cn32[k] + mm(sendt[:, 0:HALOS], halo1[k])).astype(BF)

        @pl.when(second)
        def _():
            load_cot(k).wait()

        @pl.loop(0, NODES_DEV // BLOCK)
        def _(i):
            at = pl.ds(pl.multiple_of(i * BLOCK, BLOCK), BLOCK)
            cot = cn[k, at, :].astype(F4)
            hat = xhatn[k, at, :]
            dgn[...] += jnp.sum((cot * hat).reshape(BLOCK // 8, 8, 512), axis=0)
            inv = rstdn[k, at, 0:1]
            doutn[k, at, :] = norm_back(cot, gain_n[...], hat, inv).astype(BF)

        tmpn[...] = mm_nt(doutn[k], w_nout[...])

        @pl.loop(0, NODES_DEV // BLOCK)
        def _(i):
            at = pl.ds(pl.multiple_of(i * BLOCK, BLOCK), BLOCK)
            dpren[k, at, :] = (tmpn[at, :] * silu_grad(pren[k, at, :])).astype(BF)

        dagg[...] = mm_nt(dpren[k], w_nin[512:1024]).astype(BF)

        @pl.when(first)
        def _():
            sib_de(k).wait_recv()

        tmp[...] = mm(inct[...], dagg[...])
        down[k] = cn[k].astype(F4) + mm_nt(dpren[k], w_nin[0:512])

        @pl.loop(0, EDGES_DEV // BLOCK)
        def _(i):
            at = pl.ds(pl.multiple_of(i * BLOCK, BLOCK), BLOCK)
            cot = tmp[at, :] + ce[k, at, :].astype(F4)
            tmp[at, :] = cot
            rows = lax.broadcasted_iota(jnp.int32, (BLOCK, 512), 0) + i * BLOCK
            cot = jnp.where(rows < live_count, cot, 0.0)
            hat = xhat[k, at, :]
            dge[...] += jnp.sum((cot * hat).reshape(BLOCK // 8, 8, 512), axis=0)
            inv = rstd[k, at, 0:1]
            doute[k, at, :] = norm_back(cot, gain_e[...], hat, inv).astype(BF)

        grad = mm_nt(doute[k], w_eout[...])
        pre[k] = grad * silu_grad(pre[k])
        dpre[k] = pre[k].astype(BF)
        gs[k] = mm(oht[0:TABLE], dpre[k]).astype(BF)
        gr[k] = mm(oht[TABLE:], dpre[k]).astype(BF)
        bh[k] = mm_nt(gs[k, NODES_DEV:], w_ein[512:1024]).astype(BF)

        @pl.when(first)
        def _():
            for j in range(4):
                back_copy(halo2, k, j, r_bh2).start()

        @pl.when(second)
        def _():
            for j in range(4):
                back_copy(halo1, k, j, r_bh1).start()

        down[k] += mm_nt(gs[k, 0:NODES_DEV], w_ein[512:1024]) + mm_nt(gr[k], w_ein[1024:1536])

        @pl.when(second)
        def _():
            sib_do(k).start()

        de[k] = (tmp[...] + mm_nt(dpre[k], w_ein[0:512])).astype(BF)

        @pl.when(second)
        def _():
            sib_de(k).start()

        @pl.when(first)
        def _():
            store_edge(de, k).start()

    @pl.loop(0, 4)
    def _(step):
        forward_now = (step == 0) | (step == 1 + seg)
        k = jnp.where(first, step % 2, step // 2)

        @pl.when(forward_now)
        def _():
            forward(k)

        @pl.when(jnp.logical_not(forward_now))
        def _():
            backward(k)

    def put_ein(base, value):
        for q in range(8):
            r = base + q * 16
            row = (r // 192) * ROWS_A + r % ROWS_A
            ga[(r % 192) // ROWS_A, row : row + 16, :] = value[q * 16 : q * 16 + 16].astype(BF)

    def put_b(base, width, offset, value):
        for q in range(128 // width):
            zy = base // width + q
            piece = value[q * width : (q + 1) * width].astype(BF)
            for b in range(4):
                gb[b, zy, offset : offset + width, :] = piece[:, b * 128 : (b + 1) * 128]

    def both(ref):
        return ref[...].reshape(ref.shape[0] * ref.shape[1], ref.shape[2])

    def cols(ref, m):
        return jnp.concatenate([ref[0, :, m * 128 : (m + 1) * 128], ref[1, :, m * 128 : (m + 1) * 128]], axis=0)

    def own_cols(m):
        at = slice(m * 128, (m + 1) * 128)
        return jnp.concatenate([tab[0, 0:NODES_DEV, at], tab[1, 0:NODES_DEV, at]], axis=0)

    def copy(n, src, dst, device):
        return remote(src, dst, send_sem.at[n], recv_sem.at[n], device)

    class Ring:
        def __init__(self, base, src, t, u, v, me, at, cut):
            right, left, across = (me + 1) % 4, (me + 3) % 4, (me + 2) % 4
            lo, hi = slice(0, cut), slice(cut, t.shape[0])
            self.out = [
                copy(base, src.at[across, lo], t.at[lo], at(right)),
                copy(base + 1, src.at[across, hi], t.at[hi], at(left)),
                copy(base + 2, src.at[right, hi], u.at[hi], at(right)),
                copy(base + 3, src.at[left, lo], v.at[lo], at(left)),
                copy(base + 4, t.at[lo], u.at[lo], at(right)),
                copy(base + 5, t.at[hi], v.at[hi], at(left)),
            ]
            self.src, self.t, self.u, self.v = src, t, u, v
            self.me, self.right, self.left, self.cut = me, right, left, cut

        def start(self):
            for c in self.out[:4]:
                c.start()

        def middle(self, block):
            src, t, n, cut = self.src, self.t, self.t.shape[0], self.cut
            for c, q, lo, hi in ((0, self.right, 0, cut), (1, self.left, cut, n)):
                self.out[c].wait_recv()

                @pl.loop(lo // block, hi // block)
                def _(i):
                    at = pl.ds(pl.multiple_of(i * block, block), block)
                    t[at] = (t[at].astype(F4) + src[q, at].astype(F4)).astype(BF)

                self.out[4 + c].start()

        def total(self, at):
            own = self.src[self.me, at].astype(F4)
            return own + self.u[at].astype(F4) + self.v[at].astype(F4)

        def arrive(self):
            for c in self.out[2:]:
                c.wait_recv()

    ring_a = Ring(0, ga, ta, ua, va, y, at_y, 208)
    ring_b = Ring(6, gb, tb, ub, vb, px, at_x, 2 * nz)
    ring_a2 = Ring(12, a2, ta2, ua2, va2, px, at_x, 208)
    ring_b2 = Ring(18, b2, tb2, ub2, vb2, y, at_y, nz // 2)

    for m in range(4):
        base = m * 128
        put_b(base, 16, 48, mm_tn(cols(midn, m), both(doutn)))
        put_b(base, 32, 0, mm_tn(own_cols(m), both(dpren)))
        put_b(512 + base, 32, 0, mm_tn(cols(agg, m), both(dpren)))
        put_b(base, 16, 32, mm_tn(cols(mid, m), both(doute)))
    ring_b.start()
    for m in range(4):
        base = m * 128
        put_ein(base, mm_tn(cols(ein, m), both(dpre)))
        put_ein(512 + base, mm_tn(cols(tab, m), both(gs)))
        put_ein(1024 + base, mm_tn(own_cols(m), both(gr)))
    row = lax.broadcasted_iota(jnp.int32, (GAIN, 512), 0)
    sum_e = jnp.sum(dge[...], axis=0, keepdims=True)
    sum_n = jnp.sum(dgn[...], axis=0, keepdims=True)
    gains = jnp.where(row == 0, sum_e, jnp.where(row == 1, sum_n, 0.0)).astype(BF)
    for q in range(4):
        ga[q, EDGES_DEV:, :] = gains
    ring_a.start()

    @pl.when(first)
    def _():
        for k in range(2):
            for j in range(4):
                back_copy(halo2, k, j, r_bh2).wait_recv()
            dh[k] = (down[k] + mm(sendt[:, 0:HALOS], halo2[k])).astype(BF)
            store_node(dh, k).start()

    ring_a.middle(16)
    ring_b.middle(1)
    ring_a.arrive()

    @pl.loop(0, ga.shape[1] // 16)
    def _(i):
        at = pl.ds(pl.multiple_of(i * 16, 16), 16)
        total = ring_a.total(at).astype(BF)
        for b in range(4):
            a2[b, at, :] = total[:, b * 128 : (b + 1) * 128]

    ring_a2.start()
    ring_b.arrive()

    @pl.loop(0, nz)
    def _(i):
        for q in range(4):
            b2[q, i] = ring_b.total(i * 4 + q).astype(BF)

    ring_b2.start()
    ring_a2.middle(16)
    ring_b2.middle(1)
    ring_a2.arrive()
    gains = ring_a2.total(slice(nz * ROWS_A, nz * ROWS_A + GAIN)).astype(BF)

    @pl.loop(0, nz)
    def _(i):
        at = pl.ds(pl.multiple_of(i * ROWS_A, 16), ROWS_A)
        c3[i, 0:ROWS_A, :] = ring_a2.total(at).astype(BF)
        c3[i, ROWS_A : ROWS_A + GAIN, :] = gains

    ring_b2.arrive()

    @pl.loop(0, nz)
    def _(i):
        c3[i, ROWS_A + GAIN :, :] = ring_b2.total(i).astype(BF)

    third = [copy(24 + j, c3.at[p], rc3.at[j], at_z(p)) for j, p in enumerate(z_peers)]
    for c in third:
        c.start()
    total = c3[z].astype(F4)
    for j, c in enumerate(third):
        c.wait_recv()
        total = total + rc3[j].astype(F4)
    total = total * factor

    n0 = ROWS_A + GAIN
    for p in range(4):
        b = (p % 2) * 2 + p // 2
        fin[p, 0:12, :] = total[12 * b : 12 * b + 12]
        fin[p, 12:16, :] = total[n0 + 32 + 4 * b : n0 + 32 + 4 * b + 4]
        fin[p, 16:24, :] = total[n0 + 8 * b : n0 + 8 * b + 8]
        fin[p, 24:28, :] = total[n0 + 48 + 4 * b : n0 + 48 + 4 * b + 4]
        fin[p, 28:32, :] = total[ROWS_A : ROWS_A + 4]
    base = 24 + nz - 1
    last = [copy(base + j, fin.at[p], rfin.at[px], at_x(p)) for j, p in enumerate(x_peers)]
    for c in last:
        c.start()
    rfin[px] = fin[px]
    for c in last:
        c.wait_recv()
    result = pltpu.make_async_copy(rfin, fin_out, l_fin.at[0])
    result.start()
    result.wait()
    for c in ring_a.out + ring_b.out + ring_a2.out + ring_b2.out + third + last:
        c.wait_send()

    @pl.when(first)
    def _():
        for k in range(2):
            sib_e(k).wait_send()
            sib_h(k).wait_send()
            for j in range(4):
                halo_copy(hs1, k, j, s_halo1, 0).wait_send()
                halo_copy(hs2, k, j, s_halo2, 1).wait_send()
                back_copy(halo2, k, j, r_bh2).wait_send()
            store_edge(de, k).wait()
            store_node(dh, k).wait()

    @pl.when(second)
    def _():
        for k in range(2):
            sib_do(k).wait_send()
            sib_de(k).wait_send()
            for j in range(4):
                back_copy(halo1, k, j, r_bh1).wait_send()
            store_edge(enew, k).wait()
            store_node(hnew, k).wait()


def layer_call(operands, factor):
    hbm = pl.BlockSpec(memory_space=pl.ANY)
    nz = 8
    i32 = jnp.int32

    def bf(*shape):
        return pltpu.VMEM(shape, BF)

    def fl(*shape):
        return pltpu.VMEM(shape, F4)

    dma = pltpu.SemaphoreType.DMA
    n, e = NODES_DEV, EDGES_DEV
    rows = nz * ROWS_A + GAIN
    copies = 24 + nz - 1 + 3
    return pl.pallas_call(
        functools.partial(layer_kernel, nz=nz, factor=factor),
        out_shape=[
            jax.ShapeDtypeStruct((2, n, 512), BF),
            jax.ShapeDtypeStruct((2, e, 512), BF),
            jax.ShapeDtypeStruct((4, 32, 128), F4),
        ],
        in_specs=[hbm] * 13,
        out_specs=[hbm] * 3,
        scratch_shapes=[
            pltpu.VMEM((e,), i32), pltpu.VMEM((e,), i32), pltpu.VMEM((1, 4, HALO), i32), pltpu.SMEM((1,), i32),
            bf(1536, 512), bf(512, 512), bf(1024, 512), bf(512, 512), fl(1, 512), fl(1, 512), dma((10,)),
            bf(320, e), bf(e, 320), bf(n, e), bf(e, n), bf(n, n), bf(n, n),
            bf(2, TABLE, 512), bf(2, e, 512), bf(2, n, 512), bf(2, e, 512), fl(2, n, 512),
            bf(2, HALOS, 512), bf(2, HALOS, 512), bf(2, HALOS, 512), bf(2, HALOS, 512), bf(2, HALOS, 512),
            bf(320, 512), fl(2, e, 512), bf(2, e, 512), fl(e, 512), fl(2, e, 512), fl(2, e, 128),
            bf(2, e, 512), bf(2, n, 512), fl(2, n, 512), bf(2, n, 512), fl(n, 512), fl(2, n, 512),
            fl(2, n, 128), bf(2, n, 512),
            bf(2, n, 512), bf(2, n, 512), fl(2, n, 512), bf(n, 512), bf(2, e, 512), bf(2, e, 512),
            bf(2, TABLE, 512), bf(2, n, 512), bf(2, e, 512), bf(2, n, 512), fl(8, 512), fl(8, 512),
            dma((2, 4)), dma((2, 4)), dma((2, 4)), dma((2,)), dma((2,)), dma((2,)), dma((2,)),
            dma((2, 4)), dma((2, 4)), dma((2, 4)), dma((2,)), dma((2,)), dma((2,)), dma((2,)),
            dma((2,)), dma((2,)), dma((2,)), dma((2,)), dma((2,)),
            bf(4, rows, 512), bf(4, 4 * nz, ROWS_B, 128),
            bf(rows, 512), bf(rows, 512), bf(rows, 512),
            bf(4 * nz, ROWS_B, 128), bf(4 * nz, ROWS_B, 128), bf(4 * nz, ROWS_B, 128),
            bf(4, rows, 128), bf(rows, 128), bf(rows, 128), bf(rows, 128),
            bf(4, nz, ROWS_B, 128), bf(nz, ROWS_B, 128), bf(nz, ROWS_B, 128), bf(nz, ROWS_B, 128),
            bf(nz, 128, 128), bf(nz - 1, 128, 128), fl(4, 32, 128), fl(4, 32, 128),
            dma((copies,)), dma((copies,)), dma((1,)),
        ],
        compiler_params=pltpu.CompilerParams(
            collective_id=0, has_side_effects=True, vmem_limit_bytes=56 << 20
        ),
        name="layers",
    )(*operands)


def finish_kernel(
    node_in, edge_in, fin_in, node_o, edge_o, ein_o, eout_o, nin_o, nout_o, ge_o, gn_o, rfin, sems
):
    first = pltpu.make_async_copy(fin_in, rfin, sems.at[0])
    first.start()
    moves = [pltpu.make_async_copy(node_in, node_o.at[0], sems.at[1])]
    moves += [
        pltpu.make_async_copy(edge_in.at[k], edge_o.at[0, k], sems.at[2 + k]) for k in range(2)
    ]
    for c in moves:
        c.start()
    first.wait()
    t = lax.axis_index("dom") * 2 + lax.axis_index("rep")
    lane = lax.broadcasted_iota(jnp.int32, (2, 128), 1)
    picked = jnp.zeros((2, 128), F4)
    for b in range(4):
        at = slice(b * 128, (b + 1) * 128)
        ein_o[0, :, at] = rfin[b, 0:12, :]
        eout_o[0, :, at] = rfin[b, 12:16, :]
        nin_o[0, :, at] = rfin[b, 16:24, :]
        nout_o[0, :, at] = rfin[b, 24:28, :]
        pair = rfin[b, 28:30, :]
        for i in range(4):
            hit = jnp.where(lane + b * 128 == t * 4 + i, pair, 0.0)
            value = jnp.sum(hit, axis=1, keepdims=True)
            picked = picked + jnp.where(lane == i, value, 0.0)
    ge_o[...] = picked[0:1, 0:4]
    gn_o[...] = picked[1:2, 0:4]
    for c in moves:
        c.wait()


def finish_call(node, edge, fin):
    hbm = pl.BlockSpec(memory_space=pl.ANY)
    vm = pl.BlockSpec(memory_space=pltpu.VMEM)
    return pl.pallas_call(
        finish_kernel,
        out_shape=[
            jax.ShapeDtypeStruct((1, *node.shape), BF),
            jax.ShapeDtypeStruct((1, *edge.shape), BF),
            jax.ShapeDtypeStruct((1, 12, 512), F4),
            jax.ShapeDtypeStruct((1, 4, 512), F4),
            jax.ShapeDtypeStruct((1, 8, 512), F4),
            jax.ShapeDtypeStruct((1, 4, 512), F4),
            jax.ShapeDtypeStruct((1, 4), F4),
            jax.ShapeDtypeStruct((1, 4), F4),
        ],
        in_specs=[hbm] * 3,
        out_specs=[hbm] * 2 + [vm] * 6,
        scratch_shapes=[pltpu.VMEM((4, 32, 128), F4), pltpu.SemaphoreType.DMA((4,))],
        compiler_params=pltpu.CompilerParams(vmem_limit_bytes=56 << 20),
        name="finish",
    )(node, edge, fin)


def body(
    node_latent, edge_latent, node_cot, edge_src, edge_dst, edge_count, send_index,
    w_edge_in, w_edge_out, w_node_in, w_node_out, gain_edge, gain_node,
):
    micro = node_latent.shape[0]
    factor = float(micro * lax.axis_size("rep") * NODES_DEV * lax.axis_size("dom")) ** (-0.5)
    node, edge, fin = layer_call(
        (
            edge_src, edge_dst, send_index, edge_count, node_latent, edge_latent, node_cot,
            w_edge_in, w_edge_out, w_node_in, w_node_out, gain_edge, gain_node,
        ),
        factor,
    )
    return tuple(finish_call(node, edge, fin))


def solution(mesh):
    placed = (
        P("rep", "dom", None),
        P("rep", "dom", None),
        P("rep", "dom", None),
        P("dom"),
        P("dom"),
        P("dom"),
        P("dom", None, None),
        P("segment", None, None),
        P("segment", None, None),
        P("segment", None, None),
        P("segment", None, None),
        P("segment", None),
        P("segment", None),
    )
    return jax.shard_map(
        body,
        mesh=mesh,
        in_specs=placed,
        out_specs=(
            P("segment", "rep", "dom", None),
            P("segment", "rep", "dom", None),
            P("segment", ("dom", "rep"), None),
            P("segment", ("dom", "rep"), None),
            P("segment", ("dom", "rep"), None),
            P("segment", ("dom", "rep"), None),
            P("segment", ("dom", "rep")),
            P("segment", ("dom", "rep")),
        ),
        check_vma=False,
    )
```

```python
import functools

import jax
import jax.numpy as jnp
from jax import lax
from jax.experimental import pallas as pl
from jax.experimental.pallas import tpu as pltpu
from jax.sharding import PartitionSpec as P

OFFSETS = (1, -1, 2, -2)
HALO = 16
EPS = 1e-05
MESH = pl.DeviceIdType.MESH
ROWS_A = 48
ROWS_B = 64
GAIN = 16
NODES_DEV = 128
EDGES_DEV = 384
HALOS = 64
TABLE = 192
BLOCK = 32
BF = jnp.bfloat16
F4 = jnp.float32


def mm(a, b):
    return jnp.dot(a, b, preferred_element_type=F4)


def mm_nt(a, b):
    return lax.dot_general(a, b, (((1,), (1,)), ((), ())), preferred_element_type=F4)


def mm_tn(a, b):
    return lax.dot_general(a, b, (((0,), (0,)), ((), ())), preferred_element_type=F4)


def silu_grad(pre):
    sig = jax.nn.sigmoid(pre)
    return sig * (1.0 + pre * (1.0 - sig))


def layer_kernel(
    src_in, dst_in, send_in, count_in, node_in, edge_in, cot_in,
    w_ein_in, w_eout_in, w_nin_in, w_nout_in, gain_e_in, gain_n_in,
    node_out, edge_out, fin_out,
    src_row, dst_row, send_row, count, w_ein, w_eout, w_nin, w_nout, gain_e, gain_n, l_first,
    oht, oh, inc, inct, sendt, sendm,
    tab, ein, cn, ce, cn32, halo1, halo2, hs1, hs2, bh,
    sr, pre, mid, tmp, xhat, rstd, enew, agg, pren, midn, tmpn, xhatn, rstdn, hnew,
    doutn, dpren, down, dagg, doute, dpre, gs, gr, de, dh, dge, dgn,
    s_halo1, s_halo2, r_halo, s_fe, r_fe, s_fh, r_fh,
    s_bh, r_bh1, r_bh2, s_be, r_be, s_bo, r_bo,
    l_node, l_edge, l_cot, l_nout, l_eout,
    ga, gb, ta, ua, va, tb, ub, vb, a2, ta2, ua2, va2, b2, tb2, ub2, vb2, c3, rc3, fin, rfin,
    send_sem, recv_sem, l_fin,
    *, nz, factor,
):
    seg = lax.axis_index("segment")
    dom = lax.axis_index("dom")
    n_dom = lax.axis_size("dom")
    first = seg == 0
    second = seg == 1

    def near(step, segment):
        return {"dom": (dom + step + n_dom) % n_dom, "segment": segment}

    rep = lax.axis_index("rep")
    z = dom // 8
    y = (dom // 2) % 4
    px = rep * 2 + dom % 2

    def at_y(p):
        return {"dom": z * 8 + p * 2 + dom % 2}

    def at_z(p):
        return {"dom": p * 8 + dom % 8}

    def at_x(p):
        return {"dom": (dom // 2) * 2 + p % 2, "rep": p // 2}

    z_peers = [(z + j) % nz for j in range(1, nz)]
    x_peers = [(px + j) % 4 for j in range(1, 4)]
    greet = [near(step, s) for step in OFFSETS for s in range(2)]
    greet += [at_y((y + 1) % 4), at_y((y + 3) % 4)]
    greet += [at_x(p) for p in x_peers] + [at_z(p) for p in z_peers]
    greet += [{"segment": 1 - seg}]
    barrier = pltpu.get_barrier_semaphore()
    for device in greet:
        pl.semaphore_signal(barrier, inc=1, device_id=device, device_id_type=MESH)

    def remote(src, dst, send, recv, device):
        return pltpu.make_async_remote_copy(
            src_ref=src, dst_ref=dst, send_sem=send, recv_sem=recv,
            device_id=device, device_id_type=MESH,
        )

    def load_node(k):
        return pltpu.make_async_copy(node_in.at[k], tab.at[k, 0:NODES_DEV], l_node.at[k])

    def load_edge(k):
        return pltpu.make_async_copy(edge_in.at[k], ein.at[k], l_edge.at[k])

    def load_cot(k):
        return pltpu.make_async_copy(cot_in.at[k], cn.at[k], l_cot.at[k])

    def store_node(src, k):
        return pltpu.make_async_copy(src.at[k], node_out.at[k], l_nout.at[k])

    def store_edge(src, k):
        return pltpu.make_async_copy(src.at[k], edge_out.at[k], l_eout.at[k])

    def halo_copy(src, k, j, sems, segment):
        rows = slice(j * HALO, (j + 1) * HALO)
        into = slice(NODES_DEV + j * HALO, NODES_DEV + (j + 1) * HALO)
        return remote(
            src.at[k, rows], tab.at[k, into], sems.at[k, j], r_halo.at[k, j],
            near(OFFSETS[j], segment),
        )

    def back_copy(dst, k, j, recv):
        rows = slice(j * HALO, (j + 1) * HALO)
        return remote(
            bh.at[k, rows], dst.at[k, rows], s_bh.at[k, j], recv.at[k, j],
            near(-OFFSETS[j], 0),
        )

    def sib_e(k):
        return remote(enew.at[k], ein.at[k], s_fe.at[k], r_fe.at[k], {"segment": 1 - seg})

    def sib_h(k):
        return remote(
            hnew.at[k], tab.at[k, 0:NODES_DEV], s_fh.at[k], r_fh.at[k], {"segment": 1 - seg}
        )

    def sib_de(k):
        return remote(de.at[k], ce.at[k], s_be.at[k], r_be.at[k], {"segment": 1 - seg})

    def sib_do(k):
        return remote(down.at[k], cn32.at[k], s_bo.at[k], r_bo.at[k], {"segment": 1 - seg})

    small = [
        pltpu.make_async_copy(u, v, l_first.at[i])
        for i, (u, v) in enumerate(
            [
                (src_in, src_row), (dst_in, dst_row), (send_in, send_row), (count_in, count),
                (gain_e_in, gain_e), (gain_n_in, gain_n),
            ]
        )
    ]
    large = [
        pltpu.make_async_copy(u.at[0], v, l_first.at[6 + i])
        for i, (u, v) in enumerate(
            [(w_ein_in, w_ein), (w_eout_in, w_eout), (w_nin_in, w_nin), (w_nout_in, w_nout)]
        )
    ]
    for c in small:
        c.start()

    @pl.when(first)
    def _():
        for k in range(2):
            load_node(k).start()
            load_edge(k).start()

    @pl.when(second)
    def _():
        for k in range(2):
            load_cot(k).start()

    for c in large:
        c.start()
    for c in small:
        c.wait()
    live_count = count[0]
    hot_src = lax.broadcasted_iota(jnp.int32, (TABLE, EDGES_DEV), 0) == src_row[...].reshape(1, EDGES_DEV)
    owner = lax.broadcasted_iota(jnp.int32, (NODES_DEV, EDGES_DEV), 0)
    slot = lax.broadcasted_iota(jnp.int32, (NODES_DEV, EDGES_DEV), 1)
    hot_dst = owner == dst_row[...].reshape(1, EDGES_DEV)
    hot_inc = hot_dst & (slot < live_count)
    f_src = jnp.where(hot_src, 1.0, 0.0)
    f_dst = jnp.where(hot_dst, 1.0, 0.0)
    f_inc = jnp.where(hot_inc, 1.0, 0.0)
    oht[0:TABLE] = f_src.astype(BF)
    oht[TABLE:] = f_dst.astype(BF)
    inc[...] = f_inc.astype(BF)
    oh[:, 0:TABLE] = f_src.T.astype(BF)
    oh[:, TABLE:] = f_dst.T.astype(BF)
    inct[...] = f_inc.T.astype(BF)
    node = lax.broadcasted_iota(jnp.int32, (NODES_DEV, HALO), 0)
    hots = [jnp.where(node == send_row[0, j : j + 1, :], 1.0, 0.0) for j in range(4)]
    f_send = jnp.concatenate(hots + [jnp.zeros((NODES_DEV, NODES_DEV - HALOS), F4)], axis=1)
    sendt[...] = f_send.astype(BF)
    sendm[...] = f_send.T.astype(BF)
    dge[...] = jnp.zeros_like(dge)
    dgn[...] = jnp.zeros_like(dgn)

    @pl.when(second)
    def _():
        ce[...] = jnp.zeros_like(ce)

    pl.semaphore_wait(barrier, len(greet))

    for c in large:
        c.wait()

    @pl.when(first)
    def _():
        for k in range(2):
            load_node(k).wait()
            hs1[k] = mm(sendm[0:HALOS], tab[k, 0:NODES_DEV]).astype(BF)
            for j in range(4):
                halo_copy(hs1, k, j, s_halo1, 0).start()

    def mean(v):
        return jnp.sum(v, axis=-1, keepdims=True) * (1.0 / 512.0)

    def norm_block(outer, at, k, x_ref, r_ref):
        center = outer - mean(outer)
        inv = lax.rsqrt(mean(center * center) + EPS)
        hat = center * inv
        x_ref[k, at, :] = hat
        r_ref[k, at, :] = jnp.broadcast_to(inv, (BLOCK, 128))
        return hat

    def norm_back(cot, gain, hat, inv):
        dy = cot * gain
        return inv * (dy - mean(dy) - hat * mean(dy * hat))

    def forward(k):
        @pl.when(first)
        def _():
            load_edge(k).wait()

        @pl.when(second)
        def _():
            sib_e(k).wait_recv()

        pre[k] = mm(ein[k], w_ein[0:512])

        @pl.when(second)
        def _():
            sib_h(k).wait_recv()

        own = tab[k, 0:NODES_DEV]
        sr[TABLE:] = mm(own, w_ein[1024:1536]).astype(BF)
        for j in range(4):
            halo_copy(hs1, k, j, s_halo1, 0).wait_recv()
        sr[0:TABLE] = mm(tab[k], w_ein[512:1024]).astype(BF)
        tmp[...] = mm(oh[...], sr[...])

        @pl.loop(0, EDGES_DEV // BLOCK)
        def _(i):
            at = pl.ds(pl.multiple_of(i * BLOCK, BLOCK), BLOCK)
            v = pre[k, at, :] + tmp[at, :]
            pre[k, at, :] = v
            mid[k, at, :] = (v * jax.nn.sigmoid(v)).astype(BF)

        tmp[...] = mm(mid[k], w_eout[...])

        @pl.loop(0, EDGES_DEV // BLOCK)
        def _(i):
            at = pl.ds(pl.multiple_of(i * BLOCK, BLOCK), BLOCK)
            hat = norm_block(tmp[at, :], at, k, xhat, rstd)
            rows = lax.broadcasted_iota(jnp.int32, (BLOCK, 512), 0) + i * BLOCK
            old = ein[k, at, :].astype(F4)
            enew[k, at, :] = jnp.where(rows < live_count, old + hat * gain_e[...], old).astype(BF)

        @pl.when(first)
        def _():
            sib_e(k).start()

        @pl.when(second)
        def _():
            store_edge(enew, k).start()

        agg[k] = mm(inc[...], enew[k]).astype(BF)
        pren[k] = mm(own, w_nin[0:512]) + mm(agg[k], w_nin[512:1024])

        @pl.loop(0, NODES_DEV // BLOCK)
        def _(i):
            at = pl.ds(pl.multiple_of(i * BLOCK, BLOCK), BLOCK)
            v = pren[k, at, :]
            midn[k, at, :] = (v * jax.nn.sigmoid(v)).astype(BF)

        tmpn[...] = mm(midn[k], w_nout[...])

        @pl.loop(0, NODES_DEV // BLOCK)
        def _(i):
            at = pl.ds(pl.multiple_of(i * BLOCK, BLOCK), BLOCK)
            hat = norm_block(tmpn[at, :], at, k, xhatn, rstdn)
            hnew[k, at, :] = (tab[k, at, :].astype(F4) + hat * gain_n[...]).astype(BF)

        @pl.when(first)
        def _():
            sib_h(k).start()
            hs2[k] = mm(sendm[0:HALOS], hnew[k]).astype(BF)
            for j in range(4):
                halo_copy(hs2, k, j, s_halo2, 1).start()

        @pl.when(second)
        def _():
            store_node(hnew, k).start()

    def backward(k):
        @pl.when(first)
        def _():
            sib_do(k).wait_recv()
            for j in range(4):
                back_copy(halo1, k, j, r_bh1).wait_recv()
            cn[k] = (cn32[k] + mm(sendt[:, 0:HALOS], halo1[k])).astype(BF)

        @pl.when(second)
        def _():
            load_cot(k).wait()

        @pl.loop(0, NODES_DEV // BLOCK)
        def _(i):
            at = pl.ds(pl.multiple_of(i * BLOCK, BLOCK), BLOCK)
            cot = cn[k, at, :].astype(F4)
            hat = xhatn[k, at, :]
            dgn[...] += jnp.sum((cot * hat).reshape(BLOCK // 8, 8, 512), axis=0)
            inv = rstdn[k, at, 0:1]
            doutn[k, at, :] = norm_back(cot, gain_n[...], hat, inv).astype(BF)

        tmpn[...] = mm_nt(doutn[k], w_nout[...])

        @pl.loop(0, NODES_DEV // BLOCK)
        def _(i):
            at = pl.ds(pl.multiple_of(i * BLOCK, BLOCK), BLOCK)
            dpren[k, at, :] = (tmpn[at, :] * silu_grad(pren[k, at, :])).astype(BF)

        dagg[...] = mm_nt(dpren[k], w_nin[512:1024]).astype(BF)

        @pl.when(first)
        def _():
            sib_de(k).wait_recv()

        tmp[...] = mm(inct[...], dagg[...])
        down[k] = cn[k].astype(F4) + mm_nt(dpren[k], w_nin[0:512])

        @pl.loop(0, EDGES_DEV // BLOCK)
        def _(i):
            at = pl.ds(pl.multiple_of(i * BLOCK, BLOCK), BLOCK)
            cot = tmp[at, :] + ce[k, at, :].astype(F4)
            tmp[at, :] = cot
            rows = lax.broadcasted_iota(jnp.int32, (BLOCK, 512), 0) + i * BLOCK
            cot = jnp.where(rows < live_count, cot, 0.0)
            hat = xhat[k, at, :]
            dge[...] += jnp.sum((cot * hat).reshape(BLOCK // 8, 8, 512), axis=0)
            inv = rstd[k, at, 0:1]
            doute[k, at, :] = norm_back(cot, gain_e[...], hat, inv).astype(BF)

        grad = mm_nt(doute[k], w_eout[...])
        pre[k] = grad * silu_grad(pre[k])
        dpre[k] = pre[k].astype(BF)
        gs[k] = mm(oht[0:TABLE], dpre[k]).astype(BF)
        gr[k] = mm(oht[TABLE:], dpre[k]).astype(BF)
        bh[k] = mm_nt(gs[k, NODES_DEV:], w_ein[512:1024]).astype(BF)

        @pl.when(first)
        def _():
            for j in range(4):
                back_copy(halo2, k, j, r_bh2).start()

        @pl.when(second)
        def _():
            for j in range(4):
                back_copy(halo1, k, j, r_bh1).start()

        down[k] += mm_nt(gs[k, 0:NODES_DEV], w_ein[512:1024]) + mm_nt(gr[k], w_ein[1024:1536])

        @pl.when(second)
        def _():
            sib_do(k).start()

        de[k] = (tmp[...] + mm_nt(dpre[k], w_ein[0:512])).astype(BF)

        @pl.when(second)
        def _():
            sib_de(k).start()

        @pl.when(first)
        def _():
            store_edge(de, k).start()

    @pl.loop(0, 4)
    def _(step):
        forward_now = (step == 0) | (step == 1 + seg)
        k = jnp.where(first, step % 2, step // 2)

        @pl.when(forward_now)
        def _():
            forward(k)

        @pl.when(jnp.logical_not(forward_now))
        def _():
            backward(k)

    def put_ein(base, value):
        for q in range(8):
            r = base + q * 16
            row = (r // 192) * ROWS_A + r % ROWS_A
            ga[(r % 192) // ROWS_A, row : row + 16, :] = value[q * 16 : q * 16 + 16].astype(BF)

    def put_b(base, width, offset, value):
        for q in range(128 // width):
            zy = base // width + q
            piece = value[q * width : (q + 1) * width].astype(BF)
            for b in range(4):
                gb[b, zy, offset : offset + width, :] = piece[:, b * 128 : (b + 1) * 128]

    def both(ref):
        return ref[...].reshape(ref.shape[0] * ref.shape[1], ref.shape[2])

    def cols(ref, m):
        return jnp.concatenate([ref[0, :, m * 128 : (m + 1) * 128], ref[1, :, m * 128 : (m + 1) * 128]], axis=0)

    def own_cols(m):
        at = slice(m * 128, (m + 1) * 128)
        return jnp.concatenate([tab[0, 0:NODES_DEV, at], tab[1, 0:NODES_DEV, at]], axis=0)

    def copy(n, src, dst, device):
        return remote(src, dst, send_sem.at[n], recv_sem.at[n], device)

    class Ring:
        def __init__(self, base, src, t, u, v, me, at, cut):
            right, left, across = (me + 1) % 4, (me + 3) % 4, (me + 2) % 4
            lo, hi = slice(0, cut), slice(cut, t.shape[0])
            self.out = [
                copy(base, src.at[across, lo], t.at[lo], at(right)),
                copy(base + 1, src.at[across, hi], t.at[hi], at(left)),
                copy(base + 2, src.at[right, hi], u.at[hi], at(right)),
                copy(base + 3, src.at[left, lo], v.at[lo], at(left)),
                copy(base + 4, t.at[lo], u.at[lo], at(right)),
                copy(base + 5, t.at[hi], v.at[hi], at(left)),
            ]
            self.src, self.t, self.u, self.v = src, t, u, v
            self.me, self.right, self.left, self.cut = me, right, left, cut

        def start(self):
            for c in self.out[:4]:
                c.start()

        def middle(self, block):
            src, t, n, cut = self.src, self.t, self.t.shape[0], self.cut
            for c, q, lo, hi in ((0, self.right, 0, cut), (1, self.left, cut, n)):
                self.out[c].wait_recv()

                @pl.loop(lo // block, hi // block)
                def _(i):
                    at = pl.ds(pl.multiple_of(i * block, block), block)
                    t[at] = (t[at].astype(F4) + src[q, at].astype(F4)).astype(BF)

                self.out[4 + c].start()

        def total(self, at):
            own = self.src[self.me, at].astype(F4)
            return own + self.u[at].astype(F4) + self.v[at].astype(F4)

        def arrive(self):
            for c in self.out[2:]:
                c.wait_recv()

    ring_a = Ring(0, ga, ta, ua, va, y, at_y, 208)
    ring_b = Ring(6, gb, tb, ub, vb, px, at_x, 2 * nz)
    ring_a2 = Ring(12, a2, ta2, ua2, va2, px, at_x, 208)
    ring_b2 = Ring(18, b2, tb2, ub2, vb2, y, at_y, nz // 2)

    for m in range(4):
        base = m * 128
        put_b(base, 16, 48, mm_tn(cols(midn, m), both(doutn)))
        put_b(base, 32, 0, mm_tn(own_cols(m), both(dpren)))
        put_b(512 + base, 32, 0, mm_tn(cols(agg, m), both(dpren)))
        put_b(base, 16, 32, mm_tn(cols(mid, m), both(doute)))
    ring_b.start()
    for m in range(4):
        base = m * 128
        put_ein(base, mm_tn(cols(ein, m), both(dpre)))
        put_ein(512 + base, mm_tn(cols(tab, m), both(gs)))
        put_ein(1024 + base, mm_tn(own_cols(m), both(gr)))
    row = lax.broadcasted_iota(jnp.int32, (GAIN, 512), 0)
    sum_e = jnp.sum(dge[...], axis=0, keepdims=True)
    sum_n = jnp.sum(dgn[...], axis=0, keepdims=True)
    gains = jnp.where(row == 0, sum_e, jnp.where(row == 1, sum_n, 0.0)).astype(BF)
    for q in range(4):
        ga[q, EDGES_DEV:, :] = gains
    ring_a.start()

    @pl.when(first)
    def _():
        for k in range(2):
            for j in range(4):
                back_copy(halo2, k, j, r_bh2).wait_recv()
            dh[k] = (down[k] + mm(sendt[:, 0:HALOS], halo2[k])).astype(BF)
            store_node(dh, k).start()

    ring_a.middle(16)
    ring_b.middle(1)
    ring_a.arrive()

    @pl.loop(0, ga.shape[1] // 16)
    def _(i):
        at = pl.ds(pl.multiple_of(i * 16, 16), 16)
        total = ring_a.total(at).astype(BF)
        for b in range(4):
            a2[b, at, :] = total[:, b * 128 : (b + 1) * 128]

    ring_a2.start()
    ring_b.arrive()

    @pl.loop(0, nz)
    def _(i):
        for q in range(4):
            b2[q, i] = ring_b.total(i * 4 + q).astype(BF)

    ring_b2.start()
    ring_a2.middle(16)
    ring_b2.middle(1)
    ring_a2.arrive()
    gains = ring_a2.total(slice(nz * ROWS_A, nz * ROWS_A + GAIN)).astype(BF)

    @pl.loop(0, nz)
    def _(i):
        at = pl.ds(pl.multiple_of(i * ROWS_A, 16), ROWS_A)
        c3[i, 0:ROWS_A, :] = ring_a2.total(at).astype(BF)
        c3[i, ROWS_A : ROWS_A + GAIN, :] = gains

    ring_b2.arrive()

    @pl.loop(0, nz)
    def _(i):
        c3[i, ROWS_A + GAIN :, :] = ring_b2.total(i).astype(BF)

    third = [copy(24 + j, c3.at[p], rc3.at[j], at_z(p)) for j, p in enumerate(z_peers)]
    for c in third:
        c.start()
    total = c3[z].astype(F4)
    for j, c in enumerate(third):
        c.wait_recv()
        total = total + rc3[j].astype(F4)
    total = total * factor

    n0 = ROWS_A + GAIN
    for p in range(4):
        b = (p % 2) * 2 + p // 2
        fin[p, 0:12, :] = total[12 * b : 12 * b + 12]
        fin[p, 12:16, :] = total[n0 + 32 + 4 * b : n0 + 32 + 4 * b + 4]
        fin[p, 16:24, :] = total[n0 + 8 * b : n0 + 8 * b + 8]
        fin[p, 24:28, :] = total[n0 + 48 + 4 * b : n0 + 48 + 4 * b + 4]
        fin[p, 28:32, :] = total[ROWS_A : ROWS_A + 4]
    base = 24 + nz - 1
    last = [copy(base + j, fin.at[p], rfin.at[px], at_x(p)) for j, p in enumerate(x_peers)]
    for c in last:
        c.start()
    rfin[px] = fin[px]
    for c in last:
        c.wait_recv()
    result = pltpu.make_async_copy(rfin, fin_out, l_fin.at[0])
    result.start()
    result.wait()
    for c in ring_a.out + ring_b.out + ring_a2.out + ring_b2.out + third + last:
        c.wait_send()

    @pl.when(first)
    def _():
        for k in range(2):
            sib_e(k).wait_send()
            sib_h(k).wait_send()
            for j in range(4):
                halo_copy(hs1, k, j, s_halo1, 0).wait_send()
                halo_copy(hs2, k, j, s_halo2, 1).wait_send()
                back_copy(halo2, k, j, r_bh2).wait_send()
            store_edge(de, k).wait()
            store_node(dh, k).wait()

    @pl.when(second)
    def _():
        for k in range(2):
            sib_do(k).wait_send()
            sib_de(k).wait_send()
            for j in range(4):
                back_copy(halo1, k, j, r_bh1).wait_send()
            store_edge(enew, k).wait()
            store_node(hnew, k).wait()


def layer_call(operands, factor):
    hbm = pl.BlockSpec(memory_space=pl.ANY)
    nz = 8
    i32 = jnp.int32

    def bf(*shape):
        return pltpu.VMEM(shape, BF)

    def fl(*shape):
        return pltpu.VMEM(shape, F4)

    dma = pltpu.SemaphoreType.DMA
    n, e = NODES_DEV, EDGES_DEV
    rows = nz * ROWS_A + GAIN
    copies = 24 + nz - 1 + 3
    return pl.pallas_call(
        functools.partial(layer_kernel, nz=nz, factor=factor),
        out_shape=[
            jax.ShapeDtypeStruct((2, n, 512), BF),
            jax.ShapeDtypeStruct((2, e, 512), BF),
            jax.ShapeDtypeStruct((4, 32, 128), F4),
        ],
        in_specs=[hbm] * 13,
        out_specs=[hbm] * 3,
        scratch_shapes=[
            pltpu.VMEM((e,), i32), pltpu.VMEM((e,), i32), pltpu.VMEM((1, 4, HALO), i32), pltpu.SMEM((1,), i32),
            bf(1536, 512), bf(512, 512), bf(1024, 512), bf(512, 512), fl(1, 512), fl(1, 512), dma((10,)),
            bf(320, e), bf(e, 320), bf(n, e), bf(e, n), bf(n, n), bf(n, n),
            bf(2, TABLE, 512), bf(2, e, 512), bf(2, n, 512), bf(2, e, 512), fl(2, n, 512),
            bf(2, HALOS, 512), bf(2, HALOS, 512), bf(2, HALOS, 512), bf(2, HALOS, 512), bf(2, HALOS, 512),
            bf(320, 512), fl(2, e, 512), bf(2, e, 512), fl(e, 512), fl(2, e, 512), fl(2, e, 128),
            bf(2, e, 512), bf(2, n, 512), fl(2, n, 512), bf(2, n, 512), fl(n, 512), fl(2, n, 512),
            fl(2, n, 128), bf(2, n, 512),
            bf(2, n, 512), bf(2, n, 512), fl(2, n, 512), bf(n, 512), bf(2, e, 512), bf(2, e, 512),
            bf(2, TABLE, 512), bf(2, n, 512), bf(2, e, 512), bf(2, n, 512), fl(8, 512), fl(8, 512),
            dma((2, 4)), dma((2, 4)), dma((2, 4)), dma((2,)), dma((2,)), dma((2,)), dma((2,)),
            dma((2, 4)), dma((2, 4)), dma((2, 4)), dma((2,)), dma((2,)), dma((2,)), dma((2,)),
            dma((2,)), dma((2,)), dma((2,)), dma((2,)), dma((2,)),
            bf(4, rows, 512), bf(4, 4 * nz, ROWS_B, 128),
            bf(rows, 512), bf(rows, 512), bf(rows, 512),
            bf(4 * nz, ROWS_B, 128), bf(4 * nz, ROWS_B, 128), bf(4 * nz, ROWS_B, 128),
            bf(4, rows, 128), bf(rows, 128), bf(rows, 128), bf(rows, 128),
            bf(4, nz, ROWS_B, 128), bf(nz, ROWS_B, 128), bf(nz, ROWS_B, 128), bf(nz, ROWS_B, 128),
            bf(nz, 128, 128), bf(nz - 1, 128, 128), fl(4, 32, 128), fl(4, 32, 128),
            dma((copies,)), dma((copies,)), dma((1,)),
        ],
        compiler_params=pltpu.CompilerParams(
            collective_id=0, has_side_effects=True, vmem_limit_bytes=56 << 20
        ),
        name="layers",
    )(*operands)


def finish_kernel(
    node_in, edge_in, fin_in, node_o, edge_o, ein_o, eout_o, nin_o, nout_o, ge_o, gn_o,
    rfin, node_v, edge_v, sems, out_sems,
):
    first = pltpu.make_async_copy(fin_in, rfin, sems.at[0])
    first.start()
    parts = [(node_in.at[k], node_v.at[k], node_o.at[0, k]) for k in range(2)]
    for k in range(2):
        for q in range(2):
            at = slice(q * 192, q * 192 + 192)
            parts.append((edge_in.at[k, at], edge_v.at[k, at], edge_o.at[0, k, at]))
    moves = [pltpu.make_async_copy(u, v, sems.at[1 + i]) for i, (u, v, _) in enumerate(parts)]
    stores = [pltpu.make_async_copy(v, w, out_sems.at[i]) for i, (_, v, w) in enumerate(parts)]
    for c in moves:
        c.start()
    for c, w in zip(moves, stores):
        c.wait()
        w.start()
    first.wait()
    t = lax.axis_index("dom") * 2 + lax.axis_index("rep")
    lane = lax.broadcasted_iota(jnp.int32, (2, 128), 1)
    picked = jnp.zeros((2, 128), F4)
    for b in range(4):
        at = slice(b * 128, (b + 1) * 128)
        for r in range(12):
            ein_o[r, :, at] = rfin[b, r : r + 1, :]
        eout_o[0, :, at] = rfin[b, 12:16, :]
        nin_o[0, :, at] = rfin[b, 16:24, :]
        nout_o[0, :, at] = rfin[b, 24:28, :]
        pair = rfin[b, 28:30, :]
        for i in range(4):
            hit = jnp.where(lane + b * 128 == t * 4 + i, pair, 0.0)
            value = jnp.sum(hit, axis=1, keepdims=True)
            picked = picked + jnp.where(lane == i, value, 0.0)
    ge_o[...] = picked[0:1, 0:4]
    gn_o[...] = picked[1:2, 0:4]
    for c in stores:
        c.wait()


def finish_call(node, edge, fin):
    hbm = pl.BlockSpec(memory_space=pl.ANY)
    vm = pl.BlockSpec(memory_space=pltpu.VMEM)
    return pl.pallas_call(
        finish_kernel,
        out_shape=[
            jax.ShapeDtypeStruct((1, *node.shape), BF),
            jax.ShapeDtypeStruct((1, *edge.shape), BF),
            jax.ShapeDtypeStruct((12, 1, 512), F4),
            jax.ShapeDtypeStruct((1, 4, 512), F4),
            jax.ShapeDtypeStruct((1, 8, 512), F4),
            jax.ShapeDtypeStruct((1, 4, 512), F4),
            jax.ShapeDtypeStruct((1, 4), F4),
            jax.ShapeDtypeStruct((1, 4), F4),
        ],
        in_specs=[hbm] * 3,
        out_specs=[hbm] * 2 + [vm] * 6,
        scratch_shapes=[
            pltpu.VMEM((4, 32, 128), F4), pltpu.VMEM(node.shape, BF), pltpu.VMEM(edge.shape, BF),
            pltpu.SemaphoreType.DMA((7,)), pltpu.SemaphoreType.DMA((6,)),
        ],
        compiler_params=pltpu.CompilerParams(vmem_limit_bytes=56 << 20),
        name="finish",
    )(node, edge, fin)


def body(
    node_latent, edge_latent, node_cot, edge_src, edge_dst, edge_count, send_index,
    w_edge_in, w_edge_out, w_node_in, w_node_out, gain_edge, gain_node,
):
    micro = node_latent.shape[0]
    factor = float(micro * lax.axis_size("rep") * NODES_DEV * lax.axis_size("dom")) ** (-0.5)
    node, edge, fin = layer_call(
        (
            edge_src, edge_dst, send_index, edge_count, node_latent, edge_latent, node_cot,
            w_edge_in, w_edge_out, w_node_in, w_node_out, gain_edge, gain_node,
        ),
        factor,
    )
    node, edge, ein, *rest = finish_call(node, edge, fin)
    return (node, edge, jnp.swapaxes(ein, 0, 1), *rest)


def solution(mesh):
    placed = (
        P("rep", "dom", None),
        P("rep", "dom", None),
        P("rep", "dom", None),
        P("dom"),
        P("dom"),
        P("dom"),
        P("dom", None, None),
        P("segment", None, None),
        P("segment", None, None),
        P("segment", None, None),
        P("segment", None, None),
        P("segment", None),
        P("segment", None),
    )
    return jax.shard_map(
        body,
        mesh=mesh,
        in_specs=placed,
        out_specs=(
            P("segment", "rep", "dom", None),
            P("segment", "rep", "dom", None),
            P("segment", ("dom", "rep"), None),
            P("segment", ("dom", "rep"), None),
            P("segment", ("dom", "rep"), None),
            P("segment", ("dom", "rep"), None),
            P("segment", ("dom", "rep")),
            P("segment", ("dom", "rep")),
        ),
        check_vma=False,
    )
```

```python
import functools

import jax
import jax.numpy as jnp
from jax import lax
from jax.experimental import pallas as pl
from jax.experimental.pallas import tpu as pltpu
from jax.sharding import PartitionSpec as P

OFFSETS = (1, -1, 2, -2)
HALO = 16
EPS = 1e-05
MESH = pl.DeviceIdType.MESH
ROWS_A = 48
ROWS_B = 64
GAIN = 16
NODES_DEV = 128
EDGES_DEV = 384
HALOS = 64
TABLE = 192
BLOCK = 128
BF = jnp.bfloat16
F4 = jnp.float32


def mm(a, b):
    return jnp.dot(a, b, preferred_element_type=F4)


def mm_nt(a, b):
    return lax.dot_general(a, b, (((1,), (1,)), ((), ())), preferred_element_type=F4)


def mm_tn(a, b):
    return lax.dot_general(a, b, (((0,), (0,)), ((), ())), preferred_element_type=F4)


def silu_grad(pre):
    sig = jax.nn.sigmoid(pre)
    return sig * (1.0 + pre * (1.0 - sig))


def layer_kernel(
    src_in, dst_in, send_in, count_in, node_in, edge_in, cot_in,
    w_ein_in, w_eout_in, w_nin_in, w_nout_in, gain_e_in, gain_n_in,
    node_out, edge_out, fin_out,
    src_row, dst_row, send_row, count, w_ein, w_eout, w_nin, w_nout, gain_e, gain_n, l_first,
    oht, oh, inc, inct, sendt, sendm,
    tab, ein, cn, ce, cn32, halo1, halo2, hs1, hs2, bh,
    sr, pre, mid, tmp, xhat, rstd, enew, agg, pren, midn, tmpn, xhatn, rstdn, hnew,
    doutn, dpren, down, dagg, doute, dpre, gs, gr, de, dh, dge, dgn,
    s_halo1, s_halo2, r_halo, s_fe, r_fe, s_fh, r_fh,
    s_bh, r_bh1, r_bh2, s_be, r_be, s_bo, r_bo,
    l_node, l_edge, l_cot, l_nout, l_eout,
    ga, gb, ta, ua, va, tb, ub, vb, a2, ta2, ua2, va2, b2, tb2, ub2, vb2, c3, rc3, fin, rfin,
    send_sem, recv_sem, l_fin,
    *, nz, factor,
):
    seg = lax.axis_index("segment")
    dom = lax.axis_index("dom")
    n_dom = lax.axis_size("dom")
    first = seg == 0
    second = seg == 1

    def near(step, segment):
        return {"dom": (dom + step + n_dom) % n_dom, "segment": segment}

    rep = lax.axis_index("rep")
    z = dom // 8
    y = (dom // 2) % 4
    px = rep * 2 + dom % 2

    def at_y(p):
        return {"dom": z * 8 + p * 2 + dom % 2}

    def at_z(p):
        return {"dom": p * 8 + dom % 8}

    def at_x(p):
        return {"dom": (dom // 2) * 2 + p % 2, "rep": p // 2}

    z_peers = [(z + j) % nz for j in range(1, nz)]
    x_peers = [(px + j) % 4 for j in range(1, 4)]
    greet = [near(step, s) for step in OFFSETS for s in range(2)]
    greet += [at_y((y + 1) % 4), at_y((y + 3) % 4)]
    greet += [at_x(p) for p in x_peers] + [at_z(p) for p in z_peers]
    greet += [{"segment": 1 - seg}]
    barrier = pltpu.get_barrier_semaphore()
    for device in greet:
        pl.semaphore_signal(barrier, inc=1, device_id=device, device_id_type=MESH)

    def remote(src, dst, send, recv, device):
        return pltpu.make_async_remote_copy(
            src_ref=src, dst_ref=dst, send_sem=send, recv_sem=recv,
            device_id=device, device_id_type=MESH,
        )

    def load_node(k):
        return pltpu.make_async_copy(node_in.at[k], tab.at[k, 0:NODES_DEV], l_node.at[k])

    def load_edge(k):
        return pltpu.make_async_copy(edge_in.at[k], ein.at[k], l_edge.at[k])

    def load_cot(k):
        return pltpu.make_async_copy(cot_in.at[k], cn.at[k], l_cot.at[k])

    def store_node(src, k):
        return pltpu.make_async_copy(src.at[k], node_out.at[k], l_nout.at[k])

    def store_edge(src, k):
        return pltpu.make_async_copy(src.at[k], edge_out.at[k], l_eout.at[k])

    def halo_copy(src, k, j, sems, segment):
        rows = slice(j * HALO, (j + 1) * HALO)
        into = slice(NODES_DEV + j * HALO, NODES_DEV + (j + 1) * HALO)
        return remote(
            src.at[k, rows], tab.at[k, into], sems.at[k, j], r_halo.at[k, j],
            near(OFFSETS[j], segment),
        )

    def back_copy(dst, k, j, recv):
        rows = slice(j * HALO, (j + 1) * HALO)
        return remote(
            bh.at[k, rows], dst.at[k, rows], s_bh.at[k, j], recv.at[k, j],
            near(-OFFSETS[j], 0),
        )

    def sib_e(k):
        return remote(enew.at[k], ein.at[k], s_fe.at[k], r_fe.at[k], {"segment": 1 - seg})

    def sib_h(k):
        return remote(
            hnew.at[k], tab.at[k, 0:NODES_DEV], s_fh.at[k], r_fh.at[k], {"segment": 1 - seg}
        )

    def sib_de(k):
        return remote(de.at[k], ce.at[k], s_be.at[k], r_be.at[k], {"segment": 1 - seg})

    def sib_do(k):
        return remote(down.at[k], cn32.at[k], s_bo.at[k], r_bo.at[k], {"segment": 1 - seg})

    small = [
        pltpu.make_async_copy(u, v, l_first.at[i])
        for i, (u, v) in enumerate(
            [
                (src_in, src_row), (dst_in, dst_row), (send_in, send_row), (count_in, count),
                (gain_e_in, gain_e), (gain_n_in, gain_n),
            ]
        )
    ]
    large = [
        pltpu.make_async_copy(u.at[0], v, l_first.at[6 + i])
        for i, (u, v) in enumerate(
            [(w_ein_in, w_ein), (w_eout_in, w_eout), (w_nin_in, w_nin), (w_nout_in, w_nout)]
        )
    ]
    for c in small:
        c.start()

    @pl.when(first)
    def _():
        for k in range(2):
            load_node(k).start()
            load_edge(k).start()

    @pl.when(second)
    def _():
        for k in range(2):
            load_cot(k).start()

    for c in large:
        c.start()
    for c in small:
        c.wait()
    node = lax.broadcasted_iota(jnp.int32, (NODES_DEV, HALO), 0)
    hots = [jnp.where(node == send_row[0, j : j + 1, :], 1.0, 0.0) for j in range(4)]
    f_send = jnp.concatenate(hots + [jnp.zeros((NODES_DEV, NODES_DEV - HALOS), F4)], axis=1)
    sendt[...] = f_send.astype(BF)
    sendm[...] = f_send.T.astype(BF)

    @pl.when(first)
    def _():
        for k in range(2):
            load_node(k).wait()
            hs1[k] = mm(sendm[0:HALOS], tab[k, 0:NODES_DEV]).astype(BF)

    pl.semaphore_wait(barrier, len(greet))

    @pl.when(first)
    def _():
        for k in range(2):
            for j in range(4):
                halo_copy(hs1, k, j, s_halo1, 0).start()

    live_count = count[0]
    hot_src = lax.broadcasted_iota(jnp.int32, (TABLE, EDGES_DEV), 0) == src_row[...].reshape(1, EDGES_DEV)
    owner = lax.broadcasted_iota(jnp.int32, (NODES_DEV, EDGES_DEV), 0)
    slot = lax.broadcasted_iota(jnp.int32, (NODES_DEV, EDGES_DEV), 1)
    hot_dst = owner == dst_row[...].reshape(1, EDGES_DEV)
    hot_inc = hot_dst & (slot < live_count)
    f_src = jnp.where(hot_src, 1.0, 0.0)
    f_dst = jnp.where(hot_dst, 1.0, 0.0)
    f_inc = jnp.where(hot_inc, 1.0, 0.0)
    oht[0:TABLE] = f_src.astype(BF)
    oht[TABLE:] = f_dst.astype(BF)
    inc[...] = f_inc.astype(BF)
    oh[:, 0:TABLE] = f_src.T.astype(BF)
    oh[:, TABLE:] = f_dst.T.astype(BF)
    inct[...] = f_inc.T.astype(BF)
    dge[...] = jnp.zeros_like(dge)
    dgn[...] = jnp.zeros_like(dgn)

    @pl.when(second)
    def _():
        ce[...] = jnp.zeros_like(ce)

    for c in large:
        c.wait()

    def mean(v):
        return jnp.sum(v, axis=-1, keepdims=True) * (1.0 / 512.0)

    def norm_block(outer, at, k, x_ref, r_ref):
        center = outer - mean(outer)
        inv = lax.rsqrt(mean(center * center) + EPS)
        hat = center * inv
        x_ref[k, at, :] = hat
        r_ref[k, at, :] = jnp.broadcast_to(inv, (BLOCK, 128))
        return hat

    def norm_back(cot, gain, hat, inv):
        dy = cot * gain
        return inv * (dy - mean(dy) - hat * mean(dy * hat))

    def forward(k):
        @pl.when(first)
        def _():
            load_edge(k).wait()

        @pl.when(second)
        def _():
            sib_e(k).wait_recv()

        pre[k] = mm(ein[k], w_ein[0:512])

        @pl.when(second)
        def _():
            sib_h(k).wait_recv()

        own = tab[k, 0:NODES_DEV]
        sr[TABLE:] = mm(own, w_ein[1024:1536]).astype(BF)
        for j in range(4):
            halo_copy(hs1, k, j, s_halo1, 0).wait_recv()
        sr[0:TABLE] = mm(tab[k], w_ein[512:1024]).astype(BF)
        tmp[...] = mm(oh[...], sr[...])

        @pl.loop(0, EDGES_DEV // BLOCK, unroll=True)
        def _(i):
            at = pl.ds(pl.multiple_of(i * BLOCK, BLOCK), BLOCK)
            v = pre[k, at, :] + tmp[at, :]
            pre[k, at, :] = v
            mid[k, at, :] = (v * jax.nn.sigmoid(v)).astype(BF)

        tmp[...] = mm(mid[k], w_eout[...])

        @pl.loop(0, EDGES_DEV // BLOCK, unroll=True)
        def _(i):
            at = pl.ds(pl.multiple_of(i * BLOCK, BLOCK), BLOCK)
            hat = norm_block(tmp[at, :], at, k, xhat, rstd)
            rows = lax.broadcasted_iota(jnp.int32, (BLOCK, 512), 0) + i * BLOCK
            old = ein[k, at, :].astype(F4)
            enew[k, at, :] = jnp.where(rows < live_count, old + hat * gain_e[...], old).astype(BF)

        @pl.when(first)
        def _():
            sib_e(k).start()

        @pl.when(second)
        def _():
            store_edge(enew, k).start()

        agg[k] = mm(inc[...], enew[k]).astype(BF)
        pren[k] = mm(own, w_nin[0:512]) + mm(agg[k], w_nin[512:1024])

        @pl.loop(0, NODES_DEV // BLOCK, unroll=True)
        def _(i):
            at = pl.ds(pl.multiple_of(i * BLOCK, BLOCK), BLOCK)
            v = pren[k, at, :]
            midn[k, at, :] = (v * jax.nn.sigmoid(v)).astype(BF)

        tmpn[...] = mm(midn[k], w_nout[...])

        @pl.loop(0, NODES_DEV // BLOCK, unroll=True)
        def _(i):
            at = pl.ds(pl.multiple_of(i * BLOCK, BLOCK), BLOCK)
            hat = norm_block(tmpn[at, :], at, k, xhatn, rstdn)
            hnew[k, at, :] = (tab[k, at, :].astype(F4) + hat * gain_n[...]).astype(BF)

        @pl.when(first)
        def _():
            sib_h(k).start()
            hs2[k] = mm(sendm[0:HALOS], hnew[k]).astype(BF)
            for j in range(4):
                halo_copy(hs2, k, j, s_halo2, 1).start()

        @pl.when(second)
        def _():
            store_node(hnew, k).start()

    def backward(k):
        @pl.when(first)
        def _():
            sib_do(k).wait_recv()
            for j in range(4):
                back_copy(halo1, k, j, r_bh1).wait_recv()
            cn[k] = (cn32[k] + mm(sendt[:, 0:HALOS], halo1[k])).astype(BF)

        @pl.when(second)
        def _():
            load_cot(k).wait()

        @pl.loop(0, NODES_DEV // BLOCK, unroll=True)
        def _(i):
            at = pl.ds(pl.multiple_of(i * BLOCK, BLOCK), BLOCK)
            cot = cn[k, at, :].astype(F4)
            hat = xhatn[k, at, :]
            dgn[...] += jnp.sum((cot * hat).reshape(BLOCK // 8, 8, 512), axis=0)
            inv = rstdn[k, at, 0:1]
            doutn[k, at, :] = norm_back(cot, gain_n[...], hat, inv).astype(BF)

        tmpn[...] = mm_nt(doutn[k], w_nout[...])

        @pl.loop(0, NODES_DEV // BLOCK, unroll=True)
        def _(i):
            at = pl.ds(pl.multiple_of(i * BLOCK, BLOCK), BLOCK)
            dpren[k, at, :] = (tmpn[at, :] * silu_grad(pren[k, at, :])).astype(BF)

        dagg[...] = mm_nt(dpren[k], w_nin[512:1024]).astype(BF)

        @pl.when(first)
        def _():
            sib_de(k).wait_recv()

        tmp[...] = mm(inct[...], dagg[...])
        down[k] = cn[k].astype(F4) + mm_nt(dpren[k], w_nin[0:512])

        @pl.loop(0, EDGES_DEV // BLOCK, unroll=True)
        def _(i):
            at = pl.ds(pl.multiple_of(i * BLOCK, BLOCK), BLOCK)
            cot = tmp[at, :] + ce[k, at, :].astype(F4)
            tmp[at, :] = cot
            rows = lax.broadcasted_iota(jnp.int32, (BLOCK, 512), 0) + i * BLOCK
            cot = jnp.where(rows < live_count, cot, 0.0)
            hat = xhat[k, at, :]
            dge[...] += jnp.sum((cot * hat).reshape(BLOCK // 8, 8, 512), axis=0)
            inv = rstd[k, at, 0:1]
            doute[k, at, :] = norm_back(cot, gain_e[...], hat, inv).astype(BF)

        grad = mm_nt(doute[k], w_eout[...])
        pre[k] = grad * silu_grad(pre[k])
        dpre[k] = pre[k].astype(BF)
        gs[k] = mm(oht[0:TABLE], dpre[k]).astype(BF)
        gr[k] = mm(oht[TABLE:], dpre[k]).astype(BF)
        bh[k] = mm_nt(gs[k, NODES_DEV:], w_ein[512:1024]).astype(BF)

        @pl.when(first)
        def _():
            for j in range(4):
                back_copy(halo2, k, j, r_bh2).start()

        @pl.when(second)
        def _():
            for j in range(4):
                back_copy(halo1, k, j, r_bh1).start()

        down[k] += mm_nt(gs[k, 0:NODES_DEV], w_ein[512:1024]) + mm_nt(gr[k], w_ein[1024:1536])

        @pl.when(second)
        def _():
            sib_do(k).start()

        de[k] = (tmp[...] + mm_nt(dpre[k], w_ein[0:512])).astype(BF)

        @pl.when(second)
        def _():
            sib_de(k).start()

        @pl.when(first)
        def _():
            store_edge(de, k).start()

    @pl.loop(0, 4)
    def _(step):
        forward_now = (step == 0) | (step == 1 + seg)
        k = jnp.where(first, step % 2, step // 2)

        @pl.when(forward_now)
        def _():
            forward(k)

        @pl.when(jnp.logical_not(forward_now))
        def _():
            backward(k)

    def put_ein(base, value):
        for q in range(8):
            r = base + q * 16
            row = (r // 192) * ROWS_A + r % ROWS_A
            ga[(r % 192) // ROWS_A, row : row + 16, :] = value[q * 16 : q * 16 + 16].astype(BF)

    def put_b(base, width, offset, value):
        for q in range(128 // width):
            zy = base // width + q
            piece = value[q * width : (q + 1) * width].astype(BF)
            for b in range(4):
                gb[b, zy, offset : offset + width, :] = piece[:, b * 128 : (b + 1) * 128]

    def both(ref):
        return ref[...].reshape(ref.shape[0] * ref.shape[1], ref.shape[2])

    def cols(ref, m):
        return jnp.concatenate([ref[0, :, m * 128 : (m + 1) * 128], ref[1, :, m * 128 : (m + 1) * 128]], axis=0)

    def own_cols(m):
        at = slice(m * 128, (m + 1) * 128)
        return jnp.concatenate([tab[0, 0:NODES_DEV, at], tab[1, 0:NODES_DEV, at]], axis=0)

    def copy(n, src, dst, device):
        return remote(src, dst, send_sem.at[n], recv_sem.at[n], device)

    class Ring:
        def __init__(self, base, src, t, u, v, me, at, cut):
            right, left, across = (me + 1) % 4, (me + 3) % 4, (me + 2) % 4
            lo, hi = slice(0, cut), slice(cut, t.shape[0])
            self.out = [
                copy(base, src.at[across, lo], t.at[lo], at(right)),
                copy(base + 1, src.at[across, hi], t.at[hi], at(left)),
                copy(base + 2, src.at[right, hi], u.at[hi], at(right)),
                copy(base + 3, src.at[left, lo], v.at[lo], at(left)),
                copy(base + 4, t.at[lo], u.at[lo], at(right)),
                copy(base + 5, t.at[hi], v.at[hi], at(left)),
            ]
            self.src, self.t, self.u, self.v = src, t, u, v
            self.me, self.right, self.left, self.cut = me, right, left, cut

        def start(self):
            for c in self.out[:4]:
                c.start()

        def middle(self, block):
            src, t, n, cut = self.src, self.t, self.t.shape[0], self.cut
            for c, q, lo, hi in ((0, self.right, 0, cut), (1, self.left, cut, n)):
                self.out[c].wait_recv()

                @pl.loop(lo // block, hi // block)
                def _(i):
                    at = pl.ds(pl.multiple_of(i * block, block), block)
                    t[at] = (t[at].astype(F4) + src[q, at].astype(F4)).astype(BF)

                self.out[4 + c].start()

        def total(self, at):
            own = self.src[self.me, at].astype(F4)
            return own + self.u[at].astype(F4) + self.v[at].astype(F4)

        def arrive(self):
            for c in self.out[2:]:
                c.wait_recv()

    ring_a = Ring(0, ga, ta, ua, va, y, at_y, 208)
    ring_b = Ring(6, gb, tb, ub, vb, px, at_x, 2 * nz)
    ring_a2 = Ring(12, a2, ta2, ua2, va2, px, at_x, 208)
    ring_b2 = Ring(18, b2, tb2, ub2, vb2, y, at_y, nz // 2)

    for m in range(4):
        base = m * 128
        put_b(base, 16, 48, mm_tn(cols(midn, m), both(doutn)))
        put_b(base, 32, 0, mm_tn(own_cols(m), both(dpren)))
        put_b(512 + base, 32, 0, mm_tn(cols(agg, m), both(dpren)))
        put_b(base, 16, 32, mm_tn(cols(mid, m), both(doute)))
    ring_b.start()
    for m in range(4):
        base = m * 128
        put_ein(base, mm_tn(cols(ein, m), both(dpre)))
        put_ein(512 + base, mm_tn(cols(tab, m), both(gs)))
        put_ein(1024 + base, mm_tn(own_cols(m), both(gr)))
    row = lax.broadcasted_iota(jnp.int32, (GAIN, 512), 0)
    sum_e = jnp.sum(dge[...], axis=0, keepdims=True)
    sum_n = jnp.sum(dgn[...], axis=0, keepdims=True)
    gains = jnp.where(row == 0, sum_e, jnp.where(row == 1, sum_n, 0.0)).astype(BF)
    for q in range(4):
        ga[q, EDGES_DEV:, :] = gains
    ring_a.start()

    @pl.when(first)
    def _():
        for k in range(2):
            for j in range(4):
                back_copy(halo2, k, j, r_bh2).wait_recv()
            dh[k] = (down[k] + mm(sendt[:, 0:HALOS], halo2[k])).astype(BF)
            store_node(dh, k).start()

    ring_a.middle(16)
    ring_b.middle(1)
    ring_a.arrive()

    @pl.loop(0, ga.shape[1] // 16)
    def _(i):
        at = pl.ds(pl.multiple_of(i * 16, 16), 16)
        total = ring_a.total(at).astype(BF)
        for b in range(4):
            a2[b, at, :] = total[:, b * 128 : (b + 1) * 128]

    ring_a2.start()
    ring_b.arrive()

    @pl.loop(0, nz)
    def _(i):
        for q in range(4):
            b2[q, i] = ring_b.total(i * 4 + q).astype(BF)

    ring_b2.start()
    ring_a2.middle(16)
    ring_b2.middle(1)
    ring_a2.arrive()
    gains = ring_a2.total(slice(nz * ROWS_A, nz * ROWS_A + GAIN)).astype(BF)

    @pl.loop(0, nz)
    def _(i):
        at = pl.ds(pl.multiple_of(i * ROWS_A, 16), ROWS_A)
        c3[i, 0:ROWS_A, :] = ring_a2.total(at).astype(BF)
        c3[i, ROWS_A : ROWS_A + GAIN, :] = gains

    ring_b2.arrive()

    @pl.loop(0, nz)
    def _(i):
        c3[i, ROWS_A + GAIN :, :] = ring_b2.total(i).astype(BF)

    third = [copy(24 + j, c3.at[p], rc3.at[j], at_z(p)) for j, p in enumerate(z_peers)]
    for c in third:
        c.start()
    total = c3[z].astype(F4)
    for j, c in enumerate(third):
        c.wait_recv()
        total = total + rc3[j].astype(F4)
    total = total * factor

    n0 = ROWS_A + GAIN
    for p in range(4):
        b = (p % 2) * 2 + p // 2
        fin[p, 0:12, :] = total[12 * b : 12 * b + 12]
        fin[p, 12:16, :] = total[n0 + 32 + 4 * b : n0 + 32 + 4 * b + 4]
        fin[p, 16:24, :] = total[n0 + 8 * b : n0 + 8 * b + 8]
        fin[p, 24:28, :] = total[n0 + 48 + 4 * b : n0 + 48 + 4 * b + 4]
        fin[p, 28:32, :] = total[ROWS_A : ROWS_A + 4]
    base = 24 + nz - 1
    last = [copy(base + j, fin.at[p], rfin.at[px], at_x(p)) for j, p in enumerate(x_peers)]
    for c in last:
        c.start()
    rfin[px] = fin[px]
    for c in last:
        c.wait_recv()
    result = pltpu.make_async_copy(rfin, fin_out, l_fin.at[0])
    result.start()
    result.wait()
    for c in ring_a.out + ring_b.out + ring_a2.out + ring_b2.out + third + last:
        c.wait_send()

    @pl.when(first)
    def _():
        for k in range(2):
            sib_e(k).wait_send()
            sib_h(k).wait_send()
            for j in range(4):
                halo_copy(hs1, k, j, s_halo1, 0).wait_send()
                halo_copy(hs2, k, j, s_halo2, 1).wait_send()
                back_copy(halo2, k, j, r_bh2).wait_send()
            store_edge(de, k).wait()
            store_node(dh, k).wait()

    @pl.when(second)
    def _():
        for k in range(2):
            sib_do(k).wait_send()
            sib_de(k).wait_send()
            for j in range(4):
                back_copy(halo1, k, j, r_bh1).wait_send()
            store_edge(enew, k).wait()
            store_node(hnew, k).wait()


def layer_call(operands, factor):
    hbm = pl.BlockSpec(memory_space=pl.ANY)
    nz = 8
    i32 = jnp.int32

    def bf(*shape):
        return pltpu.VMEM(shape, BF)

    def fl(*shape):
        return pltpu.VMEM(shape, F4)

    dma = pltpu.SemaphoreType.DMA
    n, e = NODES_DEV, EDGES_DEV
    rows = nz * ROWS_A + GAIN
    copies = 24 + nz - 1 + 3
    return pl.pallas_call(
        functools.partial(layer_kernel, nz=nz, factor=factor),
        out_shape=[
            jax.ShapeDtypeStruct((2, n, 512), BF),
            jax.ShapeDtypeStruct((2, e, 512), BF),
            jax.ShapeDtypeStruct((4, 32, 128), F4),
        ],
        in_specs=[hbm] * 13,
        out_specs=[hbm] * 3,
        scratch_shapes=[
            pltpu.VMEM((e,), i32), pltpu.VMEM((e,), i32), pltpu.VMEM((1, 4, HALO), i32), pltpu.SMEM((1,), i32),
            bf(1536, 512), bf(512, 512), bf(1024, 512), bf(512, 512), fl(1, 512), fl(1, 512), dma((10,)),
            bf(320, e), bf(e, 320), bf(n, e), bf(e, n), bf(n, n), bf(n, n),
            bf(2, TABLE, 512), bf(2, e, 512), bf(2, n, 512), bf(2, e, 512), fl(2, n, 512),
            bf(2, HALOS, 512), bf(2, HALOS, 512), bf(2, HALOS, 512), bf(2, HALOS, 512), bf(2, HALOS, 512),
            bf(320, 512), fl(2, e, 512), bf(2, e, 512), fl(e, 512), fl(2, e, 512), fl(2, e, 128),
            bf(2, e, 512), bf(2, n, 512), fl(2, n, 512), bf(2, n, 512), fl(n, 512), fl(2, n, 512),
            fl(2, n, 128), bf(2, n, 512),
            bf(2, n, 512), bf(2, n, 512), fl(2, n, 512), bf(n, 512), bf(2, e, 512), bf(2, e, 512),
            bf(2, TABLE, 512), bf(2, n, 512), bf(2, e, 512), bf(2, n, 512), fl(8, 512), fl(8, 512),
            dma((2, 4)), dma((2, 4)), dma((2, 4)), dma((2,)), dma((2,)), dma((2,)), dma((2,)),
            dma((2, 4)), dma((2, 4)), dma((2, 4)), dma((2,)), dma((2,)), dma((2,)), dma((2,)),
            dma((2,)), dma((2,)), dma((2,)), dma((2,)), dma((2,)),
            bf(4, rows, 512), bf(4, 4 * nz, ROWS_B, 128),
            bf(rows, 512), bf(rows, 512), bf(rows, 512),
            bf(4 * nz, ROWS_B, 128), bf(4 * nz, ROWS_B, 128), bf(4 * nz, ROWS_B, 128),
            bf(4, rows, 128), bf(rows, 128), bf(rows, 128), bf(rows, 128),
            bf(4, nz, ROWS_B, 128), bf(nz, ROWS_B, 128), bf(nz, ROWS_B, 128), bf(nz, ROWS_B, 128),
            bf(nz, 128, 128), bf(nz - 1, 128, 128), fl(4, 32, 128), fl(4, 32, 128),
            dma((copies,)), dma((copies,)), dma((1,)),
        ],
        compiler_params=pltpu.CompilerParams(
            collective_id=0, has_side_effects=True, vmem_limit_bytes=56 << 20
        ),
        name="layers",
    )(*operands)


def finish_kernel(
    node_in, edge_in, fin_in, node_o, edge_o, ein_o, eout_o, nin_o, nout_o, ge_o, gn_o,
    rfin, node_v, edge_v, sems, out_sems,
):
    first = pltpu.make_async_copy(fin_in, rfin, sems.at[0])
    first.start()
    parts = [(node_in.at[k], node_v.at[k], node_o.at[0, k]) for k in range(2)]
    for k in range(2):
        for q in range(2):
            at = slice(q * 192, q * 192 + 192)
            parts.append((edge_in.at[k, at], edge_v.at[k, at], edge_o.at[0, k, at]))
    moves = [pltpu.make_async_copy(u, v, sems.at[1 + i]) for i, (u, v, _) in enumerate(parts)]
    stores = [pltpu.make_async_copy(v, w, out_sems.at[i]) for i, (_, v, w) in enumerate(parts)]
    for c in moves:
        c.start()
    for c, w in zip(moves, stores):
        c.wait()
        w.start()
    first.wait()
    t = lax.axis_index("dom") * 2 + lax.axis_index("rep")
    lane = lax.broadcasted_iota(jnp.int32, (2, 128), 1)
    picked = jnp.zeros((2, 128), F4)
    for b in range(4):
        at = slice(b * 128, (b + 1) * 128)
        for r in range(12):
            ein_o[r, :, at] = rfin[b, r : r + 1, :]
        eout_o[0, :, at] = rfin[b, 12:16, :]
        nin_o[0, :, at] = rfin[b, 16:24, :]
        nout_o[0, :, at] = rfin[b, 24:28, :]
        pair = rfin[b, 28:30, :]
        for i in range(4):
            hit = jnp.where(lane + b * 128 == t * 4 + i, pair, 0.0)
            value = jnp.sum(hit, axis=1, keepdims=True)
            picked = picked + jnp.where(lane == i, value, 0.0)
    ge_o[...] = picked[0:1, 0:4]
    gn_o[...] = picked[1:2, 0:4]
    for c in stores:
        c.wait()


def finish_call(node, edge, fin):
    hbm = pl.BlockSpec(memory_space=pl.ANY)
    vm = pl.BlockSpec(memory_space=pltpu.VMEM)
    return pl.pallas_call(
        finish_kernel,
        out_shape=[
            jax.ShapeDtypeStruct((1, *node.shape), BF),
            jax.ShapeDtypeStruct((1, *edge.shape), BF),
            jax.ShapeDtypeStruct((12, 1, 512), F4),
            jax.ShapeDtypeStruct((1, 4, 512), F4),
            jax.ShapeDtypeStruct((1, 8, 512), F4),
            jax.ShapeDtypeStruct((1, 4, 512), F4),
            jax.ShapeDtypeStruct((1, 4), F4),
            jax.ShapeDtypeStruct((1, 4), F4),
        ],
        in_specs=[hbm] * 3,
        out_specs=[hbm] * 2 + [vm] * 6,
        scratch_shapes=[
            pltpu.VMEM((4, 32, 128), F4), pltpu.VMEM(node.shape, BF), pltpu.VMEM(edge.shape, BF),
            pltpu.SemaphoreType.DMA((7,)), pltpu.SemaphoreType.DMA((6,)),
        ],
        compiler_params=pltpu.CompilerParams(vmem_limit_bytes=56 << 20),
        name="finish",
    )(node, edge, fin)


def body(
    node_latent, edge_latent, node_cot, edge_src, edge_dst, edge_count, send_index,
    w_edge_in, w_edge_out, w_node_in, w_node_out, gain_edge, gain_node,
):
    micro = node_latent.shape[0]
    factor = float(micro * lax.axis_size("rep") * NODES_DEV * lax.axis_size("dom")) ** (-0.5)
    node, edge, fin = layer_call(
        (
            edge_src, edge_dst, send_index, edge_count, node_latent, edge_latent, node_cot,
            w_edge_in, w_edge_out, w_node_in, w_node_out, gain_edge, gain_node,
        ),
        factor,
    )
    node, edge, ein, *rest = finish_call(node, edge, fin)
    return (node, edge, jnp.swapaxes(ein, 0, 1), *rest)


def solution(mesh):
    placed = (
        P("rep", "dom", None),
        P("rep", "dom", None),
        P("rep", "dom", None),
        P("dom"),
        P("dom"),
        P("dom"),
        P("dom", None, None),
        P("segment", None, None),
        P("segment", None, None),
        P("segment", None, None),
        P("segment", None, None),
        P("segment", None),
        P("segment", None),
    )
    return jax.shard_map(
        body,
        mesh=mesh,
        in_specs=placed,
        out_specs=(
            P("segment", "rep", "dom", None),
            P("segment", "rep", "dom", None),
            P("segment", ("dom", "rep"), None),
            P("segment", ("dom", "rep"), None),
            P("segment", ("dom", "rep"), None),
            P("segment", ("dom", "rep"), None),
            P("segment", ("dom", "rep")),
            P("segment", ("dom", "rep")),
        ),
        check_vma=False,
    )
```

```python
import functools

import jax
import jax.numpy as jnp
from jax import lax
from jax.experimental import pallas as pl
from jax.experimental.pallas import tpu as pltpu
from jax.sharding import PartitionSpec as P

OFFSETS = (1, -1, 2, -2)
HALO = 16
EPS = 1e-05
MESH = pl.DeviceIdType.MESH
ROWS_A = 48
GAIN = 16
NODES_DEV = 128
EDGES_DEV = 384
HALOS = 64
TABLE = 192
BLOCK = 128
BF = jnp.bfloat16
F4 = jnp.float32


def mm(a, b):
    return jnp.dot(a, b, preferred_element_type=F4)


def mm_tn(a, b):
    return lax.dot_general(a, b, (((0,), (0,)), ((), ())), preferred_element_type=F4)


def silu_grad(pre):
    sig = jax.nn.sigmoid(pre)
    return sig * (1.0 + pre * (1.0 - sig))


def layer_kernel(
    src_in, dst_in, send_in, count_in, node_in, edge_in, cot_in,
    w_ein_in, w_eout_in, w_nin_in, w_nout_in, gain_e_in, gain_n_in,
    node_out, edge_out, fin_out,
    src_row, dst_row, send_row, count, w_ein, w_eout, w_nin, w_nout, gain_e, gain_n, l_first,
    t_ein, t_eout, t_nin, t_nout, oht, oh, inc, inct, sendt, sendm,
    tab, ein, cn, ce, cn32, halo1, halo2, hs1, hs2, bh,
    sr, pre, mid, tmp, xhat, rstd, enew, agg, pren, midn, tmpn, xhatn, rstdn, hnew,
    doutn, dpren, down, dagg, doute, dpre, gs, gr, de, dh, dge, dgn,
    s_halo1, s_halo2, r_halo, s_fe, r_fe, s_fh, r_fh,
    s_bh, r_bh1, r_bh2, s_be, r_be, s_bo, r_bo,
    l_node, l_edge, l_cot, l_nout, l_eout,
    ga, gb, ta, ua, va, tb, ub, vb, a2, ta2, ua2, va2, b2, tb2, ub2, vb2, ca, ra, cb, rb, fin,
    send_sem, recv_sem, l_fin,
    *, nz, factor,
):
    seg = lax.axis_index("segment")
    dom = lax.axis_index("dom")
    n_dom = lax.axis_size("dom")
    first = seg == 0
    second = seg == 1

    def near(step, segment):
        return {"dom": (dom + step + n_dom) % n_dom, "segment": segment}

    rep = lax.axis_index("rep")
    z = dom // 8
    y = (dom // 2) % 4
    px = rep * 2 + dom % 2

    def at_y(p):
        return {"dom": z * 8 + p * 2 + dom % 2}

    def at_z(p):
        return {"dom": p * 8 + dom % 8}

    def at_x(p):
        return {"dom": (dom // 2) * 2 + p % 2, "rep": p // 2}

    z_peers = [(z + j) % nz for j in range(1, nz)]
    x_peers = [(px + j) % 4 for j in (1, 3)]
    greet = [near(step, s) for step in OFFSETS for s in range(2)]
    greet += [at_y((y + 1) % 4), at_y((y + 3) % 4)]
    greet += [at_x(p) for p in x_peers] + [at_z(p) for p in z_peers]
    greet += [{"segment": 1 - seg}]
    barrier = pltpu.get_barrier_semaphore()
    for device in greet:
        pl.semaphore_signal(barrier, inc=1, device_id=device, device_id_type=MESH)

    def remote(src, dst, send, recv, device):
        return pltpu.make_async_remote_copy(
            src_ref=src, dst_ref=dst, send_sem=send, recv_sem=recv,
            device_id=device, device_id_type=MESH,
        )

    def load_node(k):
        return pltpu.make_async_copy(node_in.at[k], tab.at[k, 0:NODES_DEV], l_node.at[k])

    def load_edge(k):
        return pltpu.make_async_copy(edge_in.at[k], ein.at[k], l_edge.at[k])

    def load_cot(k):
        return pltpu.make_async_copy(cot_in.at[k], cn.at[k], l_cot.at[k])

    def store_node(src, k):
        return pltpu.make_async_copy(src.at[k], node_out.at[k], l_nout.at[k])

    def store_edge(src, k):
        return pltpu.make_async_copy(src.at[k], edge_out.at[k], l_eout.at[k])

    def halo_copy(src, k, j, sems, segment):
        rows = slice(j * HALO, (j + 1) * HALO)
        into = slice(NODES_DEV + j * HALO, NODES_DEV + (j + 1) * HALO)
        return remote(
            src.at[k, rows], tab.at[k, into], sems.at[k, j], r_halo.at[k, j],
            near(OFFSETS[j], segment),
        )

    def back_copy(dst, k, j, recv):
        rows = slice(j * HALO, (j + 1) * HALO)
        return remote(
            bh.at[k, rows], dst.at[k, rows], s_bh.at[k, j], recv.at[k, j],
            near(-OFFSETS[j], 0),
        )

    def sib_e(k):
        return remote(enew.at[k], ein.at[k], s_fe.at[k], r_fe.at[k], {"segment": 1 - seg})

    def sib_h(k):
        return remote(
            hnew.at[k], tab.at[k, 0:NODES_DEV], s_fh.at[k], r_fh.at[k], {"segment": 1 - seg}
        )

    def sib_de(k):
        return remote(de.at[k], ce.at[k], s_be.at[k], r_be.at[k], {"segment": 1 - seg})

    def sib_do(k):
        return remote(down.at[k], cn32.at[k], s_bo.at[k], r_bo.at[k], {"segment": 1 - seg})

    small = [
        pltpu.make_async_copy(u, v, l_first.at[i])
        for i, (u, v) in enumerate(
            [
                (src_in, src_row), (dst_in, dst_row), (send_in, send_row), (count_in, count),
                (gain_e_in, gain_e), (gain_n_in, gain_n),
            ]
        )
    ]
    large = [
        pltpu.make_async_copy(u.at[0], v, l_first.at[6 + i])
        for i, (u, v) in enumerate(
            [(w_ein_in, w_ein), (w_eout_in, w_eout), (w_nin_in, w_nin), (w_nout_in, w_nout)]
        )
    ]
    for c in small:
        c.start()

    @pl.when(first)
    def _():
        for k in range(2):
            load_node(k).start()
            load_edge(k).start()

    @pl.when(second)
    def _():
        for k in range(2):
            load_cot(k).start()

    for c in large:
        c.start()
    for c in small:
        c.wait()
    node = lax.broadcasted_iota(jnp.int32, (NODES_DEV, HALO), 0)
    hots = [jnp.where(node == send_row[0, j : j + 1, :], 1.0, 0.0) for j in range(4)]
    f_send = jnp.concatenate(hots + [jnp.zeros((NODES_DEV, NODES_DEV - HALOS), F4)], axis=1)
    sendt[...] = f_send.astype(BF)
    sendm[...] = f_send.T.astype(BF)

    @pl.when(first)
    def _():
        for k in range(2):
            load_node(k).wait()
            hs1[k] = mm(sendm[0:HALOS], tab[k, 0:NODES_DEV]).astype(BF)

    pl.semaphore_wait(barrier, len(greet))

    @pl.when(first)
    def _():
        for k in range(2):
            for j in range(4):
                halo_copy(hs1, k, j, s_halo1, 0).start()

    live_count = count[0]
    hot_src = lax.broadcasted_iota(jnp.int32, (TABLE, EDGES_DEV), 0) == src_row[...].reshape(1, EDGES_DEV)
    owner = lax.broadcasted_iota(jnp.int32, (NODES_DEV, EDGES_DEV), 0)
    slot = lax.broadcasted_iota(jnp.int32, (NODES_DEV, EDGES_DEV), 1)
    hot_dst = owner == dst_row[...].reshape(1, EDGES_DEV)
    hot_inc = hot_dst & (slot < live_count)
    f_src = jnp.where(hot_src, 1.0, 0.0)
    f_dst = jnp.where(hot_dst, 1.0, 0.0)
    f_inc = jnp.where(hot_inc, 1.0, 0.0)
    oht[0:TABLE] = f_src.astype(BF)
    oht[TABLE:] = f_dst.astype(BF)
    inc[...] = f_inc.astype(BF)
    oh[:, 0:TABLE] = f_src.T.astype(BF)
    oh[:, TABLE:] = f_dst.T.astype(BF)
    inct[...] = f_inc.T.astype(BF)
    dge[...] = jnp.zeros_like(dge)
    dgn[...] = jnp.zeros_like(dgn)

    @pl.when(second)
    def _():
        ce[...] = jnp.zeros_like(ce)

    for c in large:
        c.wait()

    def mean(v):
        return jnp.sum(v, axis=-1, keepdims=True) * (1.0 / 512.0)

    def norm_block(outer, at, k, x_ref, r_ref):
        center = outer - mean(outer)
        inv = lax.rsqrt(mean(center * center) + EPS)
        hat = center * inv
        x_ref[k, at, :] = hat
        r_ref[k, at, :] = jnp.broadcast_to(inv, (BLOCK, 128))
        return hat

    def norm_back(cot, gain, hat, inv):
        dy = cot * gain
        return inv * (dy - mean(dy) - hat * mean(dy * hat))

    def forward(k):
        @pl.when(first)
        def _():
            load_edge(k).wait()

        @pl.when(second)
        def _():
            sib_e(k).wait_recv()

        pre[k] = mm(ein[k], w_ein[0:512])

        @pl.when(second)
        def _():
            sib_h(k).wait_recv()

        own = tab[k, 0:NODES_DEV]
        sr[TABLE:] = mm(own, w_ein[1024:1536]).astype(BF)
        for j in range(4):
            halo_copy(hs1, k, j, s_halo1, 0).wait_recv()
        sr[0:TABLE] = mm(tab[k], w_ein[512:1024]).astype(BF)
        tmp[...] = mm(oh[...], sr[...])

        @pl.loop(0, EDGES_DEV // BLOCK, unroll=True)
        def _(i):
            at = pl.ds(pl.multiple_of(i * BLOCK, BLOCK), BLOCK)
            v = pre[k, at, :] + tmp[at, :]
            pre[k, at, :] = v
            mid[k, at, :] = (v * jax.nn.sigmoid(v)).astype(BF)

        tmp[...] = mm(mid[k], w_eout[...])

        @pl.loop(0, EDGES_DEV // BLOCK, unroll=True)
        def _(i):
            at = pl.ds(pl.multiple_of(i * BLOCK, BLOCK), BLOCK)
            hat = norm_block(tmp[at, :], at, k, xhat, rstd)
            rows = lax.broadcasted_iota(jnp.int32, (BLOCK, 512), 0) + i * BLOCK
            old = ein[k, at, :].astype(F4)
            enew[k, at, :] = jnp.where(rows < live_count, old + hat * gain_e[...], old).astype(BF)

        @pl.when(first)
        def _():
            sib_e(k).start()

        @pl.when(second)
        def _():
            store_edge(enew, k).start()

        agg[k] = mm(inc[...], enew[k]).astype(BF)
        pren[k] = mm(own, w_nin[0:512]) + mm(agg[k], w_nin[512:1024])

        @pl.loop(0, NODES_DEV // BLOCK, unroll=True)
        def _(i):
            at = pl.ds(pl.multiple_of(i * BLOCK, BLOCK), BLOCK)
            v = pren[k, at, :]
            midn[k, at, :] = (v * jax.nn.sigmoid(v)).astype(BF)

        tmpn[...] = mm(midn[k], w_nout[...])

        @pl.loop(0, NODES_DEV // BLOCK, unroll=True)
        def _(i):
            at = pl.ds(pl.multiple_of(i * BLOCK, BLOCK), BLOCK)
            hat = norm_block(tmpn[at, :], at, k, xhatn, rstdn)
            hnew[k, at, :] = (tab[k, at, :].astype(F4) + hat * gain_n[...]).astype(BF)

        @pl.when(first)
        def _():
            sib_h(k).start()
            hs2[k] = mm(sendm[0:HALOS], hnew[k]).astype(BF)
            for j in range(4):
                halo_copy(hs2, k, j, s_halo2, 1).start()

        @pl.when(second)
        def _():
            store_node(hnew, k).start()

    def backward(k):
        @pl.when(first)
        def _():
            sib_do(k).wait_recv()
            for j in range(4):
                back_copy(halo1, k, j, r_bh1).wait_recv()
            cn[k] = (cn32[k] + mm(sendt[:, 0:HALOS], halo1[k])).astype(BF)

        @pl.when(second)
        def _():
            load_cot(k).wait()

        @pl.loop(0, NODES_DEV // BLOCK, unroll=True)
        def _(i):
            at = pl.ds(pl.multiple_of(i * BLOCK, BLOCK), BLOCK)
            cot = cn[k, at, :].astype(F4)
            hat = xhatn[k, at, :]
            dgn[...] += jnp.sum((cot * hat).reshape(BLOCK // 8, 8, 512), axis=0)
            inv = rstdn[k, at, 0:1]
            doutn[k, at, :] = norm_back(cot, gain_n[...], hat, inv).astype(BF)

        tmpn[...] = mm(doutn[k], t_nout[...])

        @pl.loop(0, NODES_DEV // BLOCK, unroll=True)
        def _(i):
            at = pl.ds(pl.multiple_of(i * BLOCK, BLOCK), BLOCK)
            dpren[k, at, :] = (tmpn[at, :] * silu_grad(pren[k, at, :])).astype(BF)

        dagg[...] = mm(dpren[k], t_nin[:, 512:1024]).astype(BF)

        @pl.when(first)
        def _():
            sib_de(k).wait_recv()

        tmp[...] = mm(inct[...], dagg[...])
        down[k] = cn[k].astype(F4) + mm(dpren[k], t_nin[:, 0:512])

        @pl.loop(0, EDGES_DEV // BLOCK, unroll=True)
        def _(i):
            at = pl.ds(pl.multiple_of(i * BLOCK, BLOCK), BLOCK)
            cot = tmp[at, :] + ce[k, at, :].astype(F4)
            tmp[at, :] = cot
            rows = lax.broadcasted_iota(jnp.int32, (BLOCK, 512), 0) + i * BLOCK
            cot = jnp.where(rows < live_count, cot, 0.0)
            hat = xhat[k, at, :]
            dge[...] += jnp.sum((cot * hat).reshape(BLOCK // 8, 8, 512), axis=0)
            inv = rstd[k, at, 0:1]
            doute[k, at, :] = norm_back(cot, gain_e[...], hat, inv).astype(BF)

        grad = mm(doute[k], t_eout[...])
        pre[k] = grad * silu_grad(pre[k])
        dpre[k] = pre[k].astype(BF)
        gs[k] = mm(oht[0:TABLE], dpre[k]).astype(BF)
        gr[k] = mm(oht[TABLE:], dpre[k]).astype(BF)
        bh[k] = mm(gs[k, NODES_DEV:], t_ein[:, 512:1024]).astype(BF)

        @pl.when(first)
        def _():
            for j in range(4):
                back_copy(halo2, k, j, r_bh2).start()

        @pl.when(second)
        def _():
            for j in range(4):
                back_copy(halo1, k, j, r_bh1).start()

        down[k] += mm(gs[k, 0:NODES_DEV], t_ein[:, 512:1024]) + mm(gr[k], t_ein[:, 1024:1536])

        @pl.when(second)
        def _():
            sib_do(k).start()

        de[k] = (tmp[...] + mm(dpre[k], t_ein[:, 0:512])).astype(BF)

        @pl.when(second)
        def _():
            sib_de(k).start()

        @pl.when(first)
        def _():
            store_edge(de, k).start()

    @pl.loop(0, 4)
    def _(step):
        forward_now = (step == 0) | (step == 1 + seg)
        k = jnp.where(first, step % 2, step // 2)

        @pl.when(step == 2 - 2 * seg)
        def _():
            for m in range(3):
                t_ein[:, m * 512 : m * 512 + 512] = w_ein[m * 512 : m * 512 + 512].T
            for m in range(2):
                t_nin[:, m * 512 : m * 512 + 512] = w_nin[m * 512 : m * 512 + 512].T
            t_eout[...] = w_eout[...].T
            t_nout[...] = w_nout[...].T

        @pl.when(forward_now)
        def _():
            forward(k)

        @pl.when(jnp.logical_not(forward_now))
        def _():
            backward(k)

    def put_ein(base, value):
        for q in range(8):
            r = base + q * 16
            row = (r // 192) * ROWS_A + r % ROWS_A
            ga[(r % 192) // ROWS_A, row : row + 16, :] = value[q * 16 : q * 16 + 16].astype(BF)

    def put_b(m, n_lo, n_hi, e, o):
        for q in range(8):
            part = (n_lo, n_hi)[q // 4][q % 4 * 32 : q % 4 * 32 + 32]
            for p in range(4):
                b = p % 2 * 2 + p // 2
                r = q * 16 + 4 * b
                tile = jnp.concatenate([part[8 * b : 8 * b + 8], e[r : r + 4], o[r : r + 4]], axis=0)
                gb[p, m * 8 + q] = tile.astype(BF)

    def both(ref):
        return ref[...].reshape(ref.shape[0] * ref.shape[1], ref.shape[2])

    def cols(ref, m):
        return jnp.concatenate([ref[0, :, m * 128 : (m + 1) * 128], ref[1, :, m * 128 : (m + 1) * 128]], axis=0)

    def own_cols(m):
        at = slice(m * 128, (m + 1) * 128)
        return jnp.concatenate([tab[0, 0:NODES_DEV, at], tab[1, 0:NODES_DEV, at]], axis=0)

    def copy(n, src, dst, device):
        return remote(src, dst, send_sem.at[n], recv_sem.at[n], device)

    class Ring:
        def __init__(self, base, src, t, u, v, me, at, cut):
            right, left, across = (me + 1) % 4, (me + 3) % 4, (me + 2) % 4
            lo, hi = slice(0, cut), slice(cut, t.shape[0])
            self.out = [
                copy(base, src.at[across, lo], t.at[lo], at(right)),
                copy(base + 1, src.at[across, hi], t.at[hi], at(left)),
                copy(base + 2, src.at[right, hi], u.at[hi], at(right)),
                copy(base + 3, src.at[left, lo], v.at[lo], at(left)),
                copy(base + 4, t.at[lo], u.at[lo], at(right)),
                copy(base + 5, t.at[hi], v.at[hi], at(left)),
            ]
            self.src, self.t, self.u, self.v = src, t, u, v
            self.me, self.right, self.left, self.cut = me, right, left, cut

        def start(self):
            for c in self.out[:4]:
                c.start()

        def middle(self, block):
            src, t, n, cut = self.src, self.t, self.t.shape[0], self.cut
            for c, q, lo, hi in ((0, self.right, 0, cut), (1, self.left, cut, n)):
                self.out[c].wait_recv()

                @pl.loop(lo // block, hi // block)
                def _(i):
                    at = pl.ds(pl.multiple_of(i * block, block), block)
                    t[at] = (t[at].astype(F4) + src[q, at].astype(F4)).astype(BF)

                self.out[4 + c].start()

        def total(self, at):
            own = self.src[self.me, at].astype(F4)
            return own + self.u[at].astype(F4) + self.v[at].astype(F4)

        def arrive(self):
            for c in self.out[2:]:
                c.wait_recv()

    ring_a = Ring(0, ga, ta, ua, va, y, at_y, 208)
    ring_b = Ring(6, gb, tb, ub, vb, px, at_x, 2 * nz)
    ring_a2 = Ring(12, a2, ta2, ua2, va2, px, at_x, nz // 2)
    ring_b2 = Ring(18, b2, tb2, ub2, vb2, y, at_y, nz // 2)

    def nin_part(m):
        lhs = own_cols(m) if m < 4 else cols(agg, m - 4)
        return mm_tn(lhs, both(dpren))

    for m in range(4):
        put_b(
            m, nin_part(2 * m), nin_part(2 * m + 1),
            mm_tn(cols(mid, m), both(doute)), mm_tn(cols(midn, m), both(doutn)),
        )
    ring_b.start()
    for m in range(4):
        base = m * 128
        put_ein(base, mm_tn(cols(ein, m), both(dpre)))
        put_ein(512 + base, mm_tn(cols(tab, m), both(gs)))
        put_ein(1024 + base, mm_tn(own_cols(m), both(gr)))
    row = lax.broadcasted_iota(jnp.int32, (GAIN, 512), 0)
    sum_e = jnp.sum(dge[...], axis=0, keepdims=True)
    sum_n = jnp.sum(dgn[...], axis=0, keepdims=True)
    gains = jnp.where(row == 0, sum_e, jnp.where(row == 1, sum_n, 0.0)).astype(BF)
    for q in range(4):
        ga[q, EDGES_DEV:, :] = gains
    ring_a.start()

    @pl.when(first)
    def _():
        for k in range(2):
            for j in range(4):
                back_copy(halo2, k, j, r_bh2).wait_recv()
            dh[k] = (down[k] + mm(sendt[:, 0:HALOS], halo2[k])).astype(BF)
            store_node(dh, k).start()

    ring_a.middle(16)
    ring_b.middle(2)
    ring_a.arrive()
    gains = ring_a.total(slice(nz * ROWS_A, nz * ROWS_A + GAIN))[0:4]

    @pl.loop(0, nz)
    def _(i):
        at = pl.ds(pl.multiple_of(i * ROWS_A, 16), ROWS_A)
        total = ring_a.total(at)
        for p in range(4):
            b = p % 2 * 2 + p // 2
            tile = jnp.concatenate([total[12 * b : 12 * b + 12], gains], axis=0)
            a2[p, i] = tile.astype(BF)

    ring_a2.start()
    ring_b.arrive()

    @pl.loop(0, nz)
    def _(i):
        for q in range(4):
            b2[q, i] = ring_b.total(i * 4 + q).astype(BF)

    ring_b2.start()
    ring_a2.middle(2)
    ring_b2.middle(2)

    def along_z(base, ring, held, got):
        ring.arrive()
        for i in range(nz):
            held[i] = ring.total(i).astype(BF)
        moves = [copy(base + j, held.at[p], got.at[j], at_z(p)) for j, p in enumerate(z_peers)]
        for c in moves:
            c.start()
        return moves

    def z_total(moves, held, got):
        total = held[z].astype(F4)
        for j, c in enumerate(moves):
            c.wait_recv()
            total = total + got[j].astype(F4)
        return total * factor

    third_a = along_z(24, ring_a2, ca, ra)
    third_b = along_z(24 + nz - 1, ring_b2, cb, rb)
    fin[0:16] = z_total(third_a, ca, ra)
    fin[16:32] = z_total(third_b, cb, rb)
    result = pltpu.make_async_copy(fin, fin_out, l_fin.at[0])
    result.start()
    result.wait()
    for c in ring_a.out + ring_b.out + ring_a2.out + ring_b2.out + third_a + third_b:
        c.wait_send()

    @pl.when(first)
    def _():
        for k in range(2):
            sib_e(k).wait_send()
            sib_h(k).wait_send()
            for j in range(4):
                halo_copy(hs1, k, j, s_halo1, 0).wait_send()
                halo_copy(hs2, k, j, s_halo2, 1).wait_send()
                back_copy(halo2, k, j, r_bh2).wait_send()
            store_edge(de, k).wait()
            store_node(dh, k).wait()

    @pl.when(second)
    def _():
        for k in range(2):
            sib_do(k).wait_send()
            sib_de(k).wait_send()
            for j in range(4):
                back_copy(halo1, k, j, r_bh1).wait_send()
            store_edge(enew, k).wait()
            store_node(hnew, k).wait()


def layer_call(operands, factor):
    hbm = pl.BlockSpec(memory_space=pl.ANY)
    nz = 8
    i32 = jnp.int32

    def bf(*shape):
        return pltpu.VMEM(shape, BF)

    def fl(*shape):
        return pltpu.VMEM(shape, F4)

    dma = pltpu.SemaphoreType.DMA
    n, e = NODES_DEV, EDGES_DEV
    rows = nz * ROWS_A + GAIN
    copies = 24 + 2 * (nz - 1)
    return pl.pallas_call(
        functools.partial(layer_kernel, nz=nz, factor=factor),
        out_shape=[
            jax.ShapeDtypeStruct((2, n, 512), BF),
            jax.ShapeDtypeStruct((2, e, 512), BF),
            jax.ShapeDtypeStruct((32, 512), F4),
        ],
        in_specs=[hbm] * 13,
        out_specs=[hbm] * 3,
        scratch_shapes=[
            pltpu.VMEM((e,), i32), pltpu.VMEM((e,), i32), pltpu.VMEM((1, 4, HALO), i32), pltpu.SMEM((1,), i32),
            bf(1536, 512), bf(512, 512), bf(1024, 512), bf(512, 512), fl(1, 512), fl(1, 512), dma((10,)),
            bf(512, 1536), bf(512, 512), bf(512, 1024), bf(512, 512),
            bf(320, e), bf(e, 320), bf(n, e), bf(e, n), bf(n, n), bf(n, n),
            bf(2, TABLE, 512), bf(2, e, 512), bf(2, n, 512), bf(2, e, 512), fl(2, n, 512),
            bf(2, HALOS, 512), bf(2, HALOS, 512), bf(2, HALOS, 512), bf(2, HALOS, 512), bf(2, HALOS, 512),
            bf(320, 512), fl(2, e, 512), bf(2, e, 512), fl(e, 512), fl(2, e, 512), fl(2, e, 128),
            bf(2, e, 512), bf(2, n, 512), fl(2, n, 512), bf(2, n, 512), fl(n, 512), fl(2, n, 512),
            fl(2, n, 128), bf(2, n, 512),
            bf(2, n, 512), bf(2, n, 512), fl(2, n, 512), bf(n, 512), bf(2, e, 512), bf(2, e, 512),
            bf(2, TABLE, 512), bf(2, n, 512), bf(2, e, 512), bf(2, n, 512), fl(8, 512), fl(8, 512),
            dma((2, 4)), dma((2, 4)), dma((2, 4)), dma((2,)), dma((2,)), dma((2,)), dma((2,)),
            dma((2, 4)), dma((2, 4)), dma((2, 4)), dma((2,)), dma((2,)), dma((2,)), dma((2,)),
            dma((2,)), dma((2,)), dma((2,)), dma((2,)), dma((2,)),
            bf(4, rows, 512), bf(4, 4 * nz, 16, 512),
            bf(rows, 512), bf(rows, 512), bf(rows, 512),
            bf(4 * nz, 16, 512), bf(4 * nz, 16, 512), bf(4 * nz, 16, 512),
            bf(4, nz, 16, 512), bf(nz, 16, 512), bf(nz, 16, 512), bf(nz, 16, 512),
            bf(4, nz, 16, 512), bf(nz, 16, 512), bf(nz, 16, 512), bf(nz, 16, 512),
            bf(nz, 16, 512), bf(nz - 1, 16, 512), bf(nz, 16, 512), bf(nz - 1, 16, 512), fl(32, 512),
            dma((copies,)), dma((copies,)), dma((1,)),
        ],
        compiler_params=pltpu.CompilerParams(
            collective_id=0, has_side_effects=True, vmem_limit_bytes=56 << 20
        ),
        name="layers",
    )(*operands)


def finish_kernel(
    node_in, edge_in, fin_in, node_o, edge_o, ein_o, eout_o, nin_o, nout_o, ge_o, gn_o,
    rfin, node_v, edge_v, sems, out_sems,
):
    first = pltpu.make_async_copy(fin_in, rfin, sems.at[0])
    first.start()
    parts = [(node_in.at[k], node_v.at[k], node_o.at[0, k]) for k in range(2)]
    for k in range(2):
        for q in range(2):
            at = slice(q * 192, q * 192 + 192)
            parts.append((edge_in.at[k, at], edge_v.at[k, at], edge_o.at[0, k, at]))
    moves = [pltpu.make_async_copy(u, v, sems.at[1 + i]) for i, (u, v, _) in enumerate(parts)]
    stores = [pltpu.make_async_copy(v, w, out_sems.at[i]) for i, (_, v, w) in enumerate(parts)]
    for c in moves:
        c.start()
    for c, w in zip(moves, stores):
        c.wait()
        w.start()
    first.wait()
    t = lax.axis_index("dom") * 2 + lax.axis_index("rep")
    for r in range(12):
        ein_o[r] = rfin[r : r + 1]
    nin_o[0] = rfin[16:24]
    eout_o[0] = rfin[24:28]
    nout_o[0] = rfin[28:32]
    pair = rfin[12:14]
    lane = lax.broadcasted_iota(jnp.int32, (2, 512), 1)
    narrow = lax.broadcasted_iota(jnp.int32, (2, 128), 1)
    picked = jnp.zeros((2, 128), F4)
    for i in range(4):
        value = jnp.sum(jnp.where(lane == t * 4 + i, pair, 0.0), axis=1, keepdims=True)
        picked = picked + jnp.where(narrow == i, value, 0.0)
    ge_o[...] = picked[0:1, 0:4]
    gn_o[...] = picked[1:2, 0:4]
    for c in stores:
        c.wait()


def finish_call(node, edge, fin):
    hbm = pl.BlockSpec(memory_space=pl.ANY)
    vm = pl.BlockSpec(memory_space=pltpu.VMEM)
    return pl.pallas_call(
        finish_kernel,
        out_shape=[
            jax.ShapeDtypeStruct((1, *node.shape), BF),
            jax.ShapeDtypeStruct((1, *edge.shape), BF),
            jax.ShapeDtypeStruct((12, 1, 512), F4),
            jax.ShapeDtypeStruct((1, 4, 512), F4),
            jax.ShapeDtypeStruct((1, 8, 512), F4),
            jax.ShapeDtypeStruct((1, 4, 512), F4),
            jax.ShapeDtypeStruct((1, 4), F4),
            jax.ShapeDtypeStruct((1, 4), F4),
        ],
        in_specs=[hbm] * 3,
        out_specs=[hbm] * 2 + [vm] * 6,
        scratch_shapes=[
            pltpu.VMEM((32, 512), F4), pltpu.VMEM(node.shape, BF), pltpu.VMEM(edge.shape, BF),
            pltpu.SemaphoreType.DMA((7,)), pltpu.SemaphoreType.DMA((6,)),
        ],
        compiler_params=pltpu.CompilerParams(vmem_limit_bytes=56 << 20),
        name="finish",
    )(node, edge, fin)


def body(
    node_latent, edge_latent, node_cot, edge_src, edge_dst, edge_count, send_index,
    w_edge_in, w_edge_out, w_node_in, w_node_out, gain_edge, gain_node,
):
    micro = node_latent.shape[0]
    factor = float(micro * lax.axis_size("rep") * NODES_DEV * lax.axis_size("dom")) ** (-0.5)
    node, edge, fin = layer_call(
        (
            edge_src, edge_dst, send_index, edge_count, node_latent, edge_latent, node_cot,
            w_edge_in, w_edge_out, w_node_in, w_node_out, gain_edge, gain_node,
        ),
        factor,
    )
    node, edge, ein, *rest = finish_call(node, edge, fin)
    return (node, edge, jnp.swapaxes(ein, 0, 1), *rest)


def solution(mesh):
    placed = (
        P("rep", "dom", None),
        P("rep", "dom", None),
        P("rep", "dom", None),
        P("dom"),
        P("dom"),
        P("dom"),
        P("dom", None, None),
        P("segment", None, None),
        P("segment", None, None),
        P("segment", None, None),
        P("segment", None, None),
        P("segment", None),
        P("segment", None),
    )
    return jax.shard_map(
        body,
        mesh=mesh,
        in_specs=placed,
        out_specs=(
            P("segment", "rep", "dom", None),
            P("segment", "rep", "dom", None),
            P("segment", ("dom", "rep"), None),
            P("segment", ("dom", "rep"), None),
            P("segment", ("dom", "rep"), None),
            P("segment", ("dom", "rep"), None),
            P("segment", ("dom", "rep")),
            P("segment", ("dom", "rep")),
        ),
        check_vma=False,
    )
```

```python
import functools

import jax
import jax.numpy as jnp
from jax import lax
from jax.experimental import pallas as pl
from jax.experimental.pallas import tpu as pltpu
from jax.sharding import PartitionSpec as P

OFFSETS = (1, -1, 2, -2)
HALO = 16
EPS = 1e-05
MESH = pl.DeviceIdType.MESH
ROWS_A = 48
GAIN = 16
LANES = 384
NODES_DEV = 128
EDGES_DEV = 384
HALOS = 64
TABLE = 192
BLOCK = 128
BF = jnp.bfloat16
F4 = jnp.float32


def mm(a, b):
    return jnp.dot(a, b, preferred_element_type=F4)


def mm_tn(a, b):
    return lax.dot_general(a, b, (((0,), (0,)), ((), ())), preferred_element_type=F4)


def silu_grad(pre):
    sig = jax.nn.sigmoid(pre)
    return sig * (1.0 + pre * (1.0 - sig))


def layer_kernel(
    src_in, dst_in, send_in, count_in, node_in, edge_in, cot_in,
    w_ein_in, w_eout_in, w_nin_in, w_nout_in, gain_e_in, gain_n_in,
    node_out, edge_out, fin_out,
    src_row, dst_row, send_row, count, w_ein, w_eout, w_nin, w_nout, gain_e, gain_n, l_first,
    t_ein, t_eout, t_nin, t_nout, oht, oh, inc, inct, sendt, sendm,
    tab, ein, cn, ce, cn32, halo1, halo2, hs1, hs2, bh,
    sr, pre, mid, tmp, xhat, rstd, enew, agg, pren, midn, tmpn, xhatn, rstdn, hnew,
    doutn, dpren, down, dagg, doute, dpre, gs, gr, de, dh, dge, dgn,
    s_halo1, s_halo2, r_halo, s_fe, r_fe, s_fh, r_fh,
    s_bh, r_bh1, r_bh2, s_be, r_be, s_bo, r_bo,
    l_node, l_edge, l_cot, l_nout, l_eout,
    ga, gb, ta, ua, va, tb, ub, vb, a2, ta2, ua2, va2, b2, tb2, ub2, vb2, ca, ra, cb, rb, fin, gz, zr, zl, hy, ry, hx, rx,
    send_sem, recv_sem, l_fin,
    *, nz, factor,
):
    seg = lax.axis_index("segment")
    dom = lax.axis_index("dom")
    n_dom = lax.axis_size("dom")
    first = seg == 0
    second = seg == 1

    def near(step, segment):
        return {"dom": (dom + step + n_dom) % n_dom, "segment": segment}

    rep = lax.axis_index("rep")
    z = dom // 8
    y = (dom // 2) % 4
    px = rep * 2 + dom % 2

    def at_y(p):
        return {"dom": z * 8 + p * 2 + dom % 2}

    def at_z(p):
        return {"dom": p * 8 + dom % 8}

    def at_x(p):
        return {"dom": (dom // 2) * 2 + p % 2, "rep": p // 2}

    z_peers = [(z + j) % nz for j in range(1, nz)]
    x_peers = [(px + j) % 4 for j in range(1, 4)]
    y_peers = [(y + j) % 4 for j in range(1, 4)]
    greet = [near(step, s) for step in OFFSETS for s in range(2)]
    greet += [at_y(p) for p in y_peers] + [at_x(p) for p in x_peers] + [at_z(p) for p in z_peers]
    greet += [{"segment": 1 - seg}]
    barrier = pltpu.get_barrier_semaphore()
    for device in greet:
        pl.semaphore_signal(barrier, inc=1, device_id=device, device_id_type=MESH)

    def remote(src, dst, send, recv, device):
        return pltpu.make_async_remote_copy(
            src_ref=src, dst_ref=dst, send_sem=send, recv_sem=recv,
            device_id=device, device_id_type=MESH,
        )

    def load_node(k):
        return pltpu.make_async_copy(node_in.at[k], tab.at[k, 0:NODES_DEV], l_node.at[k])

    def load_edge(k):
        return pltpu.make_async_copy(edge_in.at[k], ein.at[k], l_edge.at[k])

    def load_cot(k):
        return pltpu.make_async_copy(cot_in.at[k], cn.at[k], l_cot.at[k])

    def store_node(src, k):
        return pltpu.make_async_copy(src.at[k], node_out.at[k], l_nout.at[k])

    def store_edge(src, k):
        return pltpu.make_async_copy(src.at[k], edge_out.at[k], l_eout.at[k])

    def halo_copy(src, k, j, sems, segment):
        rows = slice(j * HALO, (j + 1) * HALO)
        into = slice(NODES_DEV + j * HALO, NODES_DEV + (j + 1) * HALO)
        return remote(
            src.at[k, rows], tab.at[k, into], sems.at[k, j], r_halo.at[k, j],
            near(OFFSETS[j], segment),
        )

    def back_copy(dst, k, j, recv):
        rows = slice(j * HALO, (j + 1) * HALO)
        return remote(
            bh.at[k, rows], dst.at[k, rows], s_bh.at[k, j], recv.at[k, j],
            near(-OFFSETS[j], 0),
        )

    def sib_e(k):
        return remote(enew.at[k], ein.at[k], s_fe.at[k], r_fe.at[k], {"segment": 1 - seg})

    def sib_h(k):
        return remote(
            hnew.at[k], tab.at[k, 0:NODES_DEV], s_fh.at[k], r_fh.at[k], {"segment": 1 - seg}
        )

    def sib_de(k):
        return remote(de.at[k], ce.at[k], s_be.at[k], r_be.at[k], {"segment": 1 - seg})

    def sib_do(k):
        return remote(down.at[k], cn32.at[k], s_bo.at[k], r_bo.at[k], {"segment": 1 - seg})

    small = [
        pltpu.make_async_copy(u, v, l_first.at[i])
        for i, (u, v) in enumerate(
            [
                (src_in, src_row), (dst_in, dst_row), (send_in, send_row), (count_in, count),
                (gain_e_in, gain_e), (gain_n_in, gain_n),
            ]
        )
    ]
    large = [
        pltpu.make_async_copy(u.at[0], v, l_first.at[6 + i])
        for i, (u, v) in enumerate(
            [(w_ein_in, w_ein), (w_eout_in, w_eout), (w_nin_in, w_nin), (w_nout_in, w_nout)]
        )
    ]
    for c in small:
        c.start()

    @pl.when(first)
    def _():
        for k in range(2):
            load_node(k).start()
            load_edge(k).start()

    @pl.when(second)
    def _():
        for k in range(2):
            load_cot(k).start()

    for c in large:
        c.start()
    for c in small:
        c.wait()
    node = lax.broadcasted_iota(jnp.int32, (NODES_DEV, HALO), 0)
    hots = [jnp.where(node == send_row[0, j : j + 1, :], 1.0, 0.0) for j in range(4)]
    f_send = jnp.concatenate(hots + [jnp.zeros((NODES_DEV, NODES_DEV - HALOS), F4)], axis=1)
    sendt[...] = f_send.astype(BF)
    sendm[...] = f_send.T.astype(BF)

    @pl.when(first)
    def _():
        for k in range(2):
            load_node(k).wait()
            hs1[k] = mm(sendm[0:HALOS], tab[k, 0:NODES_DEV]).astype(BF)

    pl.semaphore_wait(barrier, len(greet))

    @pl.when(first)
    def _():
        for k in range(2):
            for j in range(4):
                halo_copy(hs1, k, j, s_halo1, 0).start()

    live_count = count[0]
    hot_src = lax.broadcasted_iota(jnp.int32, (TABLE, EDGES_DEV), 0) == src_row[...].reshape(1, EDGES_DEV)
    owner = lax.broadcasted_iota(jnp.int32, (NODES_DEV, EDGES_DEV), 0)
    slot = lax.broadcasted_iota(jnp.int32, (NODES_DEV, EDGES_DEV), 1)
    hot_dst = owner == dst_row[...].reshape(1, EDGES_DEV)
    hot_inc = hot_dst & (slot < live_count)
    f_src = jnp.where(hot_src, 1.0, 0.0)
    f_dst = jnp.where(hot_dst, 1.0, 0.0)
    f_inc = jnp.where(hot_inc, 1.0, 0.0)
    oht[0:TABLE] = f_src.astype(BF)
    oht[TABLE:] = f_dst.astype(BF)
    inc[...] = f_inc.astype(BF)
    t_src = f_src.T.astype(BF)
    oh[:, 0:NODES_DEV] = t_src[:, 0:NODES_DEV]
    oh[:, NODES_DEV : 2 * NODES_DEV] = f_dst.T.astype(BF)
    oh[:, 2 * NODES_DEV :] = t_src[:, NODES_DEV:]
    inct[...] = f_inc.T.astype(BF)
    dge[...] = jnp.zeros_like(dge)
    dgn[...] = jnp.zeros_like(dgn)

    @pl.when(second)
    def _():
        ce[...] = jnp.zeros_like(ce)

    for c in large:
        c.wait()

    def mean(v):
        return jnp.sum(v, axis=-1, keepdims=True) * (1.0 / 512.0)

    def norm_block(outer, at, k, x_ref, r_ref):
        center = outer - mean(outer)
        inv = lax.rsqrt(mean(center * center) + EPS)
        hat = center * inv
        x_ref[k, at, :] = hat
        r_ref[k, at, :] = jnp.broadcast_to(inv, (BLOCK, 128))
        return hat

    def norm_back(cot, gain, hat, inv):
        dy = cot * gain
        return inv * (dy - mean(dy) - hat * mean(dy * hat))

    def forward(k):
        @pl.when(first)
        def _():
            load_edge(k).wait()

        @pl.when(second)
        def _():
            sib_e(k).wait_recv()

        pre[k] = mm(ein[k], w_ein[0:512])

        @pl.when(second)
        def _():
            sib_h(k).wait_recv()

        own = tab[k, 0:NODES_DEV]
        sr[0:NODES_DEV] = mm(own, w_ein[512:1024]).astype(BF)
        sr[NODES_DEV : 2 * NODES_DEV] = mm(own, w_ein[1024:1536]).astype(BF)
        pre[k] += mm(oh[:, 0 : 2 * NODES_DEV], sr[0 : 2 * NODES_DEV])
        for j in range(4):
            halo_copy(hs1, k, j, s_halo1, 0).wait_recv()
        sr[2 * NODES_DEV :] = mm(tab[k, NODES_DEV:], w_ein[512:1024]).astype(BF)
        tmp[...] = mm(oh[:, 2 * NODES_DEV :], sr[2 * NODES_DEV :])

        @pl.loop(0, EDGES_DEV // BLOCK, unroll=True)
        def _(i):
            at = pl.ds(pl.multiple_of(i * BLOCK, BLOCK), BLOCK)
            v = pre[k, at, :] + tmp[at, :]
            pre[k, at, :] = v
            mid[k, at, :] = (v * jax.nn.sigmoid(v)).astype(BF)

        tmp[...] = mm(mid[k], w_eout[...])

        @pl.loop(0, EDGES_DEV // BLOCK, unroll=True)
        def _(i):
            at = pl.ds(pl.multiple_of(i * BLOCK, BLOCK), BLOCK)
            hat = norm_block(tmp[at, :], at, k, xhat, rstd)
            rows = lax.broadcasted_iota(jnp.int32, (BLOCK, 512), 0) + i * BLOCK
            old = ein[k, at, :].astype(F4)
            enew[k, at, :] = jnp.where(rows < live_count, old + hat * gain_e[...], old).astype(BF)

        @pl.when(first)
        def _():
            sib_e(k).start()

        @pl.when(second)
        def _():
            store_edge(enew, k).start()

        agg[k] = mm(inc[...], enew[k]).astype(BF)
        pren[k] = mm(own, w_nin[0:512]) + mm(agg[k], w_nin[512:1024])

        @pl.loop(0, NODES_DEV // BLOCK, unroll=True)
        def _(i):
            at = pl.ds(pl.multiple_of(i * BLOCK, BLOCK), BLOCK)
            v = pren[k, at, :]
            midn[k, at, :] = (v * jax.nn.sigmoid(v)).astype(BF)

        tmpn[...] = mm(midn[k], w_nout[...])

        @pl.loop(0, NODES_DEV // BLOCK, unroll=True)
        def _(i):
            at = pl.ds(pl.multiple_of(i * BLOCK, BLOCK), BLOCK)
            hat = norm_block(tmpn[at, :], at, k, xhatn, rstdn)
            hnew[k, at, :] = (tab[k, at, :].astype(F4) + hat * gain_n[...]).astype(BF)

        @pl.when(first)
        def _():
            hs2[k] = mm(sendm[0:HALOS], hnew[k]).astype(BF)
            for j in range(4):
                halo_copy(hs2, k, j, s_halo2, 1).start()
            sib_h(k).start()

        @pl.when(second)
        def _():
            store_node(hnew, k).start()

    def backward(k):
        @pl.when(first)
        def _():
            sib_do(k).wait_recv()
            for j in range(4):
                back_copy(halo1, k, j, r_bh1).wait_recv()
            cn[k] = (cn32[k] + mm(sendt[:, 0:HALOS], halo1[k])).astype(BF)

        @pl.when(second)
        def _():
            load_cot(k).wait()

        @pl.loop(0, NODES_DEV // BLOCK, unroll=True)
        def _(i):
            at = pl.ds(pl.multiple_of(i * BLOCK, BLOCK), BLOCK)
            cot = cn[k, at, :].astype(F4)
            hat = xhatn[k, at, :]
            dgn[...] += jnp.sum((cot * hat).reshape(BLOCK // 8, 8, 512), axis=0)
            inv = rstdn[k, at, 0:1]
            doutn[k, at, :] = norm_back(cot, gain_n[...], hat, inv).astype(BF)

        tmpn[...] = mm(doutn[k], t_nout[...])

        @pl.loop(0, NODES_DEV // BLOCK, unroll=True)
        def _(i):
            at = pl.ds(pl.multiple_of(i * BLOCK, BLOCK), BLOCK)
            dpren[k, at, :] = (tmpn[at, :] * silu_grad(pren[k, at, :])).astype(BF)

        dagg[...] = mm(dpren[k], t_nin[:, 512:1024]).astype(BF)

        @pl.when(first)
        def _():
            sib_de(k).wait_recv()

        tmp[...] = mm(inct[...], dagg[...])
        down[k] = cn[k].astype(F4) + mm(dpren[k], t_nin[:, 0:512])

        @pl.loop(0, EDGES_DEV // BLOCK, unroll=True)
        def _(i):
            at = pl.ds(pl.multiple_of(i * BLOCK, BLOCK), BLOCK)
            cot = tmp[at, :] + ce[k, at, :].astype(F4)
            tmp[at, :] = cot
            rows = lax.broadcasted_iota(jnp.int32, (BLOCK, 512), 0) + i * BLOCK
            cot = jnp.where(rows < live_count, cot, 0.0)
            hat = xhat[k, at, :]
            dge[...] += jnp.sum((cot * hat).reshape(BLOCK // 8, 8, 512), axis=0)
            inv = rstd[k, at, 0:1]
            doute[k, at, :] = norm_back(cot, gain_e[...], hat, inv).astype(BF)

        grad = mm(doute[k], t_eout[...])
        pre[k] = grad * silu_grad(pre[k])
        dpre[k] = pre[k].astype(BF)
        gs[k] = mm(oht[0:TABLE], dpre[k]).astype(BF)
        gr[k] = mm(oht[TABLE:], dpre[k]).astype(BF)
        bh[k] = mm(gs[k, NODES_DEV:], t_ein[:, 512:1024]).astype(BF)

        @pl.when(first)
        def _():
            for j in range(4):
                back_copy(halo2, k, j, r_bh2).start()

        @pl.when(second)
        def _():
            for j in range(4):
                back_copy(halo1, k, j, r_bh1).start()

        down[k] += mm(gs[k, 0:NODES_DEV], t_ein[:, 512:1024]) + mm(gr[k], t_ein[:, 1024:1536])

        @pl.when(second)
        def _():
            sib_do(k).start()

        de[k] = (tmp[...] + mm(dpre[k], t_ein[:, 0:512])).astype(BF)

        @pl.when(second)
        def _():
            sib_de(k).start()

        @pl.when(first)
        def _():
            store_edge(de, k).start()

    @pl.loop(0, 4)
    def _(step):
        forward_now = (step == 0) | (step == 1 + seg)
        k = jnp.where(first, step % 2, step // 2)

        @pl.when(step == 2 - 2 * seg)
        def _():
            for m in range(3):
                t_ein[:, m * 512 : m * 512 + 512] = w_ein[m * 512 : m * 512 + 512].T
            for m in range(2):
                t_nin[:, m * 512 : m * 512 + 512] = w_nin[m * 512 : m * 512 + 512].T
            t_eout[...] = w_eout[...].T
            t_nout[...] = w_nout[...].T

        @pl.when(forward_now)
        def _():
            forward(k)

        @pl.when(jnp.logical_not(forward_now))
        def _():
            backward(k)

    def put_ein(base, value):
        for q in range(8):
            r = base + q * 16
            row = (r // 192) * ROWS_A + r % ROWS_A
            ga[(r % 192) // ROWS_A, row : row + 16, :] = value[q * 16 : q * 16 + 16].astype(BF)

    def put_b(m, n_lo, n_hi, e, o):
        for q in range(8):
            part = (n_lo, n_hi)[q // 4][q % 4 * 32 : q % 4 * 32 + 32]
            for p in range(4):
                b = p % 2 * 2 + p // 2
                r = q * 16 + 4 * b
                tile = jnp.concatenate([part[8 * b : 8 * b + 8], e[r : r + 4], o[r : r + 4]], axis=0)
                gb[p, m * 8 + q] = tile[:, 0:LANES].astype(BF)
                gz[2 * m + q // 4, q % 4, p] = tile[:, LANES:].astype(BF)

    def both(ref):
        return ref[...].reshape(ref.shape[0] * ref.shape[1], ref.shape[2])

    def cols(ref, m):
        return jnp.concatenate([ref[0, :, m * 128 : (m + 1) * 128], ref[1, :, m * 128 : (m + 1) * 128]], axis=0)

    def own_cols(m):
        at = slice(m * 128, (m + 1) * 128)
        return jnp.concatenate([tab[0, 0:NODES_DEV, at], tab[1, 0:NODES_DEV, at]], axis=0)

    def copy(n, src, dst, device):
        return remote(src, dst, send_sem.at[n], recv_sem.at[n], device)

    class Ring:
        def __init__(self, base, src, t, u, v, me, at, cut):
            right, left, across = (me + 1) % 4, (me + 3) % 4, (me + 2) % 4
            lo, hi = slice(0, cut), slice(cut, t.shape[0])
            self.out = [
                copy(base, src.at[across, lo], t.at[lo], at(right)),
                copy(base + 1, src.at[across, hi], t.at[hi], at(left)),
                copy(base + 2, src.at[right, hi], u.at[hi], at(right)),
                copy(base + 3, src.at[left, lo], v.at[lo], at(left)),
                copy(base + 4, t.at[lo], u.at[lo], at(right)),
                copy(base + 5, t.at[hi], v.at[hi], at(left)),
            ]
            self.src, self.t, self.u, self.v = src, t, u, v
            self.me, self.right, self.left, self.cut = me, right, left, cut

        def start(self):
            for c in self.out[:4]:
                c.start()

        def middle(self, block):
            src, t, n, cut = self.src, self.t, self.t.shape[0], self.cut
            for c, q, lo, hi in ((0, self.right, 0, cut), (1, self.left, cut, n)):
                self.out[c].wait_recv()

                @pl.loop(lo // block, hi // block)
                def _(i):
                    at = pl.ds(pl.multiple_of(i * block, block), block)
                    t[at] = (t[at].astype(F4) + src[q, at].astype(F4)).astype(BF)

                self.out[4 + c].start()

        def total(self, at):
            own = self.src[self.me, at].astype(F4)
            return own + self.u[at].astype(F4) + self.v[at].astype(F4)

        def arrive(self):
            for c in self.out[2:]:
                c.wait_recv()

    ring_a = Ring(0, ga, ta, ua, va, y, at_y, 208)
    ring_b = Ring(6, gb, tb, ub, vb, px, at_x, 2 * nz)
    ring_a2 = Ring(12, a2, ta2, ua2, va2, px, at_x, nz // 2)
    ring_b2 = Ring(18, b2, tb2, ub2, vb2, y, at_y, nz // 2)

    def nin_part(m):
        lhs = own_cols(m) if m < 4 else cols(agg, m - 4)
        return mm_tn(lhs, both(dpren))

    for m in range(4):
        put_b(
            m, nin_part(2 * m), nin_part(2 * m + 1),
            mm_tn(cols(mid, m), both(doute)), mm_tn(cols(midn, m), both(doutn)),
        )
    ring_b.start()
    zc = 24 + 2 * (nz - 1)
    up, low = at_z((z + 1) % nz), at_z((z + nz - 1) % nz)
    flow_up = [copy(zc, gz.at[(z + 4) % nz], zr.at[0], up)]
    flow_up += [copy(zc + 1 + i, zr.at[i], zr.at[i + 1], up) for i in range(3)]
    flow_low = [copy(zc + 4, gz.at[(z + nz - 3) % nz], zl.at[0], low)]
    flow_low += [copy(zc + 5 + i, zl.at[i], zl.at[i + 1], low) for i in range(2)]
    flow_up[0].start()
    flow_low[0].start()

    def pass_on(i):
        for flow, held, q in ((flow_up, zr, z + 3 - i), (flow_low, zl, z + nz - 2 + i)):
            if i + 1 < len(flow):
                flow[i].wait_recv()
                for r in range(4):
                    part = held[i, r].astype(F4) + gz[q % nz, r].astype(F4)
                    held[i, r] = part.astype(BF)
                flow[i + 1].start()

    for m in range(4):
        base = m * 128
        put_ein(base, mm_tn(cols(ein, m), both(dpre)))
        put_ein(512 + base, mm_tn(cols(tab, m), both(gs)))
        put_ein(1024 + base, mm_tn(own_cols(m), both(gr)))
    row = lax.broadcasted_iota(jnp.int32, (GAIN, 512), 0)
    sum_e = jnp.sum(dge[...], axis=0, keepdims=True)
    sum_n = jnp.sum(dgn[...], axis=0, keepdims=True)
    gains = jnp.where(row == 0, sum_e, jnp.where(row == 1, sum_n, 0.0)).astype(BF)
    for q in range(4):
        ga[q, EDGES_DEV:, :] = gains
    ring_a.start()

    @pl.when(first)
    def _():
        for k in range(2):
            for j in range(4):
                back_copy(halo2, k, j, r_bh2).wait_recv()
            dh[k] = (down[k] + mm(sendt[:, 0:HALOS], halo2[k])).astype(BF)
            store_node(dh, k).start()

    pass_on(0)
    pass_on(1)
    pass_on(2)
    ring_a.middle(16)
    ring_b.middle(2)
    flow_up[3].wait_recv()
    flow_low[2].wait_recv()
    for r in range(4):
        part = gz[z, r].astype(F4) + zr[3, r].astype(F4) + zl[2, r].astype(F4)
        hy[r] = part.astype(BF)
    flow_y = [copy(zc + 7 + j, hy.at[p], ry.at[j], at_y(p)) for j, p in enumerate(y_peers)]
    for c in flow_y:
        c.start()
    ring_a.arrive()
    gains = ring_a.total(slice(nz * ROWS_A, nz * ROWS_A + GAIN))[0:4]

    @pl.loop(0, nz)
    def _(i):
        at = pl.ds(pl.multiple_of(i * ROWS_A, 16), ROWS_A)
        total = ring_a.total(at)
        for p in range(4):
            b = p % 2 * 2 + p // 2
            tile = jnp.concatenate([total[12 * b : 12 * b + 12], gains], axis=0)
            a2[p, i] = tile.astype(BF)

    ring_a2.start()
    ring_b.arrive()

    @pl.loop(0, nz)
    def _(i):
        for q in range(4):
            b2[q, i] = ring_b.total(i * 4 + q).astype(BF)

    ring_b2.start()
    part = hy[y].astype(F4)
    for j, c in enumerate(flow_y):
        c.wait_recv()
        part = part + ry[j].astype(F4)
    hx[...] = part.astype(BF)
    flow_x = [copy(zc + 10 + j, hx.at[p], rx.at[j], at_x(p)) for j, p in enumerate(x_peers)]
    for c in flow_x:
        c.start()
    ring_a2.middle(2)
    ring_b2.middle(2)

    def along_z(base, ring, held, got):
        ring.arrive()
        for i in range(nz):
            held[i] = ring.total(i).astype(BF)
        moves = [copy(base + j, held.at[p], got.at[j], at_z(p)) for j, p in enumerate(z_peers)]
        for c in moves:
            c.start()
        return moves

    def z_total(moves, held, got):
        total = held[z].astype(F4)
        for j, c in enumerate(moves):
            c.wait_recv()
            total = total + got[j].astype(F4)
        return total * factor

    third_a = along_z(24, ring_a2, ca, ra)
    third_b = along_z(24 + nz - 1, ring_b2, cb, rb)
    part = hx[px].astype(F4)
    for j, c in enumerate(flow_x):
        c.wait_recv()
        part = part + rx[j].astype(F4)
    fin[16:32, LANES:] = part * factor
    fin[0:16] = z_total(third_a, ca, ra)
    fin[16:32, 0:LANES] = z_total(third_b, cb, rb)
    result = pltpu.make_async_copy(fin, fin_out, l_fin.at[0])
    result.start()
    result.wait()
    for c in ring_a.out + ring_b.out + ring_a2.out + ring_b2.out + third_a + third_b + flow_up + flow_low + flow_y + flow_x:
        c.wait_send()

    @pl.when(first)
    def _():
        for k in range(2):
            sib_e(k).wait_send()
            sib_h(k).wait_send()
            for j in range(4):
                halo_copy(hs1, k, j, s_halo1, 0).wait_send()
                halo_copy(hs2, k, j, s_halo2, 1).wait_send()
                back_copy(halo2, k, j, r_bh2).wait_send()
            store_edge(de, k).wait()
            store_node(dh, k).wait()

    @pl.when(second)
    def _():
        for k in range(2):
            sib_do(k).wait_send()
            sib_de(k).wait_send()
            for j in range(4):
                back_copy(halo1, k, j, r_bh1).wait_send()
            store_edge(enew, k).wait()
            store_node(hnew, k).wait()


def layer_call(operands, factor):
    hbm = pl.BlockSpec(memory_space=pl.ANY)
    nz = 8
    i32 = jnp.int32

    def bf(*shape):
        return pltpu.VMEM(shape, BF)

    def fl(*shape):
        return pltpu.VMEM(shape, F4)

    dma = pltpu.SemaphoreType.DMA
    n, e = NODES_DEV, EDGES_DEV
    rows = nz * ROWS_A + GAIN
    copies = 24 + 2 * (nz - 1) + 13
    return pl.pallas_call(
        functools.partial(layer_kernel, nz=nz, factor=factor),
        out_shape=[
            jax.ShapeDtypeStruct((2, n, 512), BF),
            jax.ShapeDtypeStruct((2, e, 512), BF),
            jax.ShapeDtypeStruct((32, 512), F4),
        ],
        in_specs=[hbm] * 13,
        out_specs=[hbm] * 3,
        scratch_shapes=[
            pltpu.VMEM((e,), i32), pltpu.VMEM((e,), i32), pltpu.VMEM((1, 4, HALO), i32), pltpu.SMEM((1,), i32),
            bf(1536, 512), bf(512, 512), bf(1024, 512), bf(512, 512), fl(1, 512), fl(1, 512), dma((10,)),
            bf(512, 1536), bf(512, 512), bf(512, 1024), bf(512, 512),
            bf(320, e), bf(e, 320), bf(n, e), bf(e, n), bf(n, n), bf(n, n),
            bf(2, TABLE, 512), bf(2, e, 512), bf(2, n, 512), bf(2, e, 512), fl(2, n, 512),
            bf(2, HALOS, 512), bf(2, HALOS, 512), bf(2, HALOS, 512), bf(2, HALOS, 512), bf(2, HALOS, 512),
            bf(320, 512), fl(2, e, 512), bf(2, e, 512), fl(e, 512), fl(2, e, 512), fl(2, e, 128),
            bf(2, e, 512), bf(2, n, 512), fl(2, n, 512), bf(2, n, 512), fl(n, 512), fl(2, n, 512),
            fl(2, n, 128), bf(2, n, 512),
            bf(2, n, 512), bf(2, n, 512), fl(2, n, 512), bf(n, 512), bf(2, e, 512), bf(2, e, 512),
            bf(2, TABLE, 512), bf(2, n, 512), bf(2, e, 512), bf(2, n, 512), fl(8, 512), fl(8, 512),
            dma((2, 4)), dma((2, 4)), dma((2, 4)), dma((2,)), dma((2,)), dma((2,)), dma((2,)),
            dma((2, 4)), dma((2, 4)), dma((2, 4)), dma((2,)), dma((2,)), dma((2,)), dma((2,)),
            dma((2,)), dma((2,)), dma((2,)), dma((2,)), dma((2,)),
            bf(4, rows, 512), bf(4, 4 * nz, 16, LANES),
            bf(rows, 512), bf(rows, 512), bf(rows, 512),
            bf(4 * nz, 16, LANES), bf(4 * nz, 16, LANES), bf(4 * nz, 16, LANES),
            bf(4, nz, 16, 512), bf(nz, 16, 512), bf(nz, 16, 512), bf(nz, 16, 512),
            bf(4, nz, 16, LANES), bf(nz, 16, LANES), bf(nz, 16, LANES), bf(nz, 16, LANES),
            bf(nz, 16, 512), bf(nz - 1, 16, 512), bf(nz, 16, LANES), bf(nz - 1, 16, LANES), fl(32, 512),
            bf(nz, 4, 4, 16, 128), bf(4, 4, 4, 16, 128), bf(3, 4, 4, 16, 128),
            bf(4, 4, 16, 128), bf(3, 4, 16, 128), bf(4, 16, 128), bf(3, 16, 128),
            dma((copies,)), dma((copies,)), dma((1,)),
        ],
        compiler_params=pltpu.CompilerParams(
            collective_id=0, has_side_effects=True, vmem_limit_bytes=56 << 20
        ),
        name="layers",
    )(*operands)


def finish_kernel(
    node_in, edge_in, fin_in, node_o, edge_o, ein_o, eout_o, nin_o, nout_o, ge_o, gn_o,
    rfin, node_v, edge_v, sems, out_sems,
):
    first = pltpu.make_async_copy(fin_in, rfin, sems.at[0])
    first.start()
    parts = [(node_in.at[k], node_v.at[k], node_o.at[0, k]) for k in range(2)]
    for k in range(2):
        for q in range(2):
            at = slice(q * 192, q * 192 + 192)
            parts.append((edge_in.at[k, at], edge_v.at[k, at], edge_o.at[0, k, at]))
    moves = [pltpu.make_async_copy(u, v, sems.at[1 + i]) for i, (u, v, _) in enumerate(parts)]
    stores = [pltpu.make_async_copy(v, w, out_sems.at[i]) for i, (_, v, w) in enumerate(parts)]
    for c in moves:
        c.start()
    for c, w in zip(moves, stores):
        c.wait()
        w.start()
    first.wait()
    t = lax.axis_index("dom") * 2 + lax.axis_index("rep")
    for r in range(12):
        ein_o[r] = rfin[r : r + 1]
    nin_o[0] = rfin[16:24]
    eout_o[0] = rfin[24:28]
    nout_o[0] = rfin[28:32]
    pair = rfin[12:14]
    lane = lax.broadcasted_iota(jnp.int32, (2, 512), 1)
    narrow = lax.broadcasted_iota(jnp.int32, (2, 128), 1)
    picked = jnp.zeros((2, 128), F4)
    for i in range(4):
        value = jnp.sum(jnp.where(lane == t * 4 + i, pair, 0.0), axis=1, keepdims=True)
        picked = picked + jnp.where(narrow == i, value, 0.0)
    ge_o[...] = picked[0:1, 0:4]
    gn_o[...] = picked[1:2, 0:4]
    for c in stores:
        c.wait()


def finish_call(node, edge, fin):
    hbm = pl.BlockSpec(memory_space=pl.ANY)
    vm = pl.BlockSpec(memory_space=pltpu.VMEM)
    return pl.pallas_call(
        finish_kernel,
        out_shape=[
            jax.ShapeDtypeStruct((1, *node.shape), BF),
            jax.ShapeDtypeStruct((1, *edge.shape), BF),
            jax.ShapeDtypeStruct((12, 1, 512), F4),
            jax.ShapeDtypeStruct((1, 4, 512), F4),
            jax.ShapeDtypeStruct((1, 8, 512), F4),
            jax.ShapeDtypeStruct((1, 4, 512), F4),
            jax.ShapeDtypeStruct((1, 4), F4),
            jax.ShapeDtypeStruct((1, 4), F4),
        ],
        in_specs=[hbm] * 3,
        out_specs=[hbm] * 2 + [vm] * 6,
        scratch_shapes=[
            pltpu.VMEM((32, 512), F4), pltpu.VMEM(node.shape, BF), pltpu.VMEM(edge.shape, BF),
            pltpu.SemaphoreType.DMA((7,)), pltpu.SemaphoreType.DMA((6,)),
        ],
        compiler_params=pltpu.CompilerParams(vmem_limit_bytes=56 << 20),
        name="finish",
    )(node, edge, fin)


def body(
    node_latent, edge_latent, node_cot, edge_src, edge_dst, edge_count, send_index,
    w_edge_in, w_edge_out, w_node_in, w_node_out, gain_edge, gain_node,
):
    micro = node_latent.shape[0]
    factor = float(micro * lax.axis_size("rep") * NODES_DEV * lax.axis_size("dom")) ** (-0.5)
    node, edge, fin = layer_call(
        (
            edge_src, edge_dst, send_index, edge_count, node_latent, edge_latent, node_cot,
            w_edge_in, w_edge_out, w_node_in, w_node_out, gain_edge, gain_node,
        ),
        factor,
    )
    node, edge, ein, *rest = finish_call(node, edge, fin)
    return (node, edge, jnp.swapaxes(ein, 0, 1), *rest)


def solution(mesh):
    placed = (
        P("rep", "dom", None),
        P("rep", "dom", None),
        P("rep", "dom", None),
        P("dom"),
        P("dom"),
        P("dom"),
        P("dom", None, None),
        P("segment", None, None),
        P("segment", None, None),
        P("segment", None, None),
        P("segment", None, None),
        P("segment", None),
        P("segment", None),
    )
    return jax.shard_map(
        body,
        mesh=mesh,
        in_specs=placed,
        out_specs=(
            P("segment", "rep", "dom", None),
            P("segment", "rep", "dom", None),
            P("segment", ("dom", "rep"), None),
            P("segment", ("dom", "rep"), None),
            P("segment", ("dom", "rep"), None),
            P("segment", ("dom", "rep"), None),
            P("segment", ("dom", "rep")),
            P("segment", ("dom", "rep")),
        ),
        check_vma=False,
    )
```

```python
import functools

import jax
import jax.numpy as jnp
from jax import lax
from jax.experimental import pallas as pl
from jax.experimental.pallas import tpu as pltpu
from jax.sharding import PartitionSpec as P

OFFSETS = (1, -1, 2, -2)
HALO = 16
EPS = 1e-05
MESH = pl.DeviceIdType.MESH
ROWS_A = 48
GAIN = 16
LANES = 384
NODES_DEV = 128
EDGES_DEV = 384
HALOS = 64
TABLE = 192
BLOCK = 128
BF = jnp.bfloat16
F4 = jnp.float32


def mm(a, b):
    return jnp.dot(a, b, preferred_element_type=F4)


def mm_tn(a, b):
    return lax.dot_general(a, b, (((0,), (0,)), ((), ())), preferred_element_type=F4)


def silu_grad(pre):
    sig = jax.nn.sigmoid(pre)
    return sig * (1.0 + pre * (1.0 - sig))


def layer_kernel(
    src_in, dst_in, send_in, count_in, node_in, edge_in, cot_in,
    w_ein_in, w_eout_in, w_nin_in, w_nout_in, gain_e_in, gain_n_in,
    node_out, edge_out, fin_out,
    src_row, dst_row, send_row, count, w_ein, w_eout, w_nin, w_nout, gain_e, gain_n, l_first,
    t_ein, t_eout, t_nin, t_nout, oht, oh, inc, inct, sendt, sendm,
    tab, ein, cn, ce, cn32, halo1, halo2, hs1, hs2, bh,
    sr, pre, mid, tmp, xhat, rstd, enew, agg, pren, midn, tmpn, xhatn, rstdn, hnew,
    doutn, dpren, down, dagg, doute, dpre, gs, gr, de, dh, dge, dgn,
    s_halo1, s_halo2, r_halo, s_fe, r_fe, s_fh, r_fh,
    s_bh, r_bh1, r_bh2, s_be, r_be, s_bo, r_bo,
    l_node, l_edge, l_cot, l_nout, l_eout,
    ga, gb, ta, ua, va, tb, ub, vb, a2, ga2, b2, gb2, ca, ra, cb, rb, fin, gz, zr, zl, hy, ry, hx, rx,
    send_sem, recv_sem, l_fin,
    *, nz, factor,
):
    seg = lax.axis_index("segment")
    dom = lax.axis_index("dom")
    n_dom = lax.axis_size("dom")
    first = seg == 0
    second = seg == 1

    def near(step, segment):
        return {"dom": (dom + step + n_dom) % n_dom, "segment": segment}

    rep = lax.axis_index("rep")
    z = dom // 8
    y = (dom // 2) % 4
    px = rep * 2 + dom % 2

    def at_y(p):
        return {"dom": z * 8 + p * 2 + dom % 2}

    def at_z(p):
        return {"dom": p * 8 + dom % 8}

    def at_x(p):
        return {"dom": (dom // 2) * 2 + p % 2, "rep": p // 2}

    z_peers = [(z + j) % nz for j in range(1, nz)]
    x_peers = [(px + j) % 4 for j in range(1, 4)]
    y_peers = [(y + j) % 4 for j in range(1, 4)]
    greet = [near(step, s) for step in OFFSETS for s in range(2)]
    greet += [at_y(p) for p in y_peers] + [at_x(p) for p in x_peers] + [at_z(p) for p in z_peers]
    greet += [{"segment": 1 - seg}]
    barrier = pltpu.get_barrier_semaphore()
    for device in greet:
        pl.semaphore_signal(barrier, inc=1, device_id=device, device_id_type=MESH)

    def remote(src, dst, send, recv, device):
        return pltpu.make_async_remote_copy(
            src_ref=src, dst_ref=dst, send_sem=send, recv_sem=recv,
            device_id=device, device_id_type=MESH,
        )

    def load_node(k):
        return pltpu.make_async_copy(node_in.at[k], tab.at[k, 0:NODES_DEV], l_node.at[k])

    def load_edge(k):
        return pltpu.make_async_copy(edge_in.at[k], ein.at[k], l_edge.at[k])

    def load_cot(k):
        return pltpu.make_async_copy(cot_in.at[k], cn.at[k], l_cot.at[k])

    def store_node(src, k):
        return pltpu.make_async_copy(src.at[k], node_out.at[k], l_nout.at[k])

    def store_edge(src, k):
        return pltpu.make_async_copy(src.at[k], edge_out.at[k], l_eout.at[k])

    def halo_copy(src, k, j, sems, segment):
        rows = slice(j * HALO, (j + 1) * HALO)
        into = slice(NODES_DEV + j * HALO, NODES_DEV + (j + 1) * HALO)
        return remote(
            src.at[k, rows], tab.at[k, into], sems.at[k, j], r_halo.at[k, j],
            near(OFFSETS[j], segment),
        )

    def back_copy(dst, k, j, recv):
        rows = slice(j * HALO, (j + 1) * HALO)
        return remote(
            bh.at[k, rows], dst.at[k, rows], s_bh.at[k, j], recv.at[k, j],
            near(-OFFSETS[j], 0),
        )

    def sib_e(k):
        return remote(enew.at[k], ein.at[k], s_fe.at[k], r_fe.at[k], {"segment": 1 - seg})

    def sib_h(k):
        return remote(
            hnew.at[k], tab.at[k, 0:NODES_DEV], s_fh.at[k], r_fh.at[k], {"segment": 1 - seg}
        )

    def sib_de(k):
        return remote(de.at[k], ce.at[k], s_be.at[k], r_be.at[k], {"segment": 1 - seg})

    def sib_do(k):
        return remote(down.at[k], cn32.at[k], s_bo.at[k], r_bo.at[k], {"segment": 1 - seg})

    small = [
        pltpu.make_async_copy(u, v, l_first.at[i])
        for i, (u, v) in enumerate(
            [
                (src_in, src_row), (dst_in, dst_row), (send_in, send_row), (count_in, count),
                (gain_e_in, gain_e), (gain_n_in, gain_n),
            ]
        )
    ]
    large = [
        pltpu.make_async_copy(u.at[0], v, l_first.at[6 + i])
        for i, (u, v) in enumerate(
            [(w_ein_in, w_ein), (w_eout_in, w_eout), (w_nin_in, w_nin), (w_nout_in, w_nout)]
        )
    ]
    for c in small:
        c.start()

    @pl.when(first)
    def _():
        for k in range(2):
            load_node(k).start()
            load_edge(k).start()

    @pl.when(second)
    def _():
        for k in range(2):
            load_cot(k).start()

    for c in large:
        c.start()
    for c in small:
        c.wait()
    node = lax.broadcasted_iota(jnp.int32, (NODES_DEV, HALO), 0)
    hots = [jnp.where(node == send_row[0, j : j + 1, :], 1.0, 0.0) for j in range(4)]
    f_send = jnp.concatenate(hots + [jnp.zeros((NODES_DEV, NODES_DEV - HALOS), F4)], axis=1)
    sendt[...] = f_send.astype(BF)
    sendm[...] = f_send.T.astype(BF)

    @pl.when(first)
    def _():
        for k in range(2):
            load_node(k).wait()
            hs1[k] = mm(sendm[0:HALOS], tab[k, 0:NODES_DEV]).astype(BF)

    pl.semaphore_wait(barrier, len(greet))

    @pl.when(first)
    def _():
        for k in range(2):
            for j in range(4):
                halo_copy(hs1, k, j, s_halo1, 0).start()

    live_count = count[0]
    hot_src = lax.broadcasted_iota(jnp.int32, (TABLE, EDGES_DEV), 0) == src_row[...].reshape(1, EDGES_DEV)
    owner = lax.broadcasted_iota(jnp.int32, (NODES_DEV, EDGES_DEV), 0)
    slot = lax.broadcasted_iota(jnp.int32, (NODES_DEV, EDGES_DEV), 1)
    hot_dst = owner == dst_row[...].reshape(1, EDGES_DEV)
    hot_inc = hot_dst & (slot < live_count)
    f_src = jnp.where(hot_src, 1.0, 0.0)
    f_dst = jnp.where(hot_dst, 1.0, 0.0)
    f_inc = jnp.where(hot_inc, 1.0, 0.0)
    oht[0:TABLE] = f_src.astype(BF)
    oht[TABLE:] = f_dst.astype(BF)
    inc[...] = f_inc.astype(BF)
    t_src = f_src.T.astype(BF)
    oh[:, 0:NODES_DEV] = t_src[:, 0:NODES_DEV]
    oh[:, NODES_DEV : 2 * NODES_DEV] = f_dst.T.astype(BF)
    oh[:, 2 * NODES_DEV :] = t_src[:, NODES_DEV:]
    inct[...] = f_inc.T.astype(BF)
    dge[...] = jnp.zeros_like(dge)
    dgn[...] = jnp.zeros_like(dgn)

    @pl.when(second)
    def _():
        ce[...] = jnp.zeros_like(ce)

    for c in large:
        c.wait()

    def mean(v):
        return jnp.sum(v, axis=-1, keepdims=True) * (1.0 / 512.0)

    def norm_block(outer, at, k, x_ref, r_ref):
        center = outer - mean(outer)
        inv = lax.rsqrt(mean(center * center) + EPS)
        hat = center * inv
        x_ref[k, at, :] = hat
        r_ref[k, at, :] = jnp.broadcast_to(inv, (BLOCK, 128))
        return hat

    def norm_back(cot, gain, hat, inv):
        dy = cot * gain
        return inv * (dy - mean(dy) - hat * mean(dy * hat))

    def forward(k):
        @pl.when(first)
        def _():
            load_edge(k).wait()

        @pl.when(second)
        def _():
            sib_e(k).wait_recv()

        pre[k] = mm(ein[k], w_ein[0:512])

        @pl.when(second)
        def _():
            sib_h(k).wait_recv()

        own = tab[k, 0:NODES_DEV]
        sr[0:NODES_DEV] = mm(own, w_ein[512:1024]).astype(BF)
        sr[NODES_DEV : 2 * NODES_DEV] = mm(own, w_ein[1024:1536]).astype(BF)
        pre[k] += mm(oh[:, 0 : 2 * NODES_DEV], sr[0 : 2 * NODES_DEV])
        for j in range(4):
            halo_copy(hs1, k, j, s_halo1, 0).wait_recv()
        sr[2 * NODES_DEV :] = mm(tab[k, NODES_DEV:], w_ein[512:1024]).astype(BF)
        tmp[...] = mm(oh[:, 2 * NODES_DEV :], sr[2 * NODES_DEV :])

        @pl.loop(0, EDGES_DEV // BLOCK, unroll=True)
        def _(i):
            at = pl.ds(pl.multiple_of(i * BLOCK, BLOCK), BLOCK)
            v = pre[k, at, :] + tmp[at, :]
            pre[k, at, :] = v
            mid[k, at, :] = (v * jax.nn.sigmoid(v)).astype(BF)

        tmp[...] = mm(mid[k], w_eout[...])

        @pl.loop(0, EDGES_DEV // BLOCK, unroll=True)
        def _(i):
            at = pl.ds(pl.multiple_of(i * BLOCK, BLOCK), BLOCK)
            hat = norm_block(tmp[at, :], at, k, xhat, rstd)
            rows = lax.broadcasted_iota(jnp.int32, (BLOCK, 512), 0) + i * BLOCK
            old = ein[k, at, :].astype(F4)
            enew[k, at, :] = jnp.where(rows < live_count, old + hat * gain_e[...], old).astype(BF)

        @pl.when(first)
        def _():
            sib_e(k).start()

        @pl.when(second)
        def _():
            store_edge(enew, k).start()

        agg[k] = mm(inc[...], enew[k]).astype(BF)
        pren[k] = mm(own, w_nin[0:512]) + mm(agg[k], w_nin[512:1024])

        @pl.loop(0, NODES_DEV // BLOCK, unroll=True)
        def _(i):
            at = pl.ds(pl.multiple_of(i * BLOCK, BLOCK), BLOCK)
            v = pren[k, at, :]
            midn[k, at, :] = (v * jax.nn.sigmoid(v)).astype(BF)

        tmpn[...] = mm(midn[k], w_nout[...])

        @pl.loop(0, NODES_DEV // BLOCK, unroll=True)
        def _(i):
            at = pl.ds(pl.multiple_of(i * BLOCK, BLOCK), BLOCK)
            hat = norm_block(tmpn[at, :], at, k, xhatn, rstdn)
            hnew[k, at, :] = (tab[k, at, :].astype(F4) + hat * gain_n[...]).astype(BF)

        @pl.when(first)
        def _():
            hs2[k] = mm(sendm[0:HALOS], hnew[k]).astype(BF)
            for j in range(4):
                halo_copy(hs2, k, j, s_halo2, 1).start()
            sib_h(k).start()

        @pl.when(second)
        def _():
            store_node(hnew, k).start()

    def backward(k):
        @pl.when(first)
        def _():
            sib_do(k).wait_recv()
            for j in range(4):
                back_copy(halo1, k, j, r_bh1).wait_recv()
            cn[k] = (cn32[k] + mm(sendt[:, 0:HALOS], halo1[k])).astype(BF)

        @pl.when(second)
        def _():
            load_cot(k).wait()

        @pl.loop(0, NODES_DEV // BLOCK, unroll=True)
        def _(i):
            at = pl.ds(pl.multiple_of(i * BLOCK, BLOCK), BLOCK)
            cot = cn[k, at, :].astype(F4)
            hat = xhatn[k, at, :]
            dgn[...] += jnp.sum((cot * hat).reshape(BLOCK // 8, 8, 512), axis=0)
            inv = rstdn[k, at, 0:1]
            doutn[k, at, :] = norm_back(cot, gain_n[...], hat, inv).astype(BF)

        tmpn[...] = mm(doutn[k], t_nout[...])

        @pl.loop(0, NODES_DEV // BLOCK, unroll=True)
        def _(i):
            at = pl.ds(pl.multiple_of(i * BLOCK, BLOCK), BLOCK)
            dpren[k, at, :] = (tmpn[at, :] * silu_grad(pren[k, at, :])).astype(BF)

        dagg[...] = mm(dpren[k], t_nin[:, 512:1024]).astype(BF)

        @pl.when(first)
        def _():
            sib_de(k).wait_recv()

        tmp[...] = mm(inct[...], dagg[...])
        down[k] = cn[k].astype(F4) + mm(dpren[k], t_nin[:, 0:512])

        @pl.loop(0, EDGES_DEV // BLOCK, unroll=True)
        def _(i):
            at = pl.ds(pl.multiple_of(i * BLOCK, BLOCK), BLOCK)
            cot = tmp[at, :] + ce[k, at, :].astype(F4)
            tmp[at, :] = cot
            rows = lax.broadcasted_iota(jnp.int32, (BLOCK, 512), 0) + i * BLOCK
            cot = jnp.where(rows < live_count, cot, 0.0)
            hat = xhat[k, at, :]
            dge[...] += jnp.sum((cot * hat).reshape(BLOCK // 8, 8, 512), axis=0)
            inv = rstd[k, at, 0:1]
            doute[k, at, :] = norm_back(cot, gain_e[...], hat, inv).astype(BF)

        grad = mm(doute[k], t_eout[...])
        pre[k] = grad * silu_grad(pre[k])
        dpre[k] = pre[k].astype(BF)
        gs[k] = mm(oht[0:TABLE], dpre[k]).astype(BF)
        gr[k] = mm(oht[TABLE:], dpre[k]).astype(BF)
        bh[k] = mm(gs[k, NODES_DEV:], t_ein[:, 512:1024]).astype(BF)

        @pl.when(first)
        def _():
            for j in range(4):
                back_copy(halo2, k, j, r_bh2).start()

        @pl.when(second)
        def _():
            for j in range(4):
                back_copy(halo1, k, j, r_bh1).start()

        down[k] += mm(gs[k, 0:NODES_DEV], t_ein[:, 512:1024]) + mm(gr[k], t_ein[:, 1024:1536])

        @pl.when(second)
        def _():
            sib_do(k).start()

        de[k] = (tmp[...] + mm(dpre[k], t_ein[:, 0:512])).astype(BF)

        @pl.when(second)
        def _():
            sib_de(k).start()

        @pl.when(first)
        def _():
            store_edge(de, k).start()

    @pl.loop(0, 4)
    def _(step):
        forward_now = (step == 0) | (step == 1 + seg)
        k = jnp.where(first, step % 2, step // 2)

        @pl.when(step == 2 - 2 * seg)
        def _():
            for m in range(3):
                t_ein[:, m * 512 : m * 512 + 512] = w_ein[m * 512 : m * 512 + 512].T
            for m in range(2):
                t_nin[:, m * 512 : m * 512 + 512] = w_nin[m * 512 : m * 512 + 512].T
            t_eout[...] = w_eout[...].T
            t_nout[...] = w_nout[...].T

        @pl.when(forward_now)
        def _():
            forward(k)

        @pl.when(jnp.logical_not(forward_now))
        def _():
            backward(k)

    def put_ein(base, value):
        for q in range(8):
            r = base + q * 16
            row = (r // 192) * ROWS_A + r % ROWS_A
            ga[(r % 192) // ROWS_A, row : row + 16, :] = value[q * 16 : q * 16 + 16].astype(BF)

    def put_b(m, n_lo, n_hi, e, o):
        for q in range(8):
            part = (n_lo, n_hi)[q // 4][q % 4 * 32 : q % 4 * 32 + 32]
            for p in range(4):
                b = p % 2 * 2 + p // 2
                r = q * 16 + 4 * b
                tile = jnp.concatenate([part[8 * b : 8 * b + 8], e[r : r + 4], o[r : r + 4]], axis=0)
                gb[p, m * 8 + q] = tile[:, 0:LANES].astype(BF)
                gz[2 * m + q // 4, q % 4, p] = tile[:, LANES:].astype(BF)

    def both(ref):
        return ref[...].reshape(ref.shape[0] * ref.shape[1], ref.shape[2])

    def cols(ref, m):
        return jnp.concatenate([ref[0, :, m * 128 : (m + 1) * 128], ref[1, :, m * 128 : (m + 1) * 128]], axis=0)

    def own_cols(m):
        at = slice(m * 128, (m + 1) * 128)
        return jnp.concatenate([tab[0, 0:NODES_DEV, at], tab[1, 0:NODES_DEV, at]], axis=0)

    def copy(n, src, dst, device):
        return remote(src, dst, send_sem.at[n], recv_sem.at[n], device)

    class Ring:
        def __init__(self, base, src, t, u, v, me, at, cut):
            right, left, across = (me + 1) % 4, (me + 3) % 4, (me + 2) % 4
            lo, hi = slice(0, cut), slice(cut, t.shape[0])
            self.out = [
                copy(base, src.at[across, lo], t.at[lo], at(right)),
                copy(base + 1, src.at[across, hi], t.at[hi], at(left)),
                copy(base + 2, src.at[right, hi], u.at[hi], at(right)),
                copy(base + 3, src.at[left, lo], v.at[lo], at(left)),
                copy(base + 4, t.at[lo], u.at[lo], at(right)),
                copy(base + 5, t.at[hi], v.at[hi], at(left)),
            ]
            self.src, self.t, self.u, self.v = src, t, u, v
            self.me, self.right, self.left, self.cut = me, right, left, cut

        def start(self):
            for c in self.out[:4]:
                c.start()

        def middle(self, block):
            src, t, n, cut = self.src, self.t, self.t.shape[0], self.cut
            for c, q, lo, hi in ((0, self.right, 0, cut), (1, self.left, cut, n)):
                self.out[c].wait_recv()

                @pl.loop(lo // block, hi // block, unroll=4 if (hi - lo) // block % 4 == 0 else 1)
                def _(i):
                    at = pl.ds(pl.multiple_of(i * block, block), block)
                    t[at] = (t[at].astype(F4) + src[q, at].astype(F4)).astype(BF)

                self.out[4 + c].start()

        def total(self, at):
            own = self.src[self.me, at].astype(F4)
            return own + self.u[at].astype(F4) + self.v[at].astype(F4)

        def arrive(self):
            for c in self.out[2:]:
                c.wait_recv()

    ring_a = Ring(0, ga, ta, ua, va, y, at_y, 208)
    ring_b = Ring(6, gb, tb, ub, vb, px, at_x, 2 * nz)
    def spread(base, src, got, peers, at):
        moves = [copy(base + j, src.at[p], got.at[j], at(p)) for j, p in enumerate(peers)]
        for c in moves:
            c.start()
        return moves

    def nin_part(m):
        lhs = own_cols(m) if m < 4 else cols(agg, m - 4)
        return mm_tn(lhs, both(dpren))

    for m in range(4):
        put_b(
            m, nin_part(2 * m), nin_part(2 * m + 1),
            mm_tn(cols(mid, m), both(doute)), mm_tn(cols(midn, m), both(doutn)),
        )
    ring_b.start()
    zc = 24 + 2 * (nz - 1)
    up, low = at_z((z + 1) % nz), at_z((z + nz - 1) % nz)
    flow_up = [copy(zc, gz.at[(z + 4) % nz], zr.at[0], up)]
    flow_up += [copy(zc + 1 + i, zr.at[i], zr.at[i + 1], up) for i in range(3)]
    flow_low = [copy(zc + 4, gz.at[(z + nz - 3) % nz], zl.at[0], low)]
    flow_low += [copy(zc + 5 + i, zl.at[i], zl.at[i + 1], low) for i in range(2)]
    flow_up[0].start()
    flow_low[0].start()

    def pass_on(i):
        for flow, held, q in ((flow_up, zr, z + 3 - i), (flow_low, zl, z + nz - 2 + i)):
            if i + 1 < len(flow):
                flow[i].wait_recv()
                for r in range(4):
                    part = held[i, r].astype(F4) + gz[q % nz, r].astype(F4)
                    held[i, r] = part.astype(BF)
                flow[i + 1].start()

    for m in range(4):
        base = m * 128
        put_ein(base, mm_tn(cols(ein, m), both(dpre)))
        put_ein(512 + base, mm_tn(cols(tab, m), both(gs)))
        put_ein(1024 + base, mm_tn(own_cols(m), both(gr)))
    row = lax.broadcasted_iota(jnp.int32, (GAIN, 512), 0)
    sum_e = jnp.sum(dge[...], axis=0, keepdims=True)
    sum_n = jnp.sum(dgn[...], axis=0, keepdims=True)
    gains = jnp.where(row == 0, sum_e, jnp.where(row == 1, sum_n, 0.0)).astype(BF)
    for q in range(4):
        ga[q, EDGES_DEV:, :] = gains
    ring_a.start()

    @pl.when(first)
    def _():
        for k in range(2):
            for j in range(4):
                back_copy(halo2, k, j, r_bh2).wait_recv()
            dh[k] = (down[k] + mm(sendt[:, 0:HALOS], halo2[k])).astype(BF)
            store_node(dh, k).start()

    pass_on(0)
    pass_on(1)
    ring_b.middle(2)
    ring_a.middle(16)
    pass_on(2)
    flow_up[3].wait_recv()
    flow_low[2].wait_recv()
    for r in range(4):
        part = gz[z, r].astype(F4) + zr[3, r].astype(F4) + zl[2, r].astype(F4)
        hy[r] = part.astype(BF)
    flow_y = spread(zc + 7, hy, ry, y_peers, at_y)
    ring_a.arrive()
    gains = ring_a.total(slice(nz * ROWS_A, nz * ROWS_A + GAIN))[0:4]

    @pl.loop(0, nz, unroll=4)
    def _(i):
        at = pl.ds(pl.multiple_of(i * ROWS_A, 16), ROWS_A)
        total = ring_a.total(at)
        for p in range(4):
            b = p % 2 * 2 + p // 2
            tile = jnp.concatenate([total[12 * b : 12 * b + 12], gains], axis=0)
            a2[p, i] = tile.astype(BF)

    second_a = spread(12, a2, ga2, x_peers, at_x)
    ring_b.arrive()

    @pl.loop(0, nz, unroll=4)
    def _(i):
        for q in range(4):
            b2[q, i] = ring_b.total(i * 4 + q).astype(BF)

    second_b = spread(15, b2, gb2, y_peers, at_y)
    part = hy[y].astype(F4)
    for j, c in enumerate(flow_y):
        c.wait_recv()
        part = part + ry[j].astype(F4)
    hx[...] = part.astype(BF)
    flow_x = spread(zc + 10, hx, rx, x_peers, at_x)

    def along_z(base, moves, src, got, me, held, into):
        for c in moves:
            c.wait_recv()
        for i in range(nz):
            total = src[me, i].astype(F4)
            for j in range(3):
                total = total + got[j, i].astype(F4)
            held[i] = total.astype(BF)
        return spread(base, held, into, z_peers, at_z)

    def z_total(moves, held, got):
        total = held[z].astype(F4)
        for j, c in enumerate(moves):
            c.wait_recv()
            total = total + got[j].astype(F4)
        return total * factor

    third_a = along_z(24, second_a, a2, ga2, px, ca, ra)
    third_b = along_z(24 + nz - 1, second_b, b2, gb2, y, cb, rb)
    part = hx[px].astype(F4)
    for j, c in enumerate(flow_x):
        c.wait_recv()
        part = part + rx[j].astype(F4)
    fin[16:32, LANES:] = part * factor
    fin[0:16] = z_total(third_a, ca, ra)
    fin[16:32, 0:LANES] = z_total(third_b, cb, rb)
    result = pltpu.make_async_copy(fin, fin_out, l_fin.at[0])
    result.start()
    result.wait()
    for c in ring_a.out + ring_b.out + second_a + second_b + third_a + third_b + flow_up + flow_low + flow_y + flow_x:
        c.wait_send()

    @pl.when(first)
    def _():
        for k in range(2):
            sib_e(k).wait_send()
            sib_h(k).wait_send()
            for j in range(4):
                halo_copy(hs1, k, j, s_halo1, 0).wait_send()
                halo_copy(hs2, k, j, s_halo2, 1).wait_send()
                back_copy(halo2, k, j, r_bh2).wait_send()
            store_edge(de, k).wait()
            store_node(dh, k).wait()

    @pl.when(second)
    def _():
        for k in range(2):
            sib_do(k).wait_send()
            sib_de(k).wait_send()
            for j in range(4):
                back_copy(halo1, k, j, r_bh1).wait_send()
            store_edge(enew, k).wait()
            store_node(hnew, k).wait()


def layer_call(operands, factor):
    hbm = pl.BlockSpec(memory_space=pl.ANY)
    nz = 8
    i32 = jnp.int32

    def bf(*shape):
        return pltpu.VMEM(shape, BF)

    def fl(*shape):
        return pltpu.VMEM(shape, F4)

    dma = pltpu.SemaphoreType.DMA
    n, e = NODES_DEV, EDGES_DEV
    rows = nz * ROWS_A + GAIN
    copies = 24 + 2 * (nz - 1) + 13
    return pl.pallas_call(
        functools.partial(layer_kernel, nz=nz, factor=factor),
        out_shape=[
            jax.ShapeDtypeStruct((2, n, 512), BF),
            jax.ShapeDtypeStruct((2, e, 512), BF),
            jax.ShapeDtypeStruct((32, 512), F4),
        ],
        in_specs=[hbm] * 13,
        out_specs=[hbm] * 3,
        scratch_shapes=[
            pltpu.VMEM((e,), i32), pltpu.VMEM((e,), i32), pltpu.VMEM((1, 4, HALO), i32), pltpu.SMEM((1,), i32),
            bf(1536, 512), bf(512, 512), bf(1024, 512), bf(512, 512), fl(1, 512), fl(1, 512), dma((10,)),
            bf(512, 1536), bf(512, 512), bf(512, 1024), bf(512, 512),
            bf(320, e), bf(e, 320), bf(n, e), bf(e, n), bf(n, n), bf(n, n),
            bf(2, TABLE, 512), bf(2, e, 512), bf(2, n, 512), bf(2, e, 512), fl(2, n, 512),
            bf(2, HALOS, 512), bf(2, HALOS, 512), bf(2, HALOS, 512), bf(2, HALOS, 512), bf(2, HALOS, 512),
            bf(320, 512), fl(2, e, 512), bf(2, e, 512), fl(e, 512), fl(2, e, 512), fl(2, e, 128),
            bf(2, e, 512), bf(2, n, 512), fl(2, n, 512), bf(2, n, 512), fl(n, 512), fl(2, n, 512),
            fl(2, n, 128), bf(2, n, 512),
            bf(2, n, 512), bf(2, n, 512), fl(2, n, 512), bf(n, 512), bf(2, e, 512), bf(2, e, 512),
            bf(2, TABLE, 512), bf(2, n, 512), bf(2, e, 512), bf(2, n, 512), fl(8, 512), fl(8, 512),
            dma((2, 4)), dma((2, 4)), dma((2, 4)), dma((2,)), dma((2,)), dma((2,)), dma((2,)),
            dma((2, 4)), dma((2, 4)), dma((2, 4)), dma((2,)), dma((2,)), dma((2,)), dma((2,)),
            dma((2,)), dma((2,)), dma((2,)), dma((2,)), dma((2,)),
            bf(4, rows, 512), bf(4, 4 * nz, 16, LANES),
            bf(rows, 512), bf(rows, 512), bf(rows, 512),
            bf(4 * nz, 16, LANES), bf(4 * nz, 16, LANES), bf(4 * nz, 16, LANES),
            bf(4, nz, 16, 512), bf(3, nz, 16, 512),
            bf(4, nz, 16, LANES), bf(3, nz, 16, LANES),
            bf(nz, 16, 512), bf(nz - 1, 16, 512), bf(nz, 16, LANES), bf(nz - 1, 16, LANES), fl(32, 512),
            bf(nz, 4, 4, 16, 128), bf(4, 4, 4, 16, 128), bf(3, 4, 4, 16, 128),
            bf(4, 4, 16, 128), bf(3, 4, 16, 128), bf(4, 16, 128), bf(3, 16, 128),
            dma((copies,)), dma((copies,)), dma((1,)),
        ],
        compiler_params=pltpu.CompilerParams(
            collective_id=0, has_side_effects=True, vmem_limit_bytes=56 << 20
        ),
        name="layers",
    )(*operands)


def finish_kernel(
    node_in, edge_in, fin_in, node_o, edge_o, ein_o, eout_o, nin_o, nout_o, ge_o, gn_o,
    rfin, node_v, edge_v, sems, out_sems,
):
    first = pltpu.make_async_copy(fin_in, rfin, sems.at[0])
    first.start()
    parts = [(node_in.at[k], node_v.at[k], node_o.at[0, k]) for k in range(2)]
    for k in range(2):
        for q in range(2):
            at = slice(q * 192, q * 192 + 192)
            parts.append((edge_in.at[k, at], edge_v.at[k, at], edge_o.at[0, k, at]))
    moves = [pltpu.make_async_copy(u, v, sems.at[1 + i]) for i, (u, v, _) in enumerate(parts)]
    stores = [pltpu.make_async_copy(v, w, out_sems.at[i]) for i, (_, v, w) in enumerate(parts)]
    for c in moves:
        c.start()
    for c, w in zip(moves, stores):
        c.wait()
        w.start()
    first.wait()
    t = lax.axis_index("dom") * 2 + lax.axis_index("rep")
    for r in range(12):
        ein_o[r] = rfin[r : r + 1]
    nin_o[0] = rfin[16:24]
    eout_o[0] = rfin[24:28]
    nout_o[0] = rfin[28:32]
    pair = rfin[12:14]
    lane = lax.broadcasted_iota(jnp.int32, (2, 512), 1)
    narrow = lax.broadcasted_iota(jnp.int32, (2, 128), 1)
    picked = jnp.zeros((2, 128), F4)
    for i in range(4):
        value = jnp.sum(jnp.where(lane == t * 4 + i, pair, 0.0), axis=1, keepdims=True)
        picked = picked + jnp.where(narrow == i, value, 0.0)
    ge_o[...] = picked[0:1, 0:4]
    gn_o[...] = picked[1:2, 0:4]
    for c in stores:
        c.wait()


def finish_call(node, edge, fin):
    hbm = pl.BlockSpec(memory_space=pl.ANY)
    vm = pl.BlockSpec(memory_space=pltpu.VMEM)
    return pl.pallas_call(
        finish_kernel,
        out_shape=[
            jax.ShapeDtypeStruct((1, *node.shape), BF),
            jax.ShapeDtypeStruct((1, *edge.shape), BF),
            jax.ShapeDtypeStruct((12, 1, 512), F4),
            jax.ShapeDtypeStruct((1, 4, 512), F4),
            jax.ShapeDtypeStruct((1, 8, 512), F4),
            jax.ShapeDtypeStruct((1, 4, 512), F4),
            jax.ShapeDtypeStruct((1, 4), F4),
            jax.ShapeDtypeStruct((1, 4), F4),
        ],
        in_specs=[hbm] * 3,
        out_specs=[hbm] * 2 + [vm] * 6,
        scratch_shapes=[
            pltpu.VMEM((32, 512), F4), pltpu.VMEM(node.shape, BF), pltpu.VMEM(edge.shape, BF),
            pltpu.SemaphoreType.DMA((7,)), pltpu.SemaphoreType.DMA((6,)),
        ],
        compiler_params=pltpu.CompilerParams(vmem_limit_bytes=56 << 20),
        name="finish",
    )(node, edge, fin)


def body(
    node_latent, edge_latent, node_cot, edge_src, edge_dst, edge_count, send_index,
    w_edge_in, w_edge_out, w_node_in, w_node_out, gain_edge, gain_node,
):
    micro = node_latent.shape[0]
    factor = float(micro * lax.axis_size("rep") * NODES_DEV * lax.axis_size("dom")) ** (-0.5)
    node, edge, fin = layer_call(
        (
            edge_src, edge_dst, send_index, edge_count, node_latent, edge_latent, node_cot,
            w_edge_in, w_edge_out, w_node_in, w_node_out, gain_edge, gain_node,
        ),
        factor,
    )
    node, edge, ein, *rest = finish_call(node, edge, fin)
    return (node, edge, jnp.swapaxes(ein, 0, 1), *rest)


def solution(mesh):
    placed = (
        P("rep", "dom", None),
        P("rep", "dom", None),
        P("rep", "dom", None),
        P("dom"),
        P("dom"),
        P("dom"),
        P("dom", None, None),
        P("segment", None, None),
        P("segment", None, None),
        P("segment", None, None),
        P("segment", None, None),
        P("segment", None),
        P("segment", None),
    )
    return jax.shard_map(
        body,
        mesh=mesh,
        in_specs=placed,
        out_specs=(
            P("segment", "rep", "dom", None),
            P("segment", "rep", "dom", None),
            P("segment", ("dom", "rep"), None),
            P("segment", ("dom", "rep"), None),
            P("segment", ("dom", "rep"), None),
            P("segment", ("dom", "rep"), None),
            P("segment", ("dom", "rep")),
            P("segment", ("dom", "rep")),
        ),
        check_vma=False,
    )
```

```python
import functools

import jax
import jax.numpy as jnp
from jax import lax
from jax.experimental import pallas as pl
from jax.experimental.pallas import tpu as pltpu
from jax.sharding import PartitionSpec as P

OFFSETS = (1, -1, 2, -2)
HALO = 16
EPS = 1e-05
MESH = pl.DeviceIdType.MESH
ROWS_A = 48
GAIN = 16
LANES = 384
NODES_DEV = 128
EDGES_DEV = 384
HALOS = 64
TABLE = 192
BLOCK = 128
BF = jnp.bfloat16
F4 = jnp.float32


def mm(a, b):
    return jnp.dot(a, b, preferred_element_type=F4)


def mm_tn(a, b):
    return lax.dot_general(a, b, (((0,), (0,)), ((), ())), preferred_element_type=F4)


def silu_grad(pre):
    sig = jax.nn.sigmoid(pre)
    return sig * (1.0 + pre * (1.0 - sig))


def layer_kernel(
    src_in, dst_in, send_in, count_in, node_in, edge_in, cot_in,
    w_ein_in, w_eout_in, w_nin_in, w_nout_in, gain_e_in, gain_n_in,
    node_out, edge_out, fin_out,
    src_row, dst_row, send_row, count, w_ein, w_eout, w_nin, w_nout, gain_e, gain_n, l_first,
    t_ein, t_eout, t_nin, t_nout, oht, oh, inc, inct, sendt, sendm,
    tab, ein, cn, ce, cn32, halo1, halo2, hs1, hs2, bh,
    sr, pre, mid, tmp, xhat, rstd, enew, agg, pren, midn, tmpn, xhatn, rstdn, hnew,
    doutn, dpren, down, dagg, doute, dpre, gs, gr, de, dh, dge, dgn,
    s_halo1, s_halo2, r_halo, s_fe, r_fe, s_fh, r_fh,
    s_bh, r_bh1, r_bh2, s_be, r_be, s_bo, r_bo,
    l_node, l_edge, l_cot, l_nout, l_eout,
    ga, gb, ta, ua, va, tb, ub, vb, a2, ga2, b2, gb2, ca, ra, cb, rb, gz, zr, zl, hy, ry, hx, rx,
    send_sem, recv_sem,
    *, nz, factor,
):
    seg = lax.axis_index("segment")
    dom = lax.axis_index("dom")
    n_dom = lax.axis_size("dom")
    first = seg == 0
    second = seg == 1

    def near(step, segment):
        return {"dom": (dom + step + n_dom) % n_dom, "segment": segment}

    rep = lax.axis_index("rep")
    z = dom // 8
    y = (dom // 2) % 4
    px = rep * 2 + dom % 2

    def at_y(p):
        return {"dom": z * 8 + p * 2 + dom % 2}

    def at_z(p):
        return {"dom": p * 8 + dom % 8}

    def at_x(p):
        return {"dom": (dom // 2) * 2 + p % 2, "rep": p // 2}

    z_peers = [(z + j) % nz for j in range(1, nz)]
    x_peers = [(px + j) % 4 for j in range(1, 4)]
    y_peers = [(y + j) % 4 for j in range(1, 4)]
    greet = [near(step, s) for step in OFFSETS for s in range(2)]
    greet += [at_y(p) for p in y_peers] + [at_x(p) for p in x_peers] + [at_z(p) for p in z_peers]
    greet += [{"segment": 1 - seg}]
    def load_node(k):
        return pltpu.make_async_copy(node_in.at[k], tab.at[k, 0:NODES_DEV], l_node.at[k])

    small = [
        pltpu.make_async_copy(u, v, l_first.at[i])
        for i, (u, v) in enumerate(
            [
                (src_in, src_row), (dst_in, dst_row), (send_in, send_row), (count_in, count),
                (gain_e_in, gain_e), (gain_n_in, gain_n),
            ]
        )
    ]
    for c in small:
        c.start()

    @pl.when(first)
    def _():
        for k in range(2):
            load_node(k).start()

    barrier = pltpu.get_barrier_semaphore()
    for device in greet:
        pl.semaphore_signal(barrier, inc=1, device_id=device, device_id_type=MESH)

    def remote(src, dst, send, recv, device):
        return pltpu.make_async_remote_copy(
            src_ref=src, dst_ref=dst, send_sem=send, recv_sem=recv,
            device_id=device, device_id_type=MESH,
        )

    def load_edge(k):
        return pltpu.make_async_copy(edge_in.at[k], ein.at[k], l_edge.at[k])

    def load_cot(k):
        return pltpu.make_async_copy(cot_in.at[k], cn.at[k], l_cot.at[k])

    def store_node(src, k):
        return pltpu.make_async_copy(src.at[k], node_out.at[k], l_nout.at[k])

    def store_edge(src, k):
        return pltpu.make_async_copy(src.at[k], edge_out.at[k], l_eout.at[k])

    def halo_copy(src, k, j, sems, segment):
        rows = slice(j * HALO, (j + 1) * HALO)
        into = slice(NODES_DEV + j * HALO, NODES_DEV + (j + 1) * HALO)
        return remote(
            src.at[k, rows], tab.at[k, into], sems.at[k, j], r_halo.at[k, j],
            near(OFFSETS[j], segment),
        )

    def back_copy(dst, k, j, recv):
        rows = slice(j * HALO, (j + 1) * HALO)
        return remote(
            bh.at[k, rows], dst.at[k, rows], s_bh.at[k, j], recv.at[k, j],
            near(-OFFSETS[j], 0),
        )

    def sib_e(k):
        return remote(enew.at[k], ein.at[k], s_fe.at[k], r_fe.at[k], {"segment": 1 - seg})

    def sib_h(k):
        return remote(
            hnew.at[k], tab.at[k, 0:NODES_DEV], s_fh.at[k], r_fh.at[k], {"segment": 1 - seg}
        )

    def sib_de(k):
        return remote(de.at[k], ce.at[k], s_be.at[k], r_be.at[k], {"segment": 1 - seg})

    def sib_do(k):
        return remote(down.at[k], cn32.at[k], s_bo.at[k], r_bo.at[k], {"segment": 1 - seg})

    large = [
        pltpu.make_async_copy(u.at[0], v, l_first.at[6 + i])
        for i, (u, v) in enumerate(
            [(w_ein_in, w_ein), (w_eout_in, w_eout), (w_nin_in, w_nin), (w_nout_in, w_nout)]
        )
    ]
    @pl.when(first)
    def _():
        for k in range(2):
            load_edge(k).start()

    @pl.when(second)
    def _():
        for k in range(2):
            load_cot(k).start()

    for c in large:
        c.start()
    for c in small:
        c.wait()
    node = lax.broadcasted_iota(jnp.int32, (NODES_DEV, HALO), 0)
    hots = [jnp.where(node == send_row[0, j : j + 1, :], 1.0, 0.0) for j in range(4)]
    f_send = jnp.concatenate(hots + [jnp.zeros((NODES_DEV, NODES_DEV - HALOS), F4)], axis=1)
    sendt[...] = f_send.astype(BF)
    sendm[...] = f_send.T.astype(BF)

    @pl.when(first)
    def _():
        for k in range(2):
            load_node(k).wait()
            hs1[k] = mm(sendm[0:HALOS], tab[k, 0:NODES_DEV]).astype(BF)

    pl.semaphore_wait(barrier, len(greet))

    @pl.when(first)
    def _():
        for k in range(2):
            for j in range(4):
                halo_copy(hs1, k, j, s_halo1, 0).start()

    live_count = count[0]
    hot_src = lax.broadcasted_iota(jnp.int32, (TABLE, EDGES_DEV), 0) == src_row[...].reshape(1, EDGES_DEV)
    owner = lax.broadcasted_iota(jnp.int32, (NODES_DEV, EDGES_DEV), 0)
    slot = lax.broadcasted_iota(jnp.int32, (NODES_DEV, EDGES_DEV), 1)
    hot_dst = owner == dst_row[...].reshape(1, EDGES_DEV)
    hot_inc = hot_dst & (slot < live_count)
    f_src = jnp.where(hot_src, 1.0, 0.0)
    f_dst = jnp.where(hot_dst, 1.0, 0.0)
    f_inc = jnp.where(hot_inc, 1.0, 0.0)
    oht[0:TABLE] = f_src.astype(BF)
    oht[TABLE:] = f_dst.astype(BF)
    inc[...] = f_inc.astype(BF)
    t_src = f_src.T.astype(BF)
    oh[:, 0:NODES_DEV] = t_src[:, 0:NODES_DEV]
    oh[:, NODES_DEV : 2 * NODES_DEV] = f_dst.T.astype(BF)
    oh[:, 2 * NODES_DEV :] = t_src[:, NODES_DEV:]
    inct[...] = f_inc.T.astype(BF)
    dge[...] = jnp.zeros_like(dge)
    dgn[...] = jnp.zeros_like(dgn)

    @pl.when(second)
    def _():
        ce[...] = jnp.zeros_like(ce)

    for c in large:
        c.wait()

    def mean(v):
        return jnp.sum(v, axis=-1, keepdims=True) * (1.0 / 512.0)

    def norm_block(outer, at, k, x_ref, r_ref):
        center = outer - mean(outer)
        inv = lax.rsqrt(mean(center * center) + EPS)
        hat = center * inv
        x_ref[k, at, :] = hat
        r_ref[k, at, :] = jnp.broadcast_to(inv, (BLOCK, 128))
        return hat

    def norm_back(cot, gain, hat, inv):
        dy = cot * gain
        return inv * (dy - mean(dy) - hat * mean(dy * hat))

    def forward(k):
        @pl.when(first)
        def _():
            load_edge(k).wait()

        @pl.when(second)
        def _():
            sib_e(k).wait_recv()

        pre[k] = mm(ein[k], w_ein[0:512])

        @pl.when(second)
        def _():
            sib_h(k).wait_recv()

        own = tab[k, 0:NODES_DEV]
        sr[0:NODES_DEV] = mm(own, w_ein[512:1024]).astype(BF)
        sr[NODES_DEV : 2 * NODES_DEV] = mm(own, w_ein[1024:1536]).astype(BF)
        pre[k] += mm(oh[:, 0 : 2 * NODES_DEV], sr[0 : 2 * NODES_DEV])
        for j in range(4):
            halo_copy(hs1, k, j, s_halo1, 0).wait_recv()
        sr[2 * NODES_DEV :] = mm(tab[k, NODES_DEV:], w_ein[512:1024]).astype(BF)
        tmp[...] = mm(oh[:, 2 * NODES_DEV :], sr[2 * NODES_DEV :])

        @pl.loop(0, EDGES_DEV // BLOCK, unroll=True)
        def _(i):
            at = pl.ds(pl.multiple_of(i * BLOCK, BLOCK), BLOCK)
            v = pre[k, at, :] + tmp[at, :]
            pre[k, at, :] = v
            mid[k, at, :] = (v * jax.nn.sigmoid(v)).astype(BF)

        tmp[...] = mm(mid[k], w_eout[...])

        @pl.loop(0, EDGES_DEV // BLOCK, unroll=True)
        def _(i):
            at = pl.ds(pl.multiple_of(i * BLOCK, BLOCK), BLOCK)
            hat = norm_block(tmp[at, :], at, k, xhat, rstd)
            rows = lax.broadcasted_iota(jnp.int32, (BLOCK, 512), 0) + i * BLOCK
            old = ein[k, at, :].astype(F4)
            enew[k, at, :] = jnp.where(rows < live_count, old + hat * gain_e[...], old).astype(BF)

        @pl.when(first)
        def _():
            sib_e(k).start()

        @pl.when(second)
        def _():
            store_edge(enew, k).start()

        agg[k] = mm(inc[...], enew[k]).astype(BF)
        pren[k] = mm(own, w_nin[0:512]) + mm(agg[k], w_nin[512:1024])

        @pl.loop(0, NODES_DEV // BLOCK, unroll=True)
        def _(i):
            at = pl.ds(pl.multiple_of(i * BLOCK, BLOCK), BLOCK)
            v = pren[k, at, :]
            midn[k, at, :] = (v * jax.nn.sigmoid(v)).astype(BF)

        tmpn[...] = mm(midn[k], w_nout[...])

        @pl.loop(0, NODES_DEV // BLOCK, unroll=True)
        def _(i):
            at = pl.ds(pl.multiple_of(i * BLOCK, BLOCK), BLOCK)
            hat = norm_block(tmpn[at, :], at, k, xhatn, rstdn)
            hnew[k, at, :] = (tab[k, at, :].astype(F4) + hat * gain_n[...]).astype(BF)

        @pl.when(first)
        def _():
            hs2[k] = mm(sendm[0:HALOS], hnew[k]).astype(BF)
            for j in range(4):
                halo_copy(hs2, k, j, s_halo2, 1).start()
            sib_h(k).start()

        @pl.when(second)
        def _():
            store_node(hnew, k).start()

    def backward(k):
        @pl.when(first)
        def _():
            sib_do(k).wait_recv()
            for j in range(4):
                back_copy(halo1, k, j, r_bh1).wait_recv()
            cn[k] = (cn32[k] + mm(sendt[:, 0:HALOS], halo1[k])).astype(BF)

        @pl.when(second)
        def _():
            load_cot(k).wait()

        @pl.loop(0, NODES_DEV // BLOCK, unroll=True)
        def _(i):
            at = pl.ds(pl.multiple_of(i * BLOCK, BLOCK), BLOCK)
            cot = cn[k, at, :].astype(F4)
            hat = xhatn[k, at, :]
            dgn[...] += jnp.sum((cot * hat).reshape(BLOCK // 8, 8, 512), axis=0)
            inv = rstdn[k, at, 0:1]
            doutn[k, at, :] = norm_back(cot, gain_n[...], hat, inv).astype(BF)

        tmpn[...] = mm(doutn[k], t_nout[...])

        @pl.loop(0, NODES_DEV // BLOCK, unroll=True)
        def _(i):
            at = pl.ds(pl.multiple_of(i * BLOCK, BLOCK), BLOCK)
            dpren[k, at, :] = (tmpn[at, :] * silu_grad(pren[k, at, :])).astype(BF)

        dagg[...] = mm(dpren[k], t_nin[:, 512:1024]).astype(BF)

        @pl.when(first)
        def _():
            sib_de(k).wait_recv()

        tmp[...] = mm(inct[...], dagg[...])
        down[k] = cn[k].astype(F4) + mm(dpren[k], t_nin[:, 0:512])

        @pl.loop(0, EDGES_DEV // BLOCK, unroll=True)
        def _(i):
            at = pl.ds(pl.multiple_of(i * BLOCK, BLOCK), BLOCK)
            cot = tmp[at, :] + ce[k, at, :].astype(F4)
            tmp[at, :] = cot
            rows = lax.broadcasted_iota(jnp.int32, (BLOCK, 512), 0) + i * BLOCK
            cot = jnp.where(rows < live_count, cot, 0.0)
            hat = xhat[k, at, :]
            dge[...] += jnp.sum((cot * hat).reshape(BLOCK // 8, 8, 512), axis=0)
            inv = rstd[k, at, 0:1]
            doute[k, at, :] = norm_back(cot, gain_e[...], hat, inv).astype(BF)

        grad = mm(doute[k], t_eout[...])
        pre[k] = grad * silu_grad(pre[k])
        dpre[k] = pre[k].astype(BF)
        gs[k] = mm(oht[0:TABLE], dpre[k]).astype(BF)
        gr[k] = mm(oht[TABLE:], dpre[k]).astype(BF)
        bh[k] = mm(gs[k, NODES_DEV:], t_ein[:, 512:1024]).astype(BF)

        @pl.when(first)
        def _():
            for j in range(4):
                back_copy(halo2, k, j, r_bh2).start()

        @pl.when(second)
        def _():
            for j in range(4):
                back_copy(halo1, k, j, r_bh1).start()

        down[k] += mm(gs[k, 0:NODES_DEV], t_ein[:, 512:1024]) + mm(gr[k], t_ein[:, 1024:1536])

        @pl.when(second)
        def _():
            sib_do(k).start()

        de[k] = (tmp[...] + mm(dpre[k], t_ein[:, 0:512])).astype(BF)

        @pl.when(second)
        def _():
            sib_de(k).start()

        @pl.when(first)
        def _():
            store_edge(de, k).start()

    @pl.loop(0, 4)
    def _(step):
        forward_now = (step == 0) | (step == 1 + seg)
        k = jnp.where(first, step % 2, step // 2)

        @pl.when(step == 2 - 2 * seg)
        def _():
            for m in range(3):
                t_ein[:, m * 512 : m * 512 + 512] = w_ein[m * 512 : m * 512 + 512].T
            for m in range(2):
                t_nin[:, m * 512 : m * 512 + 512] = w_nin[m * 512 : m * 512 + 512].T
            t_eout[...] = w_eout[...].T
            t_nout[...] = w_nout[...].T

        @pl.when(forward_now)
        def _():
            forward(k)

        @pl.when(jnp.logical_not(forward_now))
        def _():
            backward(k)

    def put_ein(base, value):
        for q in range(8):
            r = base + q * 16
            row = (r // 192) * ROWS_A + r % ROWS_A
            ga[(r % 192) // ROWS_A, row : row + 16, :] = value[q * 16 : q * 16 + 16].astype(BF)

    def put_b(m, n_lo, n_hi, e, o):
        for q in range(8):
            part = (n_lo, n_hi)[q // 4][q % 4 * 32 : q % 4 * 32 + 32]
            for p in range(4):
                b = p % 2 * 2 + p // 2
                r = q * 16 + 4 * b
                tile = jnp.concatenate([part[8 * b : 8 * b + 8], e[r : r + 4], o[r : r + 4]], axis=0)
                gb[p, m * 8 + q] = tile[:, 0:LANES].astype(BF)
                gz[2 * m + q // 4, q % 4, p] = tile[:, LANES:].astype(BF)

    def both(ref):
        return ref[...].reshape(ref.shape[0] * ref.shape[1], ref.shape[2])

    def cols(ref, m):
        return jnp.concatenate([ref[0, :, m * 128 : (m + 1) * 128], ref[1, :, m * 128 : (m + 1) * 128]], axis=0)

    def own_cols(m):
        at = slice(m * 128, (m + 1) * 128)
        return jnp.concatenate([tab[0, 0:NODES_DEV, at], tab[1, 0:NODES_DEV, at]], axis=0)

    def copy(n, src, dst, device):
        return remote(src, dst, send_sem.at[n], recv_sem.at[n], device)

    class Ring:
        def __init__(self, base, src, t, u, v, me, at, cut):
            right, left, across = (me + 1) % 4, (me + 3) % 4, (me + 2) % 4
            lo, hi = slice(0, cut), slice(cut, t.shape[0])
            self.out = [
                copy(base, src.at[across, lo], t.at[lo], at(right)),
                copy(base + 1, src.at[across, hi], t.at[hi], at(left)),
                copy(base + 2, src.at[right, hi], u.at[hi], at(right)),
                copy(base + 3, src.at[left, lo], v.at[lo], at(left)),
                copy(base + 4, t.at[lo], u.at[lo], at(right)),
                copy(base + 5, t.at[hi], v.at[hi], at(left)),
            ]
            self.src, self.t, self.u, self.v = src, t, u, v
            self.me, self.right, self.left, self.cut = me, right, left, cut

        def start(self):
            for c in self.out[:4]:
                c.start()

        def middle(self, block):
            src, t, n, cut = self.src, self.t, self.t.shape[0], self.cut
            for c, q, lo, hi in ((0, self.right, 0, cut), (1, self.left, cut, n)):
                self.out[c].wait_recv()

                @pl.loop(lo // block, hi // block, unroll=4 if (hi - lo) // block % 4 == 0 else 1)
                def _(i):
                    at = pl.ds(pl.multiple_of(i * block, block), block)
                    t[at] = (t[at].astype(F4) + src[q, at].astype(F4)).astype(BF)

                self.out[4 + c].start()

        def total(self, at):
            own = self.src[self.me, at].astype(F4)
            return own + self.u[at].astype(F4) + self.v[at].astype(F4)

        def arrive(self):
            for c in self.out[2:]:
                c.wait_recv()

    ring_a = Ring(0, ga, ta, ua, va, y, at_y, 208)
    ring_b = Ring(6, gb, tb, ub, vb, px, at_x, 2 * nz)
    def spread(base, src, got, peers, at):
        moves = [copy(base + j, src.at[p], got.at[j], at(p)) for j, p in enumerate(peers)]
        for c in moves:
            c.start()
        return moves

    def nin_part(m):
        lhs = own_cols(m) if m < 4 else cols(agg, m - 4)
        return mm_tn(lhs, both(dpren))

    for m in range(4):
        put_b(
            m, nin_part(2 * m), nin_part(2 * m + 1),
            mm_tn(cols(mid, m), both(doute)), mm_tn(cols(midn, m), both(doutn)),
        )
    ring_b.start()
    zc = 24 + 2 * (nz - 1)
    up, low = at_z((z + 1) % nz), at_z((z + nz - 1) % nz)
    flow_up = [copy(zc, gz.at[(z + 4) % nz], zr.at[0], up)]
    flow_up += [copy(zc + 1 + i, zr.at[i], zr.at[i + 1], up) for i in range(3)]
    flow_low = [copy(zc + 4, gz.at[(z + nz - 3) % nz], zl.at[0], low)]
    flow_low += [copy(zc + 5 + i, zl.at[i], zl.at[i + 1], low) for i in range(2)]
    flow_up[0].start()
    flow_low[0].start()

    def pass_on(i):
        for flow, held, q in ((flow_up, zr, z + 3 - i), (flow_low, zl, z + nz - 2 + i)):
            if i + 1 < len(flow):
                flow[i].wait_recv()
                for r in range(4):
                    part = held[i, r].astype(F4) + gz[q % nz, r].astype(F4)
                    held[i, r] = part.astype(BF)
                flow[i + 1].start()

    for m in range(4):
        base = m * 128
        put_ein(base, mm_tn(cols(ein, m), both(dpre)))
        put_ein(512 + base, mm_tn(cols(tab, m), both(gs)))
        put_ein(1024 + base, mm_tn(own_cols(m), both(gr)))
    row = lax.broadcasted_iota(jnp.int32, (GAIN, 512), 0)
    sum_e = jnp.sum(dge[...], axis=0, keepdims=True)
    sum_n = jnp.sum(dgn[...], axis=0, keepdims=True)
    gains = jnp.where(row == 0, sum_e, jnp.where(row == 1, sum_n, 0.0)).astype(BF)
    for q in range(4):
        ga[q, EDGES_DEV:, :] = gains
    ring_a.start()

    @pl.when(first)
    def _():
        for k in range(2):
            for j in range(4):
                back_copy(halo2, k, j, r_bh2).wait_recv()
            dh[k] = (down[k] + mm(sendt[:, 0:HALOS], halo2[k])).astype(BF)
            store_node(dh, k).start()

    pass_on(0)
    pass_on(1)
    ring_b.middle(2)
    ring_a.middle(16)
    pass_on(2)
    flow_up[3].wait_recv()
    flow_low[2].wait_recv()
    for r in range(4):
        part = gz[z, r].astype(F4) + zr[3, r].astype(F4) + zl[2, r].astype(F4)
        hy[r] = part.astype(BF)
    flow_y = spread(zc + 7, hy, ry, y_peers, at_y)
    ring_a.arrive()
    gains = ring_a.total(slice(nz * ROWS_A, nz * ROWS_A + GAIN))[0:4]

    @pl.loop(0, nz, unroll=4)
    def _(i):
        at = pl.ds(pl.multiple_of(i * ROWS_A, 16), ROWS_A)
        total = ring_a.total(at)
        for p in range(4):
            b = p % 2 * 2 + p // 2
            tile = jnp.concatenate([total[12 * b : 12 * b + 12], gains], axis=0)
            a2[p, i] = tile.astype(BF)

    second_a = spread(12, a2, ga2, x_peers, at_x)
    ring_b.arrive()

    @pl.loop(0, nz, unroll=4)
    def _(i):
        for q in range(4):
            b2[q, i] = ring_b.total(i * 4 + q).astype(BF)

    second_b = spread(15, b2, gb2, y_peers, at_y)
    part = hy[y].astype(F4)
    for j, c in enumerate(flow_y):
        c.wait_recv()
        part = part + ry[j].astype(F4)
    hx[...] = part.astype(BF)
    flow_x = spread(zc + 10, hx, rx, x_peers, at_x)

    def along_z(base, moves, src, got, me, held, into):
        for c in moves:
            c.wait_recv()
        for i in range(nz):
            total = src[me, i].astype(F4)
            for j in range(3):
                total = total + got[j, i].astype(F4)
            held[i] = total.astype(BF)
        return spread(base, held, into, z_peers, at_z)

    def z_total(moves, held, got):
        total = held[z].astype(F4)
        for j, c in enumerate(moves):
            c.wait_recv()
            total = total + got[j].astype(F4)
        return total * factor

    third_a = along_z(24, second_a, a2, ga2, px, ca, ra)
    third_b = along_z(24 + nz - 1, second_b, b2, gb2, y, cb, rb)
    part = hx[px].astype(F4)
    for j, c in enumerate(flow_x):
        c.wait_recv()
        part = part + rx[j].astype(F4)
    fin_out[16:32, LANES:] = part * factor
    fin_out[0:16] = z_total(third_a, ca, ra)
    fin_out[16:32, 0:LANES] = z_total(third_b, cb, rb)
    for c in ring_a.out + ring_b.out + second_a + second_b + third_a + third_b + flow_up + flow_low + flow_y + flow_x:
        c.wait_send()

    @pl.when(first)
    def _():
        for k in range(2):
            sib_e(k).wait_send()
            sib_h(k).wait_send()
            for j in range(4):
                halo_copy(hs1, k, j, s_halo1, 0).wait_send()
                halo_copy(hs2, k, j, s_halo2, 1).wait_send()
                back_copy(halo2, k, j, r_bh2).wait_send()
            store_edge(de, k).wait()
            store_node(dh, k).wait()

    @pl.when(second)
    def _():
        for k in range(2):
            sib_do(k).wait_send()
            sib_de(k).wait_send()
            for j in range(4):
                back_copy(halo1, k, j, r_bh1).wait_send()
            store_edge(enew, k).wait()
            store_node(hnew, k).wait()


def layer_call(operands, factor):
    hbm = pl.BlockSpec(memory_space=pl.ANY)
    nz = 8
    i32 = jnp.int32

    def bf(*shape):
        return pltpu.VMEM(shape, BF)

    def fl(*shape):
        return pltpu.VMEM(shape, F4)

    dma = pltpu.SemaphoreType.DMA
    n, e = NODES_DEV, EDGES_DEV
    rows = nz * ROWS_A + GAIN
    copies = 24 + 2 * (nz - 1) + 13
    return pl.pallas_call(
        functools.partial(layer_kernel, nz=nz, factor=factor),
        out_shape=[
            pltpu.VMEM((2, n, 512), BF),
            pltpu.VMEM((2, e, 512), BF),
            pltpu.VMEM((32, 512), F4),
        ],
        in_specs=[hbm] * 13,
        out_specs=[pl.BlockSpec(memory_space=pltpu.VMEM)] * 3,
        scratch_shapes=[
            pltpu.VMEM((e,), i32), pltpu.VMEM((e,), i32), pltpu.VMEM((1, 4, HALO), i32), pltpu.SMEM((1,), i32),
            bf(1536, 512), bf(512, 512), bf(1024, 512), bf(512, 512), fl(1, 512), fl(1, 512), dma((10,)),
            bf(512, 1536), bf(512, 512), bf(512, 1024), bf(512, 512),
            bf(320, e), bf(e, 320), bf(n, e), bf(e, n), bf(n, n), bf(n, n),
            bf(2, TABLE, 512), bf(2, e, 512), bf(2, n, 512), bf(2, e, 512), fl(2, n, 512),
            bf(2, HALOS, 512), bf(2, HALOS, 512), bf(2, HALOS, 512), bf(2, HALOS, 512), bf(2, HALOS, 512),
            bf(320, 512), fl(2, e, 512), bf(2, e, 512), fl(e, 512), fl(2, e, 512), fl(2, e, 128),
            bf(2, e, 512), bf(2, n, 512), fl(2, n, 512), bf(2, n, 512), fl(n, 512), fl(2, n, 512),
            fl(2, n, 128), bf(2, n, 512),
            bf(2, n, 512), bf(2, n, 512), fl(2, n, 512), bf(n, 512), bf(2, e, 512), bf(2, e, 512),
            bf(2, TABLE, 512), bf(2, n, 512), bf(2, e, 512), bf(2, n, 512), fl(8, 512), fl(8, 512),
            dma((2, 4)), dma((2, 4)), dma((2, 4)), dma((2,)), dma((2,)), dma((2,)), dma((2,)),
            dma((2, 4)), dma((2, 4)), dma((2, 4)), dma((2,)), dma((2,)), dma((2,)), dma((2,)),
            dma((2,)), dma((2,)), dma((2,)), dma((2,)), dma((2,)),
            bf(4, rows, 512), bf(4, 4 * nz, 16, LANES),
            bf(rows, 512), bf(rows, 512), bf(rows, 512),
            bf(4 * nz, 16, LANES), bf(4 * nz, 16, LANES), bf(4 * nz, 16, LANES),
            bf(4, nz, 16, 512), bf(3, nz, 16, 512),
            bf(4, nz, 16, LANES), bf(3, nz, 16, LANES),
            bf(nz, 16, 512), bf(nz - 1, 16, 512), bf(nz, 16, LANES), bf(nz - 1, 16, LANES),
            bf(nz, 4, 4, 16, 128), bf(4, 4, 4, 16, 128), bf(3, 4, 4, 16, 128),
            bf(4, 4, 16, 128), bf(3, 4, 16, 128), bf(4, 16, 128), bf(3, 16, 128),
            dma((copies,)), dma((copies,)),
        ],
        compiler_params=pltpu.CompilerParams(
            collective_id=0, has_side_effects=True, vmem_limit_bytes=56 << 20
        ),
        name="layers",
    )(*operands)


def finish_kernel(
    node_in, edge_in, rfin, node_o, edge_o, ein_o, eout_o, nin_o, nout_o, ge_o, gn_o, sems
):
    stores = []
    for k in range(2):
        stores.append(pltpu.make_async_copy(edge_in.at[k], edge_o.at[0, k], sems.at[k]))
        stores.append(pltpu.make_async_copy(node_in.at[k], node_o.at[0, k], sems.at[2 + k]))
    for c in stores:
        c.start()
    t = lax.axis_index("dom") * 2 + lax.axis_index("rep")
    for r in range(12):
        ein_o[r] = rfin[r : r + 1]
    nin_o[0] = rfin[16:24]
    eout_o[0] = rfin[24:28]
    nout_o[0] = rfin[28:32]
    pair = rfin[12:14]
    lane = lax.broadcasted_iota(jnp.int32, (2, 512), 1)
    narrow = lax.broadcasted_iota(jnp.int32, (2, 128), 1)
    picked = jnp.zeros((2, 128), F4)
    for i in range(4):
        value = jnp.sum(jnp.where(lane == t * 4 + i, pair, 0.0), axis=1, keepdims=True)
        picked = picked + jnp.where(narrow == i, value, 0.0)
    ge_o[...] = picked[0:1, 0:4]
    gn_o[...] = picked[1:2, 0:4]
    for c in stores:
        c.wait()


def finish_call(node, edge, fin):
    hbm = pl.BlockSpec(memory_space=pl.ANY)
    vm = pl.BlockSpec(memory_space=pltpu.VMEM)
    return pl.pallas_call(
        finish_kernel,
        out_shape=[
            jax.ShapeDtypeStruct((1, *node.shape), BF),
            jax.ShapeDtypeStruct((1, *edge.shape), BF),
            jax.ShapeDtypeStruct((12, 1, 512), F4),
            jax.ShapeDtypeStruct((1, 4, 512), F4),
            jax.ShapeDtypeStruct((1, 8, 512), F4),
            jax.ShapeDtypeStruct((1, 4, 512), F4),
            jax.ShapeDtypeStruct((1, 4), F4),
            jax.ShapeDtypeStruct((1, 4), F4),
        ],
        in_specs=[vm] * 3,
        out_specs=[hbm] * 2 + [vm] * 6,
        scratch_shapes=[pltpu.SemaphoreType.DMA((4,))],
        compiler_params=pltpu.CompilerParams(vmem_limit_bytes=16 << 20),
        name="finish",
    )(node, edge, fin)


def body(
    node_latent, edge_latent, node_cot, edge_src, edge_dst, edge_count, send_index,
    w_edge_in, w_edge_out, w_node_in, w_node_out, gain_edge, gain_node,
):
    micro = node_latent.shape[0]
    factor = float(micro * lax.axis_size("rep") * NODES_DEV * lax.axis_size("dom")) ** (-0.5)
    node, edge, fin = layer_call(
        (
            edge_src, edge_dst, send_index, edge_count, node_latent, edge_latent, node_cot,
            w_edge_in, w_edge_out, w_node_in, w_node_out, gain_edge, gain_node,
        ),
        factor,
    )
    node, edge, ein, *rest = finish_call(node, edge, fin)
    return (node, edge, jnp.swapaxes(ein, 0, 1), *rest)


def solution(mesh):
    placed = (
        P("rep", "dom", None),
        P("rep", "dom", None),
        P("rep", "dom", None),
        P("dom"),
        P("dom"),
        P("dom"),
        P("dom", None, None),
        P("segment", None, None),
        P("segment", None, None),
        P("segment", None, None),
        P("segment", None, None),
        P("segment", None),
        P("segment", None),
    )
    return jax.shard_map(
        body,
        mesh=mesh,
        in_specs=placed,
        out_specs=(
            P("segment", "rep", "dom", None),
            P("segment", "rep", "dom", None),
            P("segment", ("dom", "rep"), None),
            P("segment", ("dom", "rep"), None),
            P("segment", ("dom", "rep"), None),
            P("segment", ("dom", "rep"), None),
            P("segment", ("dom", "rep")),
            P("segment", ("dom", "rep")),
        ),
        check_vma=False,
    )
```

```python
import functools

import jax
import jax.numpy as jnp
from jax import lax
from jax.experimental import pallas as pl
from jax.experimental.pallas import tpu as pltpu
from jax.sharding import PartitionSpec as P

OFFSETS = (1, -1, 2, -2)
HALO = 16
EPS = 1e-05
MESH = pl.DeviceIdType.MESH
ROWS_A = 48
GAIN = 16
LANES = 384
NODES_DEV = 128
EDGES_DEV = 384
HALOS = 64
TABLE = 192
BLOCK = 128
BF = jnp.bfloat16
F4 = jnp.float32


def mm(a, b):
    return jnp.dot(a, b, preferred_element_type=F4)


def mm_tn(a, b):
    return lax.dot_general(a, b, (((0,), (0,)), ((), ())), preferred_element_type=F4)


def silu_grad(pre):
    sig = jax.nn.sigmoid(pre)
    return sig * (1.0 + pre * (1.0 - sig))


def layer_kernel(
    src_in, dst_in, send_in, count_in, node_in, edge_in, cot_in,
    w_ein_in, w_eout_in, w_nin_in, w_nout_in, gain_e_in, gain_n_in,
    node_out, edge_out, fin_out,
    src_row, dst_row, send_row, count, w_ein, w_eout, w_nin, w_nout, gain_e, gain_n, l_first,
    t_ein, t_eout, t_nin, t_nout, oht, oh, inc, inct, sendt, sendm,
    tab, ein, cn, ce, cn32, halo1, halo2, hs1, hs2, bh,
    sr, pre, mid, tmp, xhat, rstd, enew, agg, pren, midn, tmpn, xhatn, rstdn, hnew,
    doutn, dpren, down, dagg, doute, dpre, gs, gr, de, dh, dge, dgn,
    s_halo1, s_halo2, r_halo, s_fe, r_fe, s_fh, r_fh,
    s_bh, r_bh1, r_bh2, s_be, r_be, s_bo, r_bo,
    l_node, l_edge, l_cot, l_nout, l_eout,
    ga, gb, ta, ua, va, tb, ub, vb, a2, ga2, b2, gb2, ca, ra, cb, rb, gz, zr, zl, hy, ry, hx, rx,
    send_sem, recv_sem,
    *, nz, factor,
):
    seg = lax.axis_index("segment")
    dom = lax.axis_index("dom")
    n_dom = lax.axis_size("dom")
    first = seg == 0
    second = seg == 1

    def near(step, segment):
        return {"dom": (dom + step + n_dom) % n_dom, "segment": segment}

    rep = lax.axis_index("rep")
    z = dom // 8
    y = (dom // 2) % 4
    px = rep * 2 + dom % 2

    def at_y(p):
        return {"dom": z * 8 + p * 2 + dom % 2}

    def at_z(p):
        return {"dom": p * 8 + dom % 8}

    def at_x(p):
        return {"dom": (dom // 2) * 2 + p % 2, "rep": p // 2}

    z_peers = [(z + j) % nz for j in range(1, nz)]
    x_peers = [(px + j) % 4 for j in range(1, 4)]
    y_peers = [(y + j) % 4 for j in range(1, 4)]
    greet = [near(step, s) for step in OFFSETS for s in range(2)]
    greet += [at_y(p) for p in y_peers] + [at_x(p) for p in x_peers] + [at_z(p) for p in z_peers]
    greet += [{"segment": 1 - seg}]
    def load_node(k):
        return pltpu.make_async_copy(node_in.at[k], tab.at[k, 0:NODES_DEV], l_node.at[k])

    small = [
        pltpu.make_async_copy(u, v, l_first.at[i])
        for i, (u, v) in enumerate(
            [
                (src_in, src_row), (dst_in, dst_row), (send_in, send_row), (count_in, count),
                (gain_e_in, gain_e), (gain_n_in, gain_n),
            ]
        )
    ]
    for c in small:
        c.start()

    @pl.when(first)
    def _():
        for k in range(2):
            load_node(k).start()

    barrier = pltpu.get_barrier_semaphore()
    for device in greet:
        pl.semaphore_signal(barrier, inc=1, device_id=device, device_id_type=MESH)

    def remote(src, dst, send, recv, device):
        return pltpu.make_async_remote_copy(
            src_ref=src, dst_ref=dst, send_sem=send, recv_sem=recv,
            device_id=device, device_id_type=MESH,
        )

    def load_edge(k):
        return pltpu.make_async_copy(edge_in.at[k], ein.at[k], l_edge.at[k])

    def load_cot(k):
        return pltpu.make_async_copy(cot_in.at[k], cn.at[k], l_cot.at[k])

    def store_node(src, k):
        return pltpu.make_async_copy(src.at[k], node_out.at[k], l_nout.at[k])

    def store_edge(src, k):
        return pltpu.make_async_copy(src.at[k], edge_out.at[k], l_eout.at[k])

    def halo_copy(src, k, j, sems, segment):
        rows = slice(j * HALO, (j + 1) * HALO)
        into = slice(NODES_DEV + j * HALO, NODES_DEV + (j + 1) * HALO)
        return remote(
            src.at[k, rows], tab.at[k, into], sems.at[k, j], r_halo.at[k, j],
            near(OFFSETS[j], segment),
        )

    def back_copy(dst, k, j, recv):
        rows = slice(j * HALO, (j + 1) * HALO)
        return remote(
            bh.at[k, rows], dst.at[k, rows], s_bh.at[k, j], recv.at[k, j],
            near(-OFFSETS[j], 0),
        )

    def sib_e(k):
        return remote(enew.at[k], ein.at[k], s_fe.at[k], r_fe.at[k], {"segment": 1 - seg})

    def sib_h(k):
        return remote(
            hnew.at[k], tab.at[k, 0:NODES_DEV], s_fh.at[k], r_fh.at[k], {"segment": 1 - seg}
        )

    def sib_de(k):
        return remote(de.at[k], ce.at[k], s_be.at[k], r_be.at[k], {"segment": 1 - seg})

    def sib_do(k):
        return remote(down.at[k], cn32.at[k], s_bo.at[k], r_bo.at[k], {"segment": 1 - seg})

    large = [
        pltpu.make_async_copy(u.at[0], v, l_first.at[6 + i])
        for i, (u, v) in enumerate(
            [(w_ein_in, w_ein), (w_eout_in, w_eout), (w_nin_in, w_nin), (w_nout_in, w_nout)]
        )
    ]
    @pl.when(first)
    def _():
        for k in range(2):
            load_edge(k).start()

    @pl.when(second)
    def _():
        for k in range(2):
            load_cot(k).start()

    for c in large:
        c.start()
    for c in small:
        c.wait()
    node = lax.broadcasted_iota(jnp.int32, (NODES_DEV, HALO), 0)
    hots = [jnp.where(node == send_row[0, j : j + 1, :], 1.0, 0.0) for j in range(4)]
    f_send = jnp.concatenate(hots + [jnp.zeros((NODES_DEV, NODES_DEV - HALOS), F4)], axis=1)
    sendt[...] = f_send.astype(BF)
    sendm[...] = f_send.T.astype(BF)

    @pl.when(first)
    def _():
        for k in range(2):
            load_node(k).wait()
            hs1[k] = mm(sendm[0:HALOS], tab[k, 0:NODES_DEV]).astype(BF)

    pl.semaphore_wait(barrier, len(greet))

    @pl.when(first)
    def _():
        for k in range(2):
            for j in range(4):
                halo_copy(hs1, k, j, s_halo1, 0).start()

    live_count = count[0]
    hot_src = lax.broadcasted_iota(jnp.int32, (TABLE, EDGES_DEV), 0) == src_row[...].reshape(1, EDGES_DEV)
    owner = lax.broadcasted_iota(jnp.int32, (NODES_DEV, EDGES_DEV), 0)
    slot = lax.broadcasted_iota(jnp.int32, (NODES_DEV, EDGES_DEV), 1)
    hot_dst = owner == dst_row[...].reshape(1, EDGES_DEV)
    hot_inc = hot_dst & (slot < live_count)
    f_src = jnp.where(hot_src, 1.0, 0.0)
    f_dst = jnp.where(hot_dst, 1.0, 0.0)
    f_inc = jnp.where(hot_inc, 1.0, 0.0)
    oht[0:TABLE] = f_src.astype(BF)
    oht[TABLE:] = f_dst.astype(BF)
    inc[...] = f_inc.astype(BF)
    t_src = f_src.T.astype(BF)
    oh[:, 0:NODES_DEV] = t_src[:, 0:NODES_DEV]
    oh[:, NODES_DEV : 2 * NODES_DEV] = f_dst.T.astype(BF)
    oh[:, 2 * NODES_DEV :] = t_src[:, NODES_DEV:]
    inct[...] = f_inc.T.astype(BF)
    dge[...] = jnp.zeros_like(dge)
    dgn[...] = jnp.zeros_like(dgn)

    @pl.when(second)
    def _():
        ce[...] = jnp.zeros_like(ce)

    for c in large:
        c.wait()

    def mean(v):
        return jnp.sum(v, axis=-1, keepdims=True) * (1.0 / 512.0)

    def norm_block(outer, at, k, x_ref, r_ref):
        center = outer - mean(outer)
        inv = lax.rsqrt(mean(center * center) + EPS)
        hat = center * inv
        x_ref[k, at, :] = hat
        r_ref[k, at, :] = jnp.broadcast_to(inv, (BLOCK, 128))
        return hat

    def norm_back(cot, gain, hat, inv):
        dy = cot * gain
        return inv * (dy - mean(dy) - hat * mean(dy * hat))

    def forward(k):
        @pl.when(first)
        def _():
            load_edge(k).wait()

        @pl.when(second)
        def _():
            sib_e(k).wait_recv()

        pre[k] = mm(ein[k], w_ein[0:512])

        @pl.when(second)
        def _():
            sib_h(k).wait_recv()

        own = tab[k, 0:NODES_DEV]
        sr[0:NODES_DEV] = mm(own, w_ein[512:1024]).astype(BF)
        sr[NODES_DEV : 2 * NODES_DEV] = mm(own, w_ein[1024:1536]).astype(BF)
        pre[k] += mm(oh[:, 0 : 2 * NODES_DEV], sr[0 : 2 * NODES_DEV])
        for j in range(4):
            halo_copy(hs1, k, j, s_halo1, 0).wait_recv()
        sr[2 * NODES_DEV :] = mm(tab[k, NODES_DEV:], w_ein[512:1024]).astype(BF)
        tmp[...] = mm(oh[:, 2 * NODES_DEV :], sr[2 * NODES_DEV :])

        @pl.loop(0, EDGES_DEV // BLOCK, unroll=True)
        def _(i):
            at = pl.ds(pl.multiple_of(i * BLOCK, BLOCK), BLOCK)
            v = pre[k, at, :] + tmp[at, :]
            pre[k, at, :] = v
            mid[k, at, :] = (v * jax.nn.sigmoid(v)).astype(BF)

        tmp[...] = mm(mid[k], w_eout[...])

        @pl.loop(0, EDGES_DEV // BLOCK, unroll=True)
        def _(i):
            at = pl.ds(pl.multiple_of(i * BLOCK, BLOCK), BLOCK)
            hat = norm_block(tmp[at, :], at, k, xhat, rstd)
            rows = lax.broadcasted_iota(jnp.int32, (BLOCK, 512), 0) + i * BLOCK
            old = ein[k, at, :].astype(F4)
            enew[k, at, :] = jnp.where(rows < live_count, old + hat * gain_e[...], old).astype(BF)

        @pl.when(first)
        def _():
            sib_e(k).start()

        @pl.when(second)
        def _():
            store_edge(enew, k).start()

        agg[k] = mm(inc[...], enew[k]).astype(BF)
        pren[k] = mm(own, w_nin[0:512]) + mm(agg[k], w_nin[512:1024])

        @pl.loop(0, NODES_DEV // BLOCK, unroll=True)
        def _(i):
            at = pl.ds(pl.multiple_of(i * BLOCK, BLOCK), BLOCK)
            v = pren[k, at, :]
            midn[k, at, :] = (v * jax.nn.sigmoid(v)).astype(BF)

        tmpn[...] = mm(midn[k], w_nout[...])

        @pl.loop(0, NODES_DEV // BLOCK, unroll=True)
        def _(i):
            at = pl.ds(pl.multiple_of(i * BLOCK, BLOCK), BLOCK)
            hat = norm_block(tmpn[at, :], at, k, xhatn, rstdn)
            hnew[k, at, :] = (tab[k, at, :].astype(F4) + hat * gain_n[...]).astype(BF)

        @pl.when(first)
        def _():
            hs2[k] = mm(sendm[0:HALOS], hnew[k]).astype(BF)
            for j in range(4):
                halo_copy(hs2, k, j, s_halo2, 1).start()
            sib_h(k).start()

        @pl.when(second)
        def _():
            store_node(hnew, k).start()

    def backward(k):
        @pl.when(first)
        def _():
            sib_do(k).wait_recv()
            for j in range(4):
                back_copy(halo1, k, j, r_bh1).wait_recv()
            cn[k] = (cn32[k] + mm(sendt[:, 0:HALOS], halo1[k])).astype(BF)

        @pl.when(second)
        def _():
            load_cot(k).wait()

        @pl.loop(0, NODES_DEV // BLOCK, unroll=True)
        def _(i):
            at = pl.ds(pl.multiple_of(i * BLOCK, BLOCK), BLOCK)
            cot = cn[k, at, :].astype(F4)
            hat = xhatn[k, at, :]
            dgn[...] += jnp.sum((cot * hat).reshape(BLOCK // 8, 8, 512), axis=0)
            inv = rstdn[k, at, 0:1]
            doutn[k, at, :] = norm_back(cot, gain_n[...], hat, inv).astype(BF)

        tmpn[...] = mm(doutn[k], t_nout[...])

        @pl.loop(0, NODES_DEV // BLOCK, unroll=True)
        def _(i):
            at = pl.ds(pl.multiple_of(i * BLOCK, BLOCK), BLOCK)
            dpren[k, at, :] = (tmpn[at, :] * silu_grad(pren[k, at, :])).astype(BF)

        dagg[...] = mm(dpren[k], t_nin[:, 512:1024]).astype(BF)

        @pl.when(first)
        def _():
            sib_de(k).wait_recv()

        tmp[...] = mm(inct[...], dagg[...])
        down[k] = cn[k].astype(F4) + mm(dpren[k], t_nin[:, 0:512])

        @pl.loop(0, EDGES_DEV // BLOCK, unroll=True)
        def _(i):
            at = pl.ds(pl.multiple_of(i * BLOCK, BLOCK), BLOCK)
            cot = tmp[at, :] + ce[k, at, :].astype(F4)
            tmp[at, :] = cot
            rows = lax.broadcasted_iota(jnp.int32, (BLOCK, 512), 0) + i * BLOCK
            cot = jnp.where(rows < live_count, cot, 0.0)
            hat = xhat[k, at, :]
            dge[...] += jnp.sum((cot * hat).reshape(BLOCK // 8, 8, 512), axis=0)
            inv = rstd[k, at, 0:1]
            doute[k, at, :] = norm_back(cot, gain_e[...], hat, inv).astype(BF)

        grad = mm(doute[k], t_eout[...])
        pre[k] = grad * silu_grad(pre[k])
        dpre[k] = pre[k].astype(BF)
        gs[k] = mm(oht[0:TABLE], dpre[k]).astype(BF)
        gr[k] = mm(oht[TABLE:], dpre[k]).astype(BF)
        bh[k] = mm(gs[k, NODES_DEV:], t_ein[:, 512:1024]).astype(BF)

        @pl.when(first)
        def _():
            for j in range(4):
                back_copy(halo2, k, j, r_bh2).start()

        @pl.when(second)
        def _():
            for j in range(4):
                back_copy(halo1, k, j, r_bh1).start()

        down[k] += mm(gs[k, 0:NODES_DEV], t_ein[:, 512:1024]) + mm(gr[k], t_ein[:, 1024:1536])

        @pl.when(second)
        def _():
            sib_do(k).start()

        de[k] = (tmp[...] + mm(dpre[k], t_ein[:, 0:512])).astype(BF)

        @pl.when(second)
        def _():
            sib_de(k).start()

        @pl.when(first)
        def _():
            store_edge(de, k).start()

    @pl.loop(0, 4)
    def _(step):
        forward_now = (step == 0) | (step == 1 + seg)
        k = jnp.where(first, step % 2, step // 2)

        @pl.when(step == 2 - 2 * seg)
        def _():
            for m in range(3):
                t_ein[:, m * 512 : m * 512 + 512] = w_ein[m * 512 : m * 512 + 512].T
            for m in range(2):
                t_nin[:, m * 512 : m * 512 + 512] = w_nin[m * 512 : m * 512 + 512].T
            t_eout[...] = w_eout[...].T
            t_nout[...] = w_nout[...].T

        @pl.when(forward_now)
        def _():
            forward(k)

        @pl.when(jnp.logical_not(forward_now))
        def _():
            backward(k)

    def put_ein(base, value):
        for q in range(8):
            r = base + q * 16
            row = (r // 192) * ROWS_A + r % ROWS_A
            ga[(r % 192) // ROWS_A, row : row + 16, :] = value[q * 16 : q * 16 + 16].astype(BF)

    def put_b(m, n_lo, n_hi, e, o):
        for q in range(8):
            part = (n_lo, n_hi)[q // 4][q % 4 * 32 : q % 4 * 32 + 32]
            for p in range(4):
                b = p % 2 * 2 + p // 2
                r = q * 16 + 4 * b
                tile = jnp.concatenate([part[8 * b : 8 * b + 8], e[r : r + 4], o[r : r + 4]], axis=0)
                gb[p, m * 8 + q] = tile[:, 0:LANES].astype(BF)
                gz[2 * m + q // 4, q % 4, p] = tile[:, LANES:].astype(BF)

    def both(ref):
        return ref[...].reshape(ref.shape[0] * ref.shape[1], ref.shape[2])

    def cols(ref, m):
        return jnp.concatenate([ref[0, :, m * 128 : (m + 1) * 128], ref[1, :, m * 128 : (m + 1) * 128]], axis=0)

    def own_cols(m):
        at = slice(m * 128, (m + 1) * 128)
        return jnp.concatenate([tab[0, 0:NODES_DEV, at], tab[1, 0:NODES_DEV, at]], axis=0)

    def copy(n, src, dst, device):
        return remote(src, dst, send_sem.at[n], recv_sem.at[n], device)

    class Ring:
        def __init__(self, base, src, t, u, v, me, at, cut):
            right, left, across = (me + 1) % 4, (me + 3) % 4, (me + 2) % 4
            lo, hi = slice(0, cut), slice(cut, t.shape[0])
            self.out = [
                copy(base, src.at[across, lo], t.at[lo], at(right)),
                copy(base + 1, src.at[across, hi], t.at[hi], at(left)),
                copy(base + 2, src.at[right, hi], u.at[hi], at(right)),
                copy(base + 3, src.at[left, lo], v.at[lo], at(left)),
                copy(base + 4, t.at[lo], u.at[lo], at(right)),
                copy(base + 5, t.at[hi], v.at[hi], at(left)),
            ]
            self.src, self.t, self.u, self.v = src, t, u, v
            self.me, self.right, self.left, self.cut = me, right, left, cut

        def start(self):
            for c in self.out[:2]:
                c.start()

        def rest(self):
            for c in self.out[2:4]:
                c.start()

        def middle(self, block):
            src, t, n, cut = self.src, self.t, self.t.shape[0], self.cut
            for c, q, lo, hi in ((0, self.right, 0, cut), (1, self.left, cut, n)):
                self.out[c].wait_recv()

                @pl.loop(lo // block, hi // block, unroll=4 if (hi - lo) // block % 4 == 0 else 1)
                def _(i):
                    at = pl.ds(pl.multiple_of(i * block, block), block)
                    t[at] = (t[at].astype(F4) + src[q, at].astype(F4)).astype(BF)

                self.out[4 + c].start()

        def total(self, at):
            own = self.src[self.me, at].astype(F4)
            return own + self.u[at].astype(F4) + self.v[at].astype(F4)

        def arrive(self):
            for c in self.out[2:]:
                c.wait_recv()

    ring_a = Ring(0, ga, ta, ua, va, y, at_y, 208)
    ring_b = Ring(6, gb, tb, ub, vb, px, at_x, 2 * nz)
    def spread(base, src, got, peers, at):
        moves = [copy(base + j, src.at[p], got.at[j], at(p)) for j, p in enumerate(peers)]
        for c in moves:
            c.start()
        return moves

    def nin_part(m):
        lhs = own_cols(m) if m < 4 else cols(agg, m - 4)
        return mm_tn(lhs, both(dpren))

    for m in range(4):
        put_b(
            m, nin_part(2 * m), nin_part(2 * m + 1),
            mm_tn(cols(mid, m), both(doute)), mm_tn(cols(midn, m), both(doutn)),
        )
    ring_b.start()
    zc = 24 + 2 * (nz - 1)
    up, low = at_z((z + 1) % nz), at_z((z + nz - 1) % nz)
    flow_up = [copy(zc, gz.at[(z + 4) % nz], zr.at[0], up)]
    flow_up += [copy(zc + 1 + i, zr.at[i], zr.at[i + 1], up) for i in range(3)]
    flow_low = [copy(zc + 4, gz.at[(z + nz - 3) % nz], zl.at[0], low)]
    flow_low += [copy(zc + 5 + i, zl.at[i], zl.at[i + 1], low) for i in range(2)]
    flow_up[0].start()
    flow_low[0].start()

    def pass_on(i):
        for flow, held, q in ((flow_up, zr, z + 3 - i), (flow_low, zl, z + nz - 2 + i)):
            if i + 1 < len(flow):
                flow[i].wait_recv()
                for r in range(4):
                    part = held[i, r].astype(F4) + gz[q % nz, r].astype(F4)
                    held[i, r] = part.astype(BF)
                flow[i + 1].start()

    for m in range(4):
        base = m * 128
        put_ein(base, mm_tn(cols(ein, m), both(dpre)))
        put_ein(512 + base, mm_tn(cols(tab, m), both(gs)))
        put_ein(1024 + base, mm_tn(own_cols(m), both(gr)))
    row = lax.broadcasted_iota(jnp.int32, (GAIN, 512), 0)
    sum_e = jnp.sum(dge[...], axis=0, keepdims=True)
    sum_n = jnp.sum(dgn[...], axis=0, keepdims=True)
    gains = jnp.where(row == 0, sum_e, jnp.where(row == 1, sum_n, 0.0)).astype(BF)
    for q in range(4):
        ga[q, EDGES_DEV:, :] = gains
    ring_b.rest()
    ring_a.start()

    @pl.when(first)
    def _():
        for k in range(2):
            for j in range(4):
                back_copy(halo2, k, j, r_bh2).wait_recv()
            dh[k] = (down[k] + mm(sendt[:, 0:HALOS], halo2[k])).astype(BF)
            store_node(dh, k).start()

    pass_on(0)
    ring_a.rest()
    pass_on(1)
    ring_b.middle(2)
    ring_a.middle(16)
    pass_on(2)
    flow_up[3].wait_recv()
    flow_low[2].wait_recv()
    for r in range(4):
        part = gz[z, r].astype(F4) + zr[3, r].astype(F4) + zl[2, r].astype(F4)
        hy[r] = part.astype(BF)
    flow_y = spread(zc + 7, hy, ry, y_peers, at_y)
    ring_a.arrive()
    gains = ring_a.total(slice(nz * ROWS_A, nz * ROWS_A + GAIN))[0:4]

    @pl.loop(0, nz, unroll=4)
    def _(i):
        at = pl.ds(pl.multiple_of(i * ROWS_A, 16), ROWS_A)
        total = ring_a.total(at)
        for p in range(4):
            b = p % 2 * 2 + p // 2
            tile = jnp.concatenate([total[12 * b : 12 * b + 12], gains], axis=0)
            a2[p, i] = tile.astype(BF)

    second_a = spread(12, a2, ga2, x_peers, at_x)
    ring_b.arrive()

    @pl.loop(0, nz, unroll=4)
    def _(i):
        for q in range(4):
            b2[q, i] = ring_b.total(i * 4 + q).astype(BF)

    second_b = spread(15, b2, gb2, y_peers, at_y)
    part = hy[y].astype(F4)
    for j, c in enumerate(flow_y):
        c.wait_recv()
        part = part + ry[j].astype(F4)
    hx[...] = part.astype(BF)
    flow_x = spread(zc + 10, hx, rx, x_peers, at_x)

    def along_z(base, moves, src, got, me, held, into):
        for c in moves:
            c.wait_recv()
        for i in range(nz):
            total = src[me, i].astype(F4)
            for j in range(3):
                total = total + got[j, i].astype(F4)
            held[i] = total.astype(BF)
        return spread(base, held, into, z_peers, at_z)

    def z_total(moves, held, got):
        total = held[z].astype(F4)
        for j, c in enumerate(moves):
            c.wait_recv()
            total = total + got[j].astype(F4)
        return total * factor

    third_a = along_z(24, second_a, a2, ga2, px, ca, ra)
    third_b = along_z(24 + nz - 1, second_b, b2, gb2, y, cb, rb)
    part = hx[px].astype(F4)
    for j, c in enumerate(flow_x):
        c.wait_recv()
        part = part + rx[j].astype(F4)
    fin_out[16:32, LANES:] = part * factor
    fin_out[0:16] = z_total(third_a, ca, ra)
    fin_out[16:32, 0:LANES] = z_total(third_b, cb, rb)
    for c in ring_a.out + ring_b.out + second_a + second_b + third_a + third_b + flow_up + flow_low + flow_y + flow_x:
        c.wait_send()

    @pl.when(first)
    def _():
        for k in range(2):
            sib_e(k).wait_send()
            sib_h(k).wait_send()
            for j in range(4):
                halo_copy(hs1, k, j, s_halo1, 0).wait_send()
                halo_copy(hs2, k, j, s_halo2, 1).wait_send()
                back_copy(halo2, k, j, r_bh2).wait_send()
            store_edge(de, k).wait()
            store_node(dh, k).wait()

    @pl.when(second)
    def _():
        for k in range(2):
            sib_do(k).wait_send()
            sib_de(k).wait_send()
            for j in range(4):
                back_copy(halo1, k, j, r_bh1).wait_send()
            store_edge(enew, k).wait()
            store_node(hnew, k).wait()


def layer_call(operands, factor):
    hbm = pl.BlockSpec(memory_space=pl.ANY)
    nz = 8
    i32 = jnp.int32

    def bf(*shape):
        return pltpu.VMEM(shape, BF)

    def fl(*shape):
        return pltpu.VMEM(shape, F4)

    dma = pltpu.SemaphoreType.DMA
    n, e = NODES_DEV, EDGES_DEV
    rows = nz * ROWS_A + GAIN
    copies = 24 + 2 * (nz - 1) + 13
    return pl.pallas_call(
        functools.partial(layer_kernel, nz=nz, factor=factor),
        out_shape=[
            pltpu.VMEM((2, n, 512), BF),
            pltpu.VMEM((2, e, 512), BF),
            pltpu.VMEM((32, 512), F4),
        ],
        in_specs=[hbm] * 13,
        out_specs=[pl.BlockSpec(memory_space=pltpu.VMEM)] * 3,
        scratch_shapes=[
            pltpu.VMEM((e,), i32), pltpu.VMEM((e,), i32), pltpu.VMEM((1, 4, HALO), i32), pltpu.SMEM((1,), i32),
            bf(1536, 512), bf(512, 512), bf(1024, 512), bf(512, 512), fl(1, 512), fl(1, 512), dma((10,)),
            bf(512, 1536), bf(512, 512), bf(512, 1024), bf(512, 512),
            bf(320, e), bf(e, 320), bf(n, e), bf(e, n), bf(n, n), bf(n, n),
            bf(2, TABLE, 512), bf(2, e, 512), bf(2, n, 512), bf(2, e, 512), fl(2, n, 512),
            bf(2, HALOS, 512), bf(2, HALOS, 512), bf(2, HALOS, 512), bf(2, HALOS, 512), bf(2, HALOS, 512),
            bf(320, 512), fl(2, e, 512), bf(2, e, 512), fl(e, 512), fl(2, e, 512), fl(2, e, 128),
            bf(2, e, 512), bf(2, n, 512), fl(2, n, 512), bf(2, n, 512), fl(n, 512), fl(2, n, 512),
            fl(2, n, 128), bf(2, n, 512),
            bf(2, n, 512), bf(2, n, 512), fl(2, n, 512), bf(n, 512), bf(2, e, 512), bf(2, e, 512),
            bf(2, TABLE, 512), bf(2, n, 512), bf(2, e, 512), bf(2, n, 512), fl(8, 512), fl(8, 512),
            dma((2, 4)), dma((2, 4)), dma((2, 4)), dma((2,)), dma((2,)), dma((2,)), dma((2,)),
            dma((2, 4)), dma((2, 4)), dma((2, 4)), dma((2,)), dma((2,)), dma((2,)), dma((2,)),
            dma((2,)), dma((2,)), dma((2,)), dma((2,)), dma((2,)),
            bf(4, rows, 512), bf(4, 4 * nz, 16, LANES),
            bf(rows, 512), bf(rows, 512), bf(rows, 512),
            bf(4 * nz, 16, LANES), bf(4 * nz, 16, LANES), bf(4 * nz, 16, LANES),
            bf(4, nz, 16, 512), bf(3, nz, 16, 512),
            bf(4, nz, 16, LANES), bf(3, nz, 16, LANES),
            bf(nz, 16, 512), bf(nz - 1, 16, 512), bf(nz, 16, LANES), bf(nz - 1, 16, LANES),
            bf(nz, 4, 4, 16, 128), bf(4, 4, 4, 16, 128), bf(3, 4, 4, 16, 128),
            bf(4, 4, 16, 128), bf(3, 4, 16, 128), bf(4, 16, 128), bf(3, 16, 128),
            dma((copies,)), dma((copies,)),
        ],
        compiler_params=pltpu.CompilerParams(
            collective_id=0, has_side_effects=True, vmem_limit_bytes=56 << 20
        ),
        name="layers",
    )(*operands)


def finish_kernel(
    node_in, edge_in, rfin, node_o, edge_o, ein_o, eout_o, nin_o, nout_o, ge_o, gn_o, sems
):
    stores = []
    for k in range(2):
        stores.append(pltpu.make_async_copy(edge_in.at[k], edge_o.at[0, k], sems.at[k]))
        stores.append(pltpu.make_async_copy(node_in.at[k], node_o.at[0, k], sems.at[2 + k]))
    for c in stores:
        c.start()
    t = lax.axis_index("dom") * 2 + lax.axis_index("rep")
    for r in range(12):
        ein_o[r] = rfin[r : r + 1]
    nin_o[0] = rfin[16:24]
    eout_o[0] = rfin[24:28]
    nout_o[0] = rfin[28:32]
    pair = rfin[12:14]
    lane = lax.broadcasted_iota(jnp.int32, (2, 512), 1)
    narrow = lax.broadcasted_iota(jnp.int32, (2, 128), 1)
    picked = jnp.zeros((2, 128), F4)
    for i in range(4):
        value = jnp.sum(jnp.where(lane == t * 4 + i, pair, 0.0), axis=1, keepdims=True)
        picked = picked + jnp.where(narrow == i, value, 0.0)
    ge_o[...] = picked[0:1, 0:4]
    gn_o[...] = picked[1:2, 0:4]
    for c in stores:
        c.wait()


def finish_call(node, edge, fin):
    hbm = pl.BlockSpec(memory_space=pl.ANY)
    vm = pl.BlockSpec(memory_space=pltpu.VMEM)
    return pl.pallas_call(
        finish_kernel,
        out_shape=[
            jax.ShapeDtypeStruct((1, *node.shape), BF),
            jax.ShapeDtypeStruct((1, *edge.shape), BF),
            jax.ShapeDtypeStruct((12, 1, 512), F4),
            jax.ShapeDtypeStruct((1, 4, 512), F4),
            jax.ShapeDtypeStruct((1, 8, 512), F4),
            jax.ShapeDtypeStruct((1, 4, 512), F4),
            jax.ShapeDtypeStruct((1, 4), F4),
            jax.ShapeDtypeStruct((1, 4), F4),
        ],
        in_specs=[vm] * 3,
        out_specs=[hbm] * 2 + [vm] * 6,
        scratch_shapes=[pltpu.SemaphoreType.DMA((4,))],
        compiler_params=pltpu.CompilerParams(vmem_limit_bytes=16 << 20),
        name="finish",
    )(node, edge, fin)


def body(
    node_latent, edge_latent, node_cot, edge_src, edge_dst, edge_count, send_index,
    w_edge_in, w_edge_out, w_node_in, w_node_out, gain_edge, gain_node,
):
    micro = node_latent.shape[0]
    factor = float(micro * lax.axis_size("rep") * NODES_DEV * lax.axis_size("dom")) ** (-0.5)
    node, edge, fin = layer_call(
        (
            edge_src, edge_dst, send_index, edge_count, node_latent, edge_latent, node_cot,
            w_edge_in, w_edge_out, w_node_in, w_node_out, gain_edge, gain_node,
        ),
        factor,
    )
    node, edge, ein, *rest = finish_call(node, edge, fin)
    return (node, edge, jnp.swapaxes(ein, 0, 1), *rest)


def solution(mesh):
    placed = (
        P("rep", "dom", None),
        P("rep", "dom", None),
        P("rep", "dom", None),
        P("dom"),
        P("dom"),
        P("dom"),
        P("dom", None, None),
        P("segment", None, None),
        P("segment", None, None),
        P("segment", None, None),
        P("segment", None, None),
        P("segment", None),
        P("segment", None),
    )
    return jax.shard_map(
        body,
        mesh=mesh,
        in_specs=placed,
        out_specs=(
            P("segment", "rep", "dom", None),
            P("segment", "rep", "dom", None),
            P("segment", ("dom", "rep"), None),
            P("segment", ("dom", "rep"), None),
            P("segment", ("dom", "rep"), None),
            P("segment", ("dom", "rep"), None),
            P("segment", ("dom", "rep")),
            P("segment", ("dom", "rep")),
        ),
        check_vma=False,
    )
```
